32 devices in a mesh: tensor: 4 (over z), example: 8 (over y, x, core).
Axes of the slice: x: 2, y: 2, z: 4, core: 2. Of those that a mesh axis runs over, the one named last changes fastest.
Arguments:
- queries: bfloat16 [1, 4096, 4096], P(None, 'example', 'tensor'), may hold values from -0.0014648438 to 0.0014648438
- basis_out: bfloat16 [4096, 4096], P('example', 'tensor'), may hold values from -0.09375 to 0.09375
- basis_in: bfloat16 [4096, 4096], P('tensor', 'example'), may hold values from -0.09375 to 0.09375
- eigvals: float32 [4096, 4096], P('tensor', 'example'), may hold values from 0.25 to 4
- input_fac: bfloat16 [128, 8, 4096], P('example', None, 'tensor'), may hold values from -6 to 6
- grad_fac: bfloat16 [128, 8, 4096], P('example', None, 'tensor'), may hold values from -6 to 6
- cand_slot: int32 [128], replicated, may hold values from 0 to 127, as said below
- score_list: int32 [8, 16], replicated, may hold values from 0 to 127, as said below
- token_count: int32 [128], replicated, may hold values from 1 to 8
Outputs:
- scores: float32 [1, 128, 8], P(None, 'example')
The draws below stay inside these ranges and needn't reach their ends.
Inputs may be any that keep to these rules, and one draw needn't show every extreme that they name: `cand_slot`: a permutation; slot s belongs to owner s // 16. `score_list`: every candidate appears exactly once; a scorer's list holds at most 4 candidates of any one owner, and some scorer takes exactly 4 from some owner.
All inputs are finite; a program needn't handle non-finite values.
Results may differ from the reference program's by a relative error of at most 0.019.
Values may be sent and summed in bfloat16 or wider, within the bound.
A program may use at most 128 MiB of HBM per device.

```python
import math
import jax
import jax.numpy as jnp
from jax import lax

D = 4096
QUERIES = 1
CAND_DEV = 16
LEN = 8
CANDIDATES = 128
N_TENSOR = 4
N_EXAMPLE = 8


def routing_tables(key):
    base_key = jax.random.fold_in(key, 11)
    key_order, key_target, key_other, key_tie, key_perm = jax.random.split(base_key, 5)
    per_pair = CAND_DEV // N_EXAMPLE
    slot_ids = jnp.arange(CAND_DEV, dtype=jnp.int32)
    destination = jnp.tile((slot_ids // per_pair)[None, :], (N_EXAMPLE, 1))
    owner_order = jax.random.permutation(key_order, N_EXAMPLE)
    half_count = N_EXAMPLE // 2
    first_owners = owner_order[:half_count]
    second_owners = owner_order[half_count:2 * half_count]
    target_one = jax.random.randint(key_target, (half_count,), 0, N_EXAMPLE).astype(jnp.int32)
    target_two = ((target_one + 1 + jax.random.randint(key_other, (half_count,), 0, N_EXAMPLE - 1)) % N_EXAMPLE).astype(jnp.int32)
    rows_first = destination[first_owners]
    rows_first = jnp.where(rows_first == target_two[:, None], target_one[:, None], rows_first)
    rows_second = destination[second_owners]
    rows_second = jnp.where(rows_second == target_one[:, None], target_two[:, None], rows_second)
    destination = destination.at[first_owners].set(rows_first).at[second_owners].set(rows_second)
    total_slots = CAND_DEV * N_EXAMPLE
    tie_break = jax.random.permutation(key_tie, total_slots).astype(jnp.int32)
    sort_key = destination.reshape(-1).astype(jnp.int32) * total_slots + tie_break
    sorted_slots = jnp.argsort(sort_key, stable=True).astype(jnp.int32)
    slot_of_cand = jax.random.permutation(key_perm, total_slots).astype(jnp.int32)
    cand_of_slot = jnp.argsort(slot_of_cand, stable=True).astype(jnp.int32)
    lists = cand_of_slot[sorted_slots].reshape(N_EXAMPLE, CAND_DEV)
    return (slot_of_cand, lists)


def draw_cand_slot(key, part):
    slot_of_cand, lists = routing_tables(key)
    return slot_of_cand


def draw_score_list(key, part):
    slot_of_cand, lists = routing_tables(key)
    return lists


def draw_token_count(key, part):
    key_count, key_full = jax.random.split(jax.random.fold_in(key, 23))
    counts = jax.random.randint(key_count, (CAND_DEV * N_EXAMPLE,), 1, LEN + 1).astype(jnp.int32)
    full_index = jax.random.randint(key_full, (), 0, CAND_DEV * N_EXAMPLE)
    return counts.at[full_index].set(LEN).astype(jnp.int32)


def levels(stream_key, dims, cuts, low, top_value):
    def one(position, parts):
        draws = jax.random.uniform(jax.random.fold_in(jax.random.fold_in(stream_key, 6), position), (parts,), jnp.float32, low / len(cuts), top_value / len(cuts))
        return jnp.repeat(jnp.exp(draws), dims[position] // parts).reshape((-1,) + (1,) * (len(dims) - position - 1))

    loudness = one(*cuts[0])
    for cut in cuts[1:]:
        loudness = loudness * one(*cut)
    return loudness


def scatter_about(own_key, dims, deviation, bound, cuts=(), held_as=jnp.bfloat16):
    result = deviation * jax.random.normal(own_key, dims, jnp.float32)
    if cuts:
        result = result * levels(own_key, dims, cuts, -0.22, 0.18)
    return jnp.clip(result, -bound, bound).astype(held_as)


def setup_inputs(seed: int = 0) -> dict:
    key_list = jax.random.split(jax.random.key(seed), 10)
    queries = scatter_about(key_list[0], (QUERIES, D, D), (D * D) ** -0.5, 0.0014648438, ((1, 8), (2, 4)))
    basis_out = scatter_about(key_list[1], (D, D), D ** -0.5, 0.09375, ((0, 8), (1, 4)))
    basis_in = scatter_about(key_list[2], (D, D), D ** -0.5, 0.09375, ((0, 4), (1, 8)))
    eigvals = jnp.clip(jnp.exp(math.log(4.0) - 2.7725887 * jax.random.uniform(key_list[3], (D, D), jnp.float32) ** levels(key_list[3], (D, D), ((0, 4), (1, 8)), -0.2, 0.2)), 0.25, 4.0)
    input_fac = scatter_about(key_list[4], (CANDIDATES, LEN, D), 1.0, 6.0, ((0, 8), (2, 4)))
    grad_fac = scatter_about(key_list[5], (CANDIDATES, LEN, D), 1.0, 6.0, ((0, 8), (2, 4)))
    cand_slot = draw_cand_slot(jax.random.fold_in(key_list[9], 71), 0)
    score_list = draw_score_list(jax.random.fold_in(key_list[9], 71), 0)
    token_count = draw_token_count(jax.random.fold_in(key_list[9], 71), 0)
    return dict(queries=queries, basis_out=basis_out, basis_in=basis_in, eigvals=eigvals, input_fac=input_fac, grad_fac=grad_fac, cand_slot=cand_slot, score_list=score_list, token_count=token_count)


def reference(queries, basis_out, basis_in, eigvals, input_fac, grad_fac, cand_slot, score_list, token_count):
    out_block = D // N_EXAMPLE
    in_block = D // N_TENSOR

    def rotate_one(gradient):
        def out_step(running, block_index):
            rows_basis = lax.dynamic_slice_in_dim(basis_out, block_index * out_block, out_block, 0)
            rows_grad = lax.dynamic_slice_in_dim(gradient, block_index * out_block, out_block, 0)
            block_term = jnp.dot(rows_basis.T, rows_grad, preferred_element_type=jnp.float32).astype(jnp.bfloat16)
            block_term = lax.optimization_barrier(block_term)
            return running + block_term.astype(jnp.float32), None

        mixed_sum, _ = lax.scan(out_step, jnp.zeros((D, D), jnp.float32), jnp.arange(N_EXAMPLE, dtype=jnp.int32))
        rotated = mixed_sum.astype(jnp.bfloat16)

        def in_step(running, block_index):
            cols_rot = lax.dynamic_slice_in_dim(rotated, block_index * in_block, in_block, 1)
            rows_basis = lax.dynamic_slice_in_dim(basis_in, block_index * in_block, in_block, 0)
            block_term = jnp.dot(cols_rot, rows_basis, preferred_element_type=jnp.float32).astype(jnp.bfloat16)
            block_term = lax.optimization_barrier(block_term)
            return running + block_term.astype(jnp.float32), None

        core_sum, _ = lax.scan(in_step, jnp.zeros((D, D), jnp.float32), jnp.arange(N_TENSOR, dtype=jnp.int32))
        scaled = (core_sum / eigvals.T).astype(jnp.bfloat16)
        turned = jnp.dot(basis_out, scaled, preferred_element_type=jnp.float32).astype(jnp.bfloat16)
        return jnp.dot(turned, basis_in.T, preferred_element_type=jnp.float32).astype(jnp.bfloat16)

    precond = lax.map(rotate_one, queries)

    def score_one(candidate):
        cand_place = cand_slot[candidate]
        cand_acts = lax.dynamic_index_in_dim(input_fac, cand_place, 0, keepdims=False)
        cand_grads = lax.dynamic_index_in_dim(grad_fac, cand_place, 0, keepdims=False)
        weighted = jnp.stack([jnp.dot(cand_grads, precond[query_index], preferred_element_type=jnp.float32) for query_index in range(QUERIES)])
        token_scores = jnp.sum(cand_acts.astype(jnp.float32)[None] * weighted, axis=2)
        live_mask = jnp.arange(LEN, dtype=jnp.int32) < token_count[candidate]
        return jnp.where(live_mask[None], token_scores, jnp.float32(0.0))

    scored = lax.map(score_one, score_list.reshape(-1))
    return jnp.transpose(scored, (1, 0, 2))
```

```python
import functools

import jax
import jax.numpy as jnp
from jax import lax
from jax.experimental import pallas as pl
from jax.experimental.pallas import tpu as pltpu
from jax.sharding import PartitionSpec as P

BF = jnp.bfloat16
F32 = jnp.float32
MESH = pl.DeviceIdType.MESH
VMEM_LIMIT = 60 * 1024 * 1024
LANES = 128


def flip(index, bit):
    size = 1 << bit
    return index + size * (1 - 2 * ((index // size) % 2))


def flip_mask(index, mask, bits):
    for bit in range(bits):
        if (mask >> bit) & 1:
            index = flip(index, bit)
    return index


def level_of(mask, order):
    for place, bit in enumerate(order):
        if (mask >> bit) & 1:
            return place
    return len(order)


def last_level(mask, order):
    return max(place for place, bit in enumerate(order) if (mask >> bit) & 1)


def remote(src, dst, send, recv, **where):
    return pltpu.make_async_remote_copy(
        src_ref=src, dst_ref=dst, send_sem=send, recv_sem=recv, device_id=where, device_id_type=MESH
    )


def tile_loop(size, tile, step):
    while size % tile:
        tile //= 2

    def run(i, carry):
        step(pl.ds(pl.multiple_of(i * tile, tile), tile))
        return carry

    lax.fori_loop(0, size // tile, run, 0)


class Schedule:
    def __init__(self):
        self.actions = []

    def at(self, when, action):
        self.actions.append((when, len(self.actions), action))

    def run(self):
        for _, _, action in sorted(self.actions, key=lambda item: item[:2]):
            action()


class Gather:
    def __init__(self, me, bits, view, own, send_sem, recv_sem, drains):
        self.me, self.bits, self.view, self.own = me, bits, view, own
        self.send_sem, self.recv_sem, self.drains = send_sem, recv_sem, drains
        upper = list(range(1, bits))
        self.orders = [upper + [0], upper[::-1] + [0]]
        self.done = set()

    def send(self, h, mask, bit):
        there = self.view(h, flip_mask(self.me, mask, self.bits))
        src = self.own(h) if mask == 0 else there
        slot = mask | (1 << bit)
        copy = remote(src, there, self.send_sem.at[h, slot], self.recv_sem.at[h, slot], example=flip(self.me, bit))
        copy.start()
        self.drains.append(copy.wait_send)

    def start(self):
        for place in range(self.bits - 1):
            for h in range(2):
                self.send(h, 0, self.orders[h][place])
            if place == 0:
                for h in range(2):
                    self.send(h, 0, 0)

    def ensure(self, h, mask):
        if mask == 0 or (h, mask) in self.done:
            return
        self.done.add((h, mask))
        here = self.view(h, flip_mask(self.me, mask, self.bits))
        remote(here, here, self.send_sem.at[h, mask], self.recv_sem.at[h, mask], example=flip(self.me, 0)).wait_recv()
        for bit in self.orders[h][last_level(mask, self.orders[h]) + 1 :]:
            self.send(h, mask, bit)

    def masks(self):
        pairs = [(h, mask) for mask in range(1, 1 << self.bits) for h in range(2)]
        return sorted(pairs, key=lambda p: (last_level(p[1], self.orders[p[0]]), bin(p[1]).count("1"), p[1], p[0]))


class Line:
    def __init__(self, t, n, piece, send_sem, recv_sem, drains):
        self.t, self.n, self.piece = t, n, piece
        self.send_sem, self.recv_sem, self.drains = send_sem, recv_sem, drains
        self.done = set()

    def send(self, cond, s, src, way):
        ref = self.piece(src, s)
        copy = remote(ref, ref, self.send_sem.at[way, s, src], self.recv_sem.at[s, src], tensor=self.t + 1 - 2 * way)

        @pl.when(cond)
        def _():
            copy.start()

        def drain():
            @pl.when(cond)
            def _():
                copy.wait_send()

        self.drains.append(drain)

    def own(self, s):
        self.send(self.t < self.n - 1, s, self.t, 0)
        self.send(self.t > 0, s, self.t, 1)

    def ensure(self, s, d):
        if (s, d) in self.done:
            return
        self.done.add((s, d))
        for way in range(2):
            sign = 1 - 2 * way
            src = self.t - sign * d
            here = src >= 0 if way == 0 else src < self.n
            on = self.t < self.n - 1 if way == 0 else self.t > 0

            @pl.when(here)
            def _():
                ref = self.piece(src, s)
                remote(ref, ref, self.send_sem.at[way, s, src], self.recv_sem.at[s, src],
                       tensor=self.t - sign).wait_recv()

            if d < self.n - 1:
                self.send(here & on, s, src, way)


def whole_kernel(
    n, bits, tk,
    q_ref, bi_ref, bo_ref, grads_ref, acts_ref, eig_ref, out_ref,
    left, bo_all, bi_all, prod, core_in, xy_in, fin, gall, zheld, zin, cacc, aall, acc, red_t, red_e,
    own_sem, grad_send, grad_recv, bo_send, bo_recv, g_send, g_recv, bi_send, bi_recv, a_send, a_recv,
    core_send, core_recv, xy_send, xy_recv, z_send, z_recv, rt_send, rt_recv, re_send, re_recv,
):
    me = lax.axis_index("example")
    t = lax.axis_index("tensor")
    count = 1 << bits
    pair = me // 2
    core = me % 2
    chip_bits = bits - 1
    wide, width = q_ref.shape
    slices = width // LANES
    total_rows = left.shape[0]
    half = total_rows // 2
    orders = [list(range(chip_bits)), list(range(chip_bits))[::-1]]
    drains = []
    plan = Schedule()

    tables = []
    for h in range(2):
        table = {}
        for place in range(chip_bits):
            for mask in range(1 << chip_bits):
                if level_of(mask, orders[h]) > place:
                    table[(place, mask)] = len(table)
        tables.append(table)

    q_copy = pltpu.make_async_copy(q_ref, left.at[pl.ds(0, wide)], own_sem.at[0])
    q_copy.start()
    bi_copy = pltpu.make_async_copy(
        bi_ref, bi_all.at[pair, pl.ds(pl.multiple_of(core * width, width), width)], own_sem.at[1]
    )
    bo_copies = []
    for s in range(slices):
        for h in range(2):
            copy = pltpu.make_async_copy(
                bo_ref.at[:, pl.ds(h * width + s * LANES, LANES)],
                bo_all.at[t, s, :, pl.ds(h * LANES, LANES)],
                own_sem.at[2 + 2 * s + h],
            )
            copy.start()
            bo_copies.append(copy)
    bi_copy.start()

    barrier = pltpu.get_barrier_semaphore()
    for k in range(1, n):
        pl.semaphore_signal(barrier, inc=1, device_id={"tensor": (t + k) % n}, device_id_type=MESH)
    for k in range(1, count):
        pl.semaphore_signal(barrier, inc=1, device_id={"example": (me + k) % count}, device_id_type=MESH)
    far = pair != t

    @pl.when(far)
    def _():
        for h in range(2):
            pl.semaphore_signal(
                barrier, inc=1, device_id={"tensor": pair, "example": 2 * t + h}, device_id_type=MESH
            )
        pl.semaphore_wait(barrier, n + count)

    @pl.when(jnp.logical_not(far))
    def _():
        pl.semaphore_wait(barrier, n + count - 2)

    def grad_rows(c):
        return left.at[pl.ds(pl.multiple_of(wide + c * tk, tk), tk)]

    def grad_piece(h):
        return grads_ref.at[:, pl.ds(h * width, width)]

    def is_self(c):
        return jnp.logical_not(far) & (core == c)

    def grads_out():
        for h in range(2):
            copy = remote(grad_piece(h), grad_rows(core), grad_send.at[h], grad_recv.at[core],
                          tensor=pair, example=2 * t + h)
            local = pltpu.make_async_copy(grad_piece(h), grad_rows(core), grad_send.at[h])

            @pl.when(jnp.logical_not(is_self(h)))
            def _():
                copy.start()

            @pl.when(is_self(h))
            def _():
                local.start()
                local.wait()

            def drain(copy=copy, h=h):
                @pl.when(jnp.logical_not(is_self(h)))
                def _():
                    copy.wait_send()

            drains.append(drain)

    def grads_in():
        for c in range(2):
            @pl.when(jnp.logical_not(is_self(c)))
            def _():
                remote(grad_rows(c), grad_rows(c), grad_send.at[c], grad_recv.at[c],
                       tensor=pair, example=2 * t + c).wait_recv()

    bo_line = Line(t, n, lambda src, s: bo_all.at[src, s], bo_send, bo_recv, drains)
    g_line = Line(t, n, lambda src, s: gall.at[src, s], g_send, g_recv, drains)
    quarter = width // 2

    def bi_view(h, e):
        return bi_all.at[e // 2, pl.ds(pl.multiple_of((e % 2) * width + h * quarter, quarter), quarter)]

    bi_gather = Gather(me, bits, bi_view, lambda h: bi_ref.at[pl.ds(h * quarter, quarter)], bi_send, bi_recv, drains)

    def a_view(h, e):
        return aall.at[e, pl.ds(h * (wide // 2), wide // 2)]

    a_gather = Gather(me, bits, a_view, lambda h: a_view(h, me), a_send, a_recv, drains)

    core_done = set()

    def core_copy(s, cm):
        return remote(prod.at[s, cm, 1 - core], core_in.at[s, cm], core_send.at[s, cm], core_recv.at[s, cm],
                      example=flip(me, 0))

    def rotate(s, cm):
        owner = flip_mask(pair, cm, chip_bits)

        def step(rows):
            res = jnp.dot(left[rows, :], bo_all[owner, s], preferred_element_type=F32).astype(BF)
            prod[s, cm, 0, rows, :] = res[:, :LANES]
            prod[s, cm, 1, rows, :] = res[:, LANES:]

        tile_loop(total_rows, 256, step)
        copy = core_copy(s, cm)
        copy.start()
        drains.append(copy.wait_send)

    def xy_copy(s, h, mask, place):
        bit = orders[h][place]
        slot = tables[h][(place, mask & ~(1 << bit))]
        rows = pl.ds(h * half, half)
        return remote(prod.at[s, mask, core, rows], xy_in.at[s, slot, rows], xy_send.at[s, h, mask],
                      xy_recv.at[s, h, slot], example=flip(me, bit + 1))

    def add_up(s, h, mask):
        if (s, mask) not in core_done:
            core_done.add((s, mask))
            core_copy(s, mask).wait_recv()
        level = level_of(mask, orders[h])
        for place in range(level):
            xy_copy(s, h, mask | (1 << orders[h][place]), place).wait_recv()
        inboxes = [tables[h][(place, mask)] for place in range(level)]

        def step(rows):
            rows = pl.ds(pl.multiple_of(rows.start + h * half, rows.size), rows.size)
            total = prod[s, mask, core, rows, :].astype(F32) + core_in[s, mask, rows, :].astype(F32)
            for slot in inboxes:
                total += xy_in[s, slot, rows, :].astype(F32)
            if mask:
                prod[s, mask, core, rows, :] = total.astype(BF)
            else:
                fin[s, rows, :] = total.astype(BF)

        tile_loop(half, 128, step)
        if mask:
            copy = xy_copy(s, h, mask, level)
            copy.start()
            drains.append(copy.wait_send)

    def keep_grads(s):
        gall[t, s] = fin[s, wide:, :]

    def z_product(a, block, rows):
        right = acts_ref[...] if a == 0 else fin[a - 1, :wide, :]
        return jnp.dot(bi_all[block, rows, :], right, preferred_element_type=F32)

    def z_unit(a, q, block_up, block_down):
        up = (t == q) & (block_up > q)
        down = (t == n - 1 - q) & (block_down < n - 1 - q)
        block = jnp.where(up, block_up, block_down)
        toward = jnp.where(up, 1, -1)
        slot = block + jnp.where(up, 1, 0)
        copy = remote(zheld.at[a, block], zin.at[a, slot], z_send.at[a, block], z_recv.at[a, slot], tensor=t + toward)

        @pl.when(up | down)
        def _():
            def first(rows):
                zheld[a, block, rows, :] = z_product(a, block, rows).astype(BF)

            tile_loop(wide, 256, first)
            if q:
                remote(zin.at[a, slot], zin.at[a, slot], z_send.at[a, block], z_recv.at[a, slot],
                       tensor=t - toward).wait_recv()

                def second(rows):
                    total = zheld[a, block, rows, :].astype(F32) + zin[a, slot, rows, :].astype(F32)
                    zheld[a, block, rows, :] = total.astype(BF)

                tile_loop(wide, 256, second)
            copy.start()

        def drain():
            @pl.when(up | down)
            def _():
                copy.wait_send()

        drains.append(drain)

    def z_own_product(a):
        def first(rows):
            cacc[rows, :] = z_product(a, t, rows)

        tile_loop(wide, 256, first)

    def z_own_sum(a):
        for way in range(2):
            slot = t + 1 - way

            @pl.when(t > 0 if way == 0 else t < n - 1)
            def _():
                remote(zin.at[a, slot], zin.at[a, slot], z_send.at[a, t], z_recv.at[a, slot],
                       tensor=t - 1 + 2 * way).wait_recv()

                def second(rows):
                    cacc[rows, :] += zin[a, slot, rows, :].astype(F32)

                tile_loop(wide, 256, second)

    def keep_acts():
        def step(rows):
            aall[me, rows, :] = cacc[rows, :].astype(BF)

        tile_loop(wide, 256, step)

    def score(s):
        def step(rows):
            scaled = (cacc[rows, :] / eig_ref[rows, s * LANES : (s + 1) * LANES]).astype(BF)
            for group in range(n):
                weighted = lax.dot_general(
                    scaled, gall[group, s], (((1,), (1,)), ((), ())), preferred_element_type=F32
                )
                for c in range(2):
                    e = 2 * group + c
                    part = weighted[:, c * tk : (c + 1) * tk] * aall[e, rows, :].astype(F32)
                    acc[e] += jnp.sum(part.reshape(-1, 8, tk), axis=0)

        tile_loop(wide, 256, step)

    def begin():
        for copy in bo_copies[:2]:
            copy.wait()
        bo_line.own(0)
        bi_gather.start()
        grads_out()
        acc[...] = jnp.zeros_like(acc)
        for copy in bo_copies[2:]:
            copy.wait()
        if slices > 1:
            bo_line.own(1)
        q_copy.wait()
        bi_copy.wait()

    plan.at(-1, begin)
    hop = 5.5
    period = 16.5
    for s in range(slices):
        base = 4 + s * period
        for d in range(1, n):
            plan.at(base + d * hop, functools.partial(bo_line.ensure, s, d))
        if s + 2 < slices:
            plan.at(base + 2.1 * hop, functools.partial(bo_line.own, s + 2))

    for place, (h, mask) in enumerate(bi_gather.masks()):
        upper = last_level(mask & ~1, bi_gather.orders[h]) if mask & ~1 else -1
        ready = 4 + 10.5 * (upper + bin(mask >> 1).count("1")) + 1 if upper >= 0 else 3
        plan.at(ready + (mask & 1), functools.partial(bi_gather.ensure, h, mask))

    def need_bi(cm):
        for h in range(2):
            for c in range(2):
                bi_gather.ensure(h, 2 * cm + c)

    for cm in range(n):
        ready = 5 if cm == 0 else 25 if bin(cm).count("1") == 1 else 36
        block = flip_mask(pair, cm, chip_bits)
        plan.at(ready, functools.partial(need_bi, cm))
        for q in range(n - 1):
            plan.at(ready + 0.2 + 6 * q, functools.partial(z_unit, 0, q, block, block))
    acts_end = 36 + 6 * n
    plan.at(acts_end, lambda: (z_own_product(0), z_own_sum(0), keep_acts(), a_gather.start()))
    for h, mask in a_gather.masks():
        upper = last_level(mask & ~1, a_gather.orders[h]) if mask & ~1 else -1
        ready = acts_end + 3 + 3 * max(upper + bin(mask >> 1).count("1"), 0)
        plan.at(ready + (mask & 1), functools.partial(a_gather.ensure, h, mask))

    def first_masks():
        return sorted(range(1 << chip_bits), key=lambda m: (min(level_of(m, o) for o in orders), -bin(m).count("1")))

    for s in range(slices):
        base = 4 + s * period + n * hop - 1
        if s == 0:
            plan.at(base, grads_in)
        for i, cm in enumerate(first_masks()):
            plan.at(base + 0.8 * i, functools.partial(rotate, s, cm))
        for h in range(2):
            for cm in first_masks():
                level = level_of(cm, orders[h])
                plan.at(base + 1.7 + 6 * level, functools.partial(add_up, s, h, cm))
        done = base + 2.5 + 6 * chip_bits
        plan.at(done, functools.partial(keep_grads, s))
        plan.at(done, functools.partial(g_line.own, s))
        for d in range(1, n):
            plan.at(done + 4 * d, functools.partial(g_line.ensure, s, d))
        a = s + 1
        for q in range(n - 1):
            for k in range(n - 1 - q):
                plan.at(done + 0.1 + 6 * q + 6 * k * (q > 0) + 0.5 * k, functools.partial(z_unit, a, q, n - 1 - k, k))
        own = max(done + 6 * n, acts_end + 16 + s)
        plan.at(own - 1, functools.partial(z_own_product, a))
        plan.at(own, functools.partial(z_own_sum, a))
        plan.at(own + 0.1, functools.partial(score, s))

    plan.run()

    red_t[t] = jnp.concatenate([jnp.sum(acc[e], axis=0, keepdims=True) for e in range(count)], axis=0)
    copies = []
    for k in range(1, n):
        copy = remote(red_t.at[t], red_t.at[t], rt_send.at[k - 1], rt_recv.at[t], tensor=(t + k) % n)
        copy.start()
        copies.append(copy)
    for drain in drains:
        drain()
    for k in range(1, n):
        src = (t + k) % n
        remote(red_t.at[src], red_t.at[src], rt_send.at[k - 1], rt_recv.at[src], tensor=src).wait_recv()
    total = red_t[0]
    for k in range(1, n):
        total += red_t[k]
    red_e[me] = total
    for k in range(1, count):
        copy = remote(red_e.at[me], red_e.at[me], re_send.at[k - 1], re_recv.at[me], example=(me + k) % count)
        copy.start()
        copies.append(copy)
    for k in range(1, count):
        src = (me + k) % count
        remote(red_e.at[src], red_e.at[src], re_send.at[k - 1], re_recv.at[src], example=src).wait_recv()
    total = red_e[0]
    for k in range(1, count):
        total += red_e[k]
    out_ref[...] = total
    for copy in copies:
        copy.wait_send()


def token_totals(q_t, bi_t, bo, grads, acts_t, eig, n, count):
    bits = count.bit_length() - 1
    wide, width = q_t.shape
    tk = grads.shape[0]
    slices = width // LANES
    rows = wide + 2 * tk
    chips = count // 2
    anywhere = pl.BlockSpec(memory_space=pl.ANY)
    vmem = pl.BlockSpec(memory_space=pltpu.VMEM)
    dma = pltpu.SemaphoreType.DMA
    return pl.pallas_call(
        functools.partial(whole_kernel, n, bits, tk),
        out_shape=jax.ShapeDtypeStruct((count, tk), F32),
        in_specs=[anywhere, anywhere, anywhere, anywhere, vmem, vmem],
        out_specs=vmem,
        scratch_shapes=[
            pltpu.VMEM((rows, width), BF),
            pltpu.VMEM((n, slices, width, 2 * LANES), BF),
            pltpu.VMEM((n, wide, wide), BF),
            pltpu.VMEM((slices, chips, 2, rows, LANES), BF),
            pltpu.VMEM((slices, chips, rows, LANES), BF),
            pltpu.VMEM((slices, chips - 1, rows, LANES), BF),
            pltpu.VMEM((slices, rows, LANES), BF),
            pltpu.VMEM((n, slices, 2 * tk, LANES), BF),
            pltpu.VMEM((slices + 1, n, wide, LANES), BF),
            pltpu.VMEM((slices + 1, n + 1, wide, LANES), BF),
            pltpu.VMEM((wide, LANES), F32),
            pltpu.VMEM((count, wide, tk), BF),
            pltpu.VMEM((count, 8, tk), F32),
            pltpu.VMEM((n, count, tk), F32),
            pltpu.VMEM((count, count, tk), F32),
            dma((2 + 2 * slices,)),
            dma((2,)),
            dma((2,)),
            dma((2, slices, n)),
            dma((slices, n)),
            dma((2, slices, n)),
            dma((slices, n)),
            dma((2, count)),
            dma((2, count)),
            dma((2, count)),
            dma((2, count)),
            dma((slices, chips)),
            dma((slices, chips)),
            dma((slices, 2, chips)),
            dma((slices, 2, chips)),
            dma((slices + 1, n)),
            dma((slices + 1, n + 1)),
            dma((n,)),
            dma((n,)),
            dma((count,)),
            dma((count,)),
        ],
        compiler_params=pltpu.CompilerParams(
            collective_id=0, has_side_effects=True, vmem_limit_bytes=VMEM_LIMIT
        ),
        name="token_totals",
    )(q_t, bi_t, bo, grads, acts_t, eig)


def body(
    queries, basis_out, basis_in, eigvals, input_fac, grad_fac, cand_slot, score_list, token_count
):
    count = lax.axis_size("example")
    n = lax.axis_size("tensor")
    my_index = lax.axis_index("example")
    cand_total = cand_slot.shape[0]
    token_len = input_fac.shape[1]
    wide = queries.shape[2]
    acts = input_fac.reshape(-1, wide)
    grads = grad_fac.reshape(-1, wide)

    by_slot = []
    for q in range(queries.shape[0]):
        totals = token_totals(queries[q].T, basis_in.T, basis_out, grads, acts.T, eigvals, n, count)
        by_slot.append(totals.reshape(cand_total, token_len))
    by_slot = jnp.stack(by_slot)

    my_list = lax.dynamic_index_in_dim(score_list, my_index, 0, keepdims=False)
    ids = jnp.arange(cand_total, dtype=jnp.int32)
    matches = my_list[:, None] == ids[None, :]
    my_slot = jnp.sum(jnp.where(matches, cand_slot[None, :], 0), axis=1)
    my_count = jnp.sum(jnp.where(matches, token_count[None, :], 0), axis=1)
    pick = my_slot[:, None] == ids[None, :]
    scores = jnp.sum(jnp.where(pick[None, :, :, None], by_slot[:, None], F32(0.0)), axis=2)
    live = jnp.arange(token_len, dtype=jnp.int32)[None, :] < my_count[:, None]
    return jnp.where(live[None], scores, F32(0.0))


def solution(mesh):
    in_specs = (
        P(None, "example", "tensor"),
        P("example", "tensor"),
        P("tensor", "example"),
        P("tensor", "example"),
        P("example", None, "tensor"),
        P("example", None, "tensor"),
        P(),
        P(),
        P(),
    )
    out_specs = P(None, "example", None)
    return jax.shard_map(body, mesh=mesh, in_specs=in_specs, out_specs=out_specs, check_vma=False)
```

```python
import functools

import jax
import jax.numpy as jnp
from jax import lax
from jax.experimental import pallas as pl
from jax.experimental.pallas import tpu as pltpu
from jax.sharding import PartitionSpec as P

BF = jnp.bfloat16
F32 = jnp.float32
MESH = pl.DeviceIdType.MESH
VMEM_LIMIT = 60 * 1024 * 1024
LANES = 128


def flip(index, bit):
    size = 1 << bit
    return index + size * (1 - 2 * ((index // size) % 2))


def flip_mask(index, mask, bits):
    for bit in range(bits):
        if (mask >> bit) & 1:
            index = flip(index, bit)
    return index


def level_of(mask, order):
    for place, bit in enumerate(order):
        if (mask >> bit) & 1:
            return place
    return len(order)


def last_level(mask, order):
    return max(place for place, bit in enumerate(order) if (mask >> bit) & 1)


def remote(src, dst, send, recv, **where):
    return pltpu.make_async_remote_copy(
        src_ref=src, dst_ref=dst, send_sem=send, recv_sem=recv, device_id=where, device_id_type=MESH
    )


def tile_loop(size, tile, step):
    while size % tile:
        tile //= 2

    def run(i, carry):
        step(pl.ds(pl.multiple_of(i * tile, tile), tile))
        return carry

    lax.fori_loop(0, size // tile, run, 0)


TUNED_ORDER = (
    "begin", ("bo", 0, 0), "grads_out", ("bo", 0, 1), ("bo", 1, 0), ("bo", 0, 2), ("bi", 0, 2), ("bi", 1, 1),
    ("bi", 1, 4), ("bi", 0, 1), "own_in", ("z", 0, 0, 0), ("bo", 2, 0), ("bo", 1, 1), ("bi", 1, 5), ("bi", 0, 3),
    ("bi", 1, 2), "grads_in", ("bi", 1, 3), ("z", 0, 0, 1), ("bi", 0, 4), ("z", 0, 1, 0), ("bo", 0, 3),
    ("rot", 0, 0), ("bi", 0, 5), ("rot", 0, 2), ("z", 0, 0, 2), ("rot", 0, 3), ("core", 0, 3), ("add", 0, 1, 3),
    ("rot", 0, 1), ("add", 0, 0, 3), ("core", 0, 1), ("add", 0, 0, 1), ("bo", 1, 2), ("bo", 3, 0), ("bi", 1, 6),
    ("bo", 2, 1), ("core", 0, 2), ("add", 0, 1, 2), ("bi", 0, 6), ("add", 0, 1, 1), ("z", 0, 1, 2), ("bi", 0, 7),
    ("bi", 1, 7), ("z", 0, 0, 3), ("add", 0, 0, 2), ("bo", 1, 3), ("rot", 1, 3), ("core", 0, 0), ("add", 0, 1, 0),
    ("core", 1, 3), ("add", 1, 0, 3), ("add", 1, 1, 3), ("add", 0, 0, 0), ("z", 1, 0, 0), ("z", 1, 0, 2),
    ("rot", 1, 2), ("rot", 1, 1), ("z", 1, 0, 1), ("z", 0, 1, 1), ("keep", 0), ("core", 1, 2), ("add", 1, 1, 2),
    ("bo", 2, 2), ("core", 1, 1), ("g", 0, 0), ("add", 1, 1, 1), ("rot", 1, 0), ("z", 0, 2, 2), ("z", 0, 1, 3),
    ("add", 1, 0, 1), ("bo", 2, 3), ("rot", 2, 3), ("z", 0, 2, 0), ("z", 0, 2, 1), ("bo", 3, 1), ("add", 1, 0, 2),
    ("core", 2, 3), ("add", 2, 1, 3), ("z", 1, 1, 0), ("add", 2, 0, 3), ("rot", 2, 1), ("rot", 2, 0),
    ("core", 1, 0), ("rot", 2, 2), ("add", 1, 0, 0), ("add", 1, 1, 0), ("keep", 1), ("z", 0, 2, 3), ("z", 2, 0, 1),
    ("core", 2, 1), ("add", 2, 1, 1), ("core", 2, 2), ("add", 2, 1, 2), ("g", 1, 0), ("z", 1, 1, 1),
    ("add", 2, 0, 2), ("add", 2, 0, 1), "acts", ("z", 2, 0, 0), ("z", 2, 0, 2), ("bo", 3, 2), ("bo", 3, 3),
    ("rot", 3, 3), ("rot", 3, 0), ("rot", 3, 2), ("zown", 1), ("core", 3, 3), ("z", 1, 2, 0), ("core", 2, 0),
    ("add", 2, 1, 0), ("add", 3, 0, 3), ("add", 3, 1, 3), ("rot", 3, 1), ("g", 0, 1), ("add", 2, 0, 0),
    ("z", 3, 0, 0), ("z", 2, 1, 1), ("z", 2, 1, 0), ("g", 1, 1), ("core", 3, 2), ("add", 3, 1, 2), ("z", 3, 0, 1),
    ("core", 3, 1), ("add", 3, 0, 1), ("keep", 2), ("g", 2, 0), ("add", 3, 0, 2), ("z", 3, 1, 0), ("z", 2, 2, 0),
    ("core", 3, 0), ("a", 0, 4), ("add", 3, 1, 1), ("a", 1, 2), ("g", 1, 2), ("z", 3, 1, 1), ("g", 2, 1),
    ("a", 0, 1), ("add", 3, 0, 0), ("a", 1, 4), ("add", 3, 1, 0), ("z", 4, 0, 0), ("z", 3, 2, 0), ("a", 0, 2),
    ("a", 0, 3), ("a", 1, 6), ("keep", 3), ("g", 3, 0), ("z", 4, 0, 1), ("z", 4, 1, 0), ("a", 0, 6), ("z", 3, 0, 2),
    ("a", 0, 5), ("a", 1, 1), ("g", 0, 2), ("a", 1, 3), ("zsum", 1), ("g", 2, 2), ("a", 1, 5), ("g", 0, 3),
    ("a", 1, 7), ("z", 4, 0, 2), ("g", 3, 1), ("a", 0, 7), ("score", 0), ("zown", 2), ("g", 1, 3), ("zsum", 2),
    ("score", 1), ("z", 4, 2, 0), ("zown", 3), ("z", 4, 1, 1), ("zsum", 3), ("g", 2, 3), ("g", 3, 2), ("score", 2),
    ("zown", 4), ("g", 3, 3), ("zsum", 4), ("score", 3),
)


class Schedule:
    def __init__(self):
        self.actions = {}
        self.done = set()

    def at(self, when, name, action, *needs):
        self.actions[name] = (when, len(self.actions), action, needs)

    def do(self, name):
        if name in self.done:
            return
        self.done.add(name)
        for need in self.actions[name][3]:
            self.do(need)
        self.actions[name][2]()

    def run(self):
        for name in sorted(self.actions, key=lambda name: self.actions[name][:2]):
            self.do(name)


class Gather:
    def __init__(self, me, bits, view, own, send_sem, recv_sem, drains):
        self.me, self.bits, self.view, self.own = me, bits, view, own
        self.send_sem, self.recv_sem, self.drains = send_sem, recv_sem, drains
        upper = list(range(1, bits))
        self.orders = [upper + [0], upper[::-1] + [0]]

    def send(self, h, mask, bit):
        there = self.view(h, flip_mask(self.me, mask, self.bits))
        src = self.own(h) if mask == 0 else there
        slot = mask | (1 << bit)
        copy = remote(src, there, self.send_sem.at[h, slot], self.recv_sem.at[h, slot], example=flip(self.me, bit))
        copy.start()
        self.drains.append(copy.wait_send)

    def start(self):
        for place in range(self.bits - 1):
            for h in range(2):
                self.send(h, 0, self.orders[h][place])
            if place == 0:
                for h in range(2):
                    self.send(h, 0, 0)

    def before(self, h, mask):
        return mask & ~(1 << self.orders[h][last_level(mask, self.orders[h])])

    def receive(self, h, mask):
        here = self.view(h, flip_mask(self.me, mask, self.bits))
        remote(here, here, self.send_sem.at[h, mask], self.recv_sem.at[h, mask], example=flip(self.me, 0)).wait_recv()
        for bit in self.orders[h][last_level(mask, self.orders[h]) + 1 :]:
            self.send(h, mask, bit)

    def masks(self):
        pairs = [(h, mask) for mask in range(1, 1 << self.bits) for h in range(2)]
        return sorted(pairs, key=lambda p: (last_level(p[1], self.orders[p[0]]), bin(p[1]).count("1"), p[1], p[0]))


class Line:
    def __init__(self, t, n, piece, send_sem, recv_sem, drains):
        self.t, self.n, self.piece = t, n, piece
        self.send_sem, self.recv_sem, self.drains = send_sem, recv_sem, drains

    def send(self, cond, s, src, way):
        ref = self.piece(src, s)
        copy = remote(ref, ref, self.send_sem.at[way, s, src], self.recv_sem.at[s, src], tensor=self.t + 1 - 2 * way)

        @pl.when(cond)
        def _():
            copy.start()

        def drain():
            @pl.when(cond)
            def _():
                copy.wait_send()

        self.drains.append(drain)

    def own(self, s):
        self.send(self.t < self.n - 1, s, self.t, 0)
        self.send(self.t > 0, s, self.t, 1)

    def receive(self, s, d):
        for way in range(2):
            sign = 1 - 2 * way
            src = self.t - sign * d
            here = src >= 0 if way == 0 else src < self.n
            on = self.t < self.n - 1 if way == 0 else self.t > 0

            @pl.when(here)
            def _():
                ref = self.piece(src, s)
                remote(ref, ref, self.send_sem.at[way, s, src], self.recv_sem.at[s, src],
                       tensor=self.t - sign).wait_recv()

            if d < self.n - 1:
                self.send(here & on, s, src, way)


def plan_times(n, slices, chip_bits):
    hop, period, lag, step, rise = 5.5, 16.5, 21.0, 6.0, 6.0
    times = {"begin": -9.0, "own_in": 0.5, "grads_out": 0.1, "grads_in": 20.0}
    orders = [list(range(chip_bits)), list(range(chip_bits))[::-1]]
    full = [[bit + 1 for bit in order] + [0] for order in orders]
    count = 2 << chip_bits

    def gather(label, base, gap):
        for h in range(2):
            for mask in range(1, count):
                upper = last_level(mask & ~1, full[h]) + bin(mask >> 1).count("1") if mask & ~1 else 0
                times[label, h, mask] = base + gap * upper + (mask & 1)

    gather("bi", 3.0, 10.5)
    for cm in range(n):
        ready = 3.0 + 10.5 * (cm.bit_length() + (bin(cm).count("1") > 1)) + 2 if cm else 4.5
        for q in range(n - 1):
            times["z", 0, q, cm] = ready + step * q
    acts = 3.0 + 10.5 * (chip_bits + 1) + step * n
    times["acts"] = acts
    gather("a", acts + 3, 3.0)
    for s in range(slices):
        base = 4 + s * period
        times["bo", s, 0] = base - period - hop if s else 0.0
        for d in range(1, n):
            times["bo", s, d] = base + d * hop
        rot = base + lag
        for i, cm in enumerate(sorted(range(n), key=lambda m: -bin(m).count("1"))):
            times["rot", s, cm] = rot + 0.8 * i
            times["core", s, cm] = rot + 1.6 + 0.8 * i
            for h in range(2):
                times["add", s, h, cm] = rot + 1.7 + rise * level_of(cm, orders[h]) + 0.1 * i
        done = rot + 2.5 + rise * chip_bits
        times["keep", s] = done
        for d in range(n):
            times["g", s, d] = done + 4.0 * d
        a = s + 1
        for q in range(n - 1):
            for k in range(n - 1 - q):
                times["z", a, q, k] = done + 0.1 + step * (q + (k if q else 0)) + 0.5 * k
        own = done + step * n
        times["zown", a] = own - 1
        times["zsum", a] = own
        times["score", s] = own + 0.1
    if set(TUNED_ORDER) == set(times):
        times = {name: float(place) for place, name in enumerate(TUNED_ORDER)}
    return times


def whole_kernel(
    n, bits, tk,
    q_ref, bi_ref, bo_ref, grads_ref, acts_ref, eig_ref, out_ref,
    left, bo_all, bi_all, prod, core_in, xy_in, fin, gall, zheld, zin, cacc, aall, acc, red_t, red_e,
    own_sem, grad_send, grad_recv, bo_send, bo_recv, g_send, g_recv, bi_send, bi_recv, a_send, a_recv,
    core_send, core_recv, xy_send, xy_recv, z_send, z_recv, rt_send, rt_recv, re_send, re_recv,
):
    me = lax.axis_index("example")
    t = lax.axis_index("tensor")
    count = 1 << bits
    pair = me // 2
    core = me % 2
    chip_bits = bits - 1
    wide, width = q_ref.shape
    slices = width // LANES
    total_rows = left.shape[0]
    half = total_rows // 2
    orders = [list(range(chip_bits)), list(range(chip_bits))[::-1]]
    drains = []
    plan = Schedule()

    tables = []
    for h in range(2):
        table = {}
        for place in range(chip_bits):
            for mask in range(1 << chip_bits):
                if level_of(mask, orders[h]) > place:
                    table[(place, mask)] = len(table)
        tables.append(table)

    q_copy = pltpu.make_async_copy(q_ref, left.at[pl.ds(0, wide)], own_sem.at[0])
    q_copy.start()
    bi_copy = pltpu.make_async_copy(
        bi_ref, bi_all.at[pair, pl.ds(pl.multiple_of(core * width, width), width)], own_sem.at[1]
    )
    bo_copies = []
    for s in range(slices):
        for h in range(2):
            copy = pltpu.make_async_copy(
                bo_ref.at[:, pl.ds(h * width + s * LANES, LANES)],
                bo_all.at[t, s, :, pl.ds(h * LANES, LANES)],
                own_sem.at[2 + 2 * s + h],
            )
            copy.start()
            bo_copies.append(copy)
    bi_copy.start()

    barrier = pltpu.get_barrier_semaphore()
    for k in range(1, n):
        pl.semaphore_signal(barrier, inc=1, device_id={"tensor": (t + k) % n}, device_id_type=MESH)
    for k in range(1, count):
        pl.semaphore_signal(barrier, inc=1, device_id={"example": (me + k) % count}, device_id_type=MESH)
    far = pair != t

    @pl.when(far)
    def _():
        for h in range(2):
            pl.semaphore_signal(
                barrier, inc=1, device_id={"tensor": pair, "example": 2 * t + h}, device_id_type=MESH
            )
        pl.semaphore_wait(barrier, n + count)

    @pl.when(jnp.logical_not(far))
    def _():
        pl.semaphore_wait(barrier, n + count - 2)

    def grad_rows(c):
        return left.at[pl.ds(pl.multiple_of(wide + c * tk, tk), tk)]

    def grad_piece(h):
        return grads_ref.at[:, pl.ds(h * width, width)]

    def is_self(c):
        return jnp.logical_not(far) & (core == c)

    def grads_out():
        for h in range(2):
            copy = remote(grad_piece(h), grad_rows(core), grad_send.at[h], grad_recv.at[core],
                          tensor=pair, example=2 * t + h)
            local = pltpu.make_async_copy(grad_piece(h), grad_rows(core), grad_send.at[h])

            @pl.when(jnp.logical_not(is_self(h)))
            def _():
                copy.start()

            @pl.when(is_self(h))
            def _():
                local.start()
                local.wait()

            def drain(copy=copy, h=h):
                @pl.when(jnp.logical_not(is_self(h)))
                def _():
                    copy.wait_send()

            drains.append(drain)

    def grads_in():
        for c in range(2):
            @pl.when(jnp.logical_not(is_self(c)))
            def _():
                remote(grad_rows(c), grad_rows(c), grad_send.at[c], grad_recv.at[c],
                       tensor=pair, example=2 * t + c).wait_recv()

    bo_line = Line(t, n, lambda src, s: bo_all.at[src, s], bo_send, bo_recv, drains)
    g_line = Line(t, n, lambda src, s: gall.at[src, s], g_send, g_recv, drains)
    quarter = width // 2

    def bi_view(h, e):
        return bi_all.at[e // 2, pl.ds(pl.multiple_of((e % 2) * width + h * quarter, quarter), quarter)]

    bi_gather = Gather(me, bits, bi_view, lambda h: bi_ref.at[pl.ds(h * quarter, quarter)], bi_send, bi_recv, drains)

    def a_view(h, e):
        return aall.at[e, pl.ds(h * (wide // 2), wide // 2)]

    a_gather = Gather(me, bits, a_view, lambda h: a_view(h, me), a_send, a_recv, drains)

    def core_copy(s, cm):
        return remote(prod.at[s, cm, 1 - core], core_in.at[s, cm], core_send.at[s, cm], core_recv.at[s, cm],
                      example=flip(me, 0))

    def rotate(s, cm):
        owner = flip_mask(pair, cm, chip_bits)

        def step(rows):
            res = jnp.dot(left[rows, :], bo_all[owner, s], preferred_element_type=F32).astype(BF)
            prod[s, cm, 0, rows, :] = res[:, :LANES]
            prod[s, cm, 1, rows, :] = res[:, LANES:]

        tile_loop(total_rows, total_rows, step)
        copy = core_copy(s, cm)
        copy.start()
        drains.append(copy.wait_send)

    def xy_copy(s, h, mask, place):
        bit = orders[h][place]
        slot = tables[h][(place, mask & ~(1 << bit))]
        rows = pl.ds(h * half, half)
        return remote(prod.at[s, mask, core, rows], xy_in.at[s, slot, rows], xy_send.at[s, h, mask],
                      xy_recv.at[s, h, slot], example=flip(me, bit + 1))

    def add_up(s, h, mask):
        level = level_of(mask, orders[h])
        for place in range(level):
            xy_copy(s, h, mask | (1 << orders[h][place]), place).wait_recv()
        inboxes = [tables[h][(place, mask)] for place in range(level)]

        def step(rows):
            rows = pl.ds(pl.multiple_of(rows.start + h * half, rows.size), rows.size)
            total = prod[s, mask, core, rows, :].astype(F32) + core_in[s, mask, rows, :].astype(F32)
            for slot in inboxes:
                total += xy_in[s, slot, rows, :].astype(F32)
            if mask:
                prod[s, mask, core, rows, :] = total.astype(BF)
            else:
                fin[s, rows, :] = total.astype(BF)

        tile_loop(half, 128, step)
        if mask:
            copy = xy_copy(s, h, mask, level)
            copy.start()
            drains.append(copy.wait_send)

    def keep_grads(s):
        gall[t, s] = fin[s, wide:, :]

    def z_product(a, block, rows):
        right = acts_ref[...] if a == 0 else fin[a - 1, :wide, :]
        return jnp.dot(bi_all[block, rows, :], right, preferred_element_type=F32)

    def z_unit(a, q, block_up, block_down):
        up = (t == q) & (block_up > q)
        down = (t == n - 1 - q) & (block_down < n - 1 - q)
        block = jnp.where(up, block_up, block_down)
        toward = jnp.where(up, 1, -1)
        slot = block + jnp.where(up, 1, 0)
        copy = remote(zheld.at[a, block], zin.at[a, slot], z_send.at[a, block], z_recv.at[a, slot], tensor=t + toward)

        @pl.when(up | down)
        def _():
            def first(rows):
                zheld[a, block, rows, :] = z_product(a, block, rows).astype(BF)

            tile_loop(wide, 512, first)
            if q:
                remote(zin.at[a, slot], zin.at[a, slot], z_send.at[a, block], z_recv.at[a, slot],
                       tensor=t - toward).wait_recv()

                def second(rows):
                    total = zheld[a, block, rows, :].astype(F32) + zin[a, slot, rows, :].astype(F32)
                    zheld[a, block, rows, :] = total.astype(BF)

                tile_loop(wide, 256, second)
            copy.start()

        def drain():
            @pl.when(up | down)
            def _():
                copy.wait_send()

        drains.append(drain)

    def z_own_product(a):
        def first(rows):
            cacc[rows, :] = z_product(a, t, rows)

        tile_loop(wide, 512, first)

    def z_own_sum(a):
        for way in range(2):
            slot = t + 1 - way

            @pl.when(t > 0 if way == 0 else t < n - 1)
            def _():
                remote(zin.at[a, slot], zin.at[a, slot], z_send.at[a, t], z_recv.at[a, slot],
                       tensor=t - 1 + 2 * way).wait_recv()

                def second(rows):
                    cacc[rows, :] += zin[a, slot, rows, :].astype(F32)

                tile_loop(wide, 256, second)

    def keep_acts():
        def step(rows):
            aall[me, rows, :] = cacc[rows, :].astype(BF)

        tile_loop(wide, 256, step)

    def score(s):
        def step(rows):
            scaled = (cacc[rows, :] / eig_ref[rows, s * LANES : (s + 1) * LANES]).astype(BF)
            for group in range(n):
                weighted = lax.dot_general(
                    scaled, gall[group, s], (((1,), (1,)), ((), ())), preferred_element_type=F32
                )
                for c in range(2):
                    e = 2 * group + c
                    part = weighted[:, c * tk : (c + 1) * tk] * aall[e, rows, :].astype(F32)
                    acc[e] += jnp.sum(part.reshape(-1, 8, tk), axis=0)

        tile_loop(wide, 256, step)

    def begin():
        bi_gather.start()
        for copy in bo_copies:
            copy.wait()

    def own_in():
        acc[...] = jnp.zeros_like(acc)
        q_copy.wait()
        bi_copy.wait()

    part = functools.partial
    times = plan_times(n, slices, chip_bits)
    plan.at(times["begin"], "begin", begin)
    plan.at(times["own_in"], "own_in", own_in, "begin")
    plan.at(times["grads_out"], "grads_out", grads_out, "begin")
    plan.at(times["grads_in"], "grads_in", grads_in, "grads_out")

    def plan_line(label, line, s, *needs):
        plan.at(times[label, s, 0], (label, s, 0), part(line.own, s), *needs)
        for d in range(1, n):
            plan.at(times[label, s, d], (label, s, d), part(line.receive, s, d), (label, s, d - 1))

    def plan_gather(label, gather, start):
        for h, mask in gather.masks():
            before = gather.before(h, mask)
            plan.at(times[label, h, mask], (label, h, mask), part(gather.receive, h, mask),
                    (label, h, before) if before else start)

    for s in range(slices):
        plan_line("bo", bo_line, s, "begin")
    plan_gather("bi", bi_gather, "begin")

    def bi_of(cm):
        return [("bi", h, 2 * cm + c) for h in range(2) for c in range(2) if cm or c]

    def plan_z(a, q, k, block_up, block_down, *needs):
        name = ("z", a, q, k)
        plan.at(times[name], name, part(z_unit, a, q, block_up, block_down), *needs)

    for cm in range(n):
        block = flip_mask(pair, cm, chip_bits)
        for q in range(n - 1):
            plan_z(0, q, cm, block, block, *(bi_of(cm) + ["own_in"] if q == 0 else [("z", 0, q - 1, cm)]))
    all_bi = [name for cm in range(n) for name in bi_of(cm)]

    def acts_in():
        z_own_product(0)
        z_own_sum(0)
        keep_acts()
        a_gather.start()

    plan.at(times["acts"], "acts", acts_in, *[("z", 0, n - 2, cm) for cm in range(n)])
    plan_gather("a", a_gather, "acts")
    all_acts = [("a", h, mask) for h, mask in a_gather.masks()]

    for s in range(slices):
        for cm in range(n):
            name = ("rot", s, cm)
            plan.at(times[name], name, part(rotate, s, cm), "own_in", "grads_in", *[("bo", s, d) for d in range(n)])
            plan.at(times["core", s, cm], ("core", s, cm), lambda s=s, cm=cm: core_copy(s, cm).wait_recv(), name)
            for h in range(2):
                level = level_of(cm, orders[h])
                sent = [("add", s, h, cm | (1 << orders[h][place])) for place in range(level)]
                plan.at(times["add", s, h, cm], ("add", s, h, cm), part(add_up, s, h, cm), ("core", s, cm), *sent)
        rotated = [("add", s, h, 0) for h in range(2)]
        plan_line("g", g_line, s, ("keep", s))
        plan.at(times["keep", s], ("keep", s), part(keep_grads, s), *rotated)
        a = s + 1
        for q in range(n - 1):
            for k in range(n - 1 - q):
                needs = rotated + all_bi if q == 0 else [("z", a, q - 1, k)]
                plan_z(a, q, k, n - 1 - k, k, *needs)
        free = ("score", s - 1) if s else "acts"
        plan.at(times["zown", a], ("zown", a), part(z_own_product, a), free, *(rotated + all_bi))
        sums = [("z", a, q, n - 2 - q) for q in range(n - 1)]
        plan.at(times["zsum", a], ("zsum", a), part(z_own_sum, a), ("zown", a), *sums)
        plan.at(times["score", s], ("score", s), part(score, s), ("zsum", a), *([("g", s, d) for d in range(n)] + all_acts))

    plan.run()

    red_t[t] = jnp.concatenate([jnp.sum(acc[e], axis=0, keepdims=True) for e in range(count)], axis=0)
    copies = []
    for k in range(1, n):
        copy = remote(red_t.at[t], red_t.at[t], rt_send.at[k - 1], rt_recv.at[t], tensor=(t + k) % n)
        copy.start()
        copies.append(copy)
    for drain in drains:
        drain()
    for k in range(1, n):
        src = (t + k) % n
        remote(red_t.at[src], red_t.at[src], rt_send.at[k - 1], rt_recv.at[src], tensor=src).wait_recv()
    total = red_t[0]
    for k in range(1, n):
        total += red_t[k]
    red_e[me] = total
    for k in range(1, count):
        copy = remote(red_e.at[me], red_e.at[me], re_send.at[k - 1], re_recv.at[me], example=(me + k) % count)
        copy.start()
        copies.append(copy)
    for k in range(1, count):
        src = (me + k) % count
        remote(red_e.at[src], red_e.at[src], re_send.at[k - 1], re_recv.at[src], example=src).wait_recv()
    total = red_e[0]
    for k in range(1, count):
        total += red_e[k]
    out_ref[...] = total
    for copy in copies:
        copy.wait_send()


def token_totals(q_t, bi_t, bo, grads, acts_t, eig, n, count):
    bits = count.bit_length() - 1
    wide, width = q_t.shape
    tk = grads.shape[0]
    slices = width // LANES
    rows = wide + 2 * tk
    chips = count // 2
    anywhere = pl.BlockSpec(memory_space=pl.ANY)
    vmem = pl.BlockSpec(memory_space=pltpu.VMEM)
    dma = pltpu.SemaphoreType.DMA
    return pl.pallas_call(
        functools.partial(whole_kernel, n, bits, tk),
        out_shape=jax.ShapeDtypeStruct((count, tk), F32),
        in_specs=[anywhere, anywhere, anywhere, anywhere, vmem, vmem],
        out_specs=vmem,
        scratch_shapes=[
            pltpu.VMEM((rows, width), BF),
            pltpu.VMEM((n, slices, width, 2 * LANES), BF),
            pltpu.VMEM((n, wide, wide), BF),
            pltpu.VMEM((slices, chips, 2, rows, LANES), BF),
            pltpu.VMEM((slices, chips, rows, LANES), BF),
            pltpu.VMEM((slices, chips - 1, rows, LANES), BF),
            pltpu.VMEM((slices, rows, LANES), BF),
            pltpu.VMEM((n, slices, 2 * tk, LANES), BF),
            pltpu.VMEM((slices + 1, n, wide, LANES), BF),
            pltpu.VMEM((slices + 1, n + 1, wide, LANES), BF),
            pltpu.VMEM((wide, LANES), F32),
            pltpu.VMEM((count, wide, tk), BF),
            pltpu.VMEM((count, 8, tk), F32),
            pltpu.VMEM((n, count, tk), F32),
            pltpu.VMEM((count, count, tk), F32),
            dma((2 + 2 * slices,)),
            dma((2,)),
            dma((2,)),
            dma((2, slices, n)),
            dma((slices, n)),
            dma((2, slices, n)),
            dma((slices, n)),
            dma((2, count)),
            dma((2, count)),
            dma((2, count)),
            dma((2, count)),
            dma((slices, chips)),
            dma((slices, chips)),
            dma((slices, 2, chips)),
            dma((slices, 2, chips)),
            dma((slices + 1, n)),
            dma((slices + 1, n + 1)),
            dma((n,)),
            dma((n,)),
            dma((count,)),
            dma((count,)),
        ],
        compiler_params=pltpu.CompilerParams(
            collective_id=0, has_side_effects=True, vmem_limit_bytes=VMEM_LIMIT
        ),
        name="token_totals",
    )(q_t, bi_t, bo, grads, acts_t, eig)


def body(
    queries, basis_out, basis_in, eigvals, input_fac, grad_fac, cand_slot, score_list, token_count
):
    count = lax.axis_size("example")
    n = lax.axis_size("tensor")
    my_index = lax.axis_index("example")
    cand_total = cand_slot.shape[0]
    token_len = input_fac.shape[1]
    wide = queries.shape[2]
    acts = input_fac.reshape(-1, wide)
    grads = grad_fac.reshape(-1, wide)

    by_slot = []
    for q in range(queries.shape[0]):
        totals = token_totals(queries[q].T, basis_in.T, basis_out, grads, acts.T, eigvals, n, count)
        by_slot.append(totals.reshape(cand_total, token_len))
    by_slot = jnp.stack(by_slot)

    my_list = lax.dynamic_index_in_dim(score_list, my_index, 0, keepdims=False)
    ids = jnp.arange(cand_total, dtype=jnp.int32)
    matches = my_list[:, None] == ids[None, :]
    my_slot = jnp.sum(jnp.where(matches, cand_slot[None, :], 0), axis=1)
    my_count = jnp.sum(jnp.where(matches, token_count[None, :], 0), axis=1)
    pick = my_slot[:, None] == ids[None, :]
    scores = jnp.sum(jnp.where(pick[None, :, :, None], by_slot[:, None], F32(0.0)), axis=2)
    live = jnp.arange(token_len, dtype=jnp.int32)[None, :] < my_count[:, None]
    return jnp.where(live[None], scores, F32(0.0))


def solution(mesh):
    in_specs = (
        P(None, "example", "tensor"),
        P("example", "tensor"),
        P("tensor", "example"),
        P("tensor", "example"),
        P("example", None, "tensor"),
        P("example", None, "tensor"),
        P(),
        P(),
        P(),
    )
    out_specs = P(None, "example", None)
    return jax.shard_map(body, mesh=mesh, in_specs=in_specs, out_specs=out_specs, check_vma=False)
```

```python
import functools

import jax
import jax.numpy as jnp
from jax import lax
from jax.experimental import pallas as pl
from jax.experimental.pallas import tpu as pltpu
from jax.sharding import PartitionSpec as P

BF = jnp.bfloat16
F32 = jnp.float32
MESH = pl.DeviceIdType.MESH
VMEM_LIMIT = 60 * 1024 * 1024
LANES = 128


def flip(index, bit):
    size = 1 << bit
    return index + size * (1 - 2 * ((index // size) % 2))


def flip_mask(index, mask, bits):
    for bit in range(bits):
        if (mask >> bit) & 1:
            index = flip(index, bit)
    return index


def level_of(mask, order):
    for place, bit in enumerate(order):
        if (mask >> bit) & 1:
            return place
    return len(order)


def last_level(mask, order):
    return max(place for place, bit in enumerate(order) if (mask >> bit) & 1)


def remote(src, dst, send, recv, **where):
    return pltpu.make_async_remote_copy(
        src_ref=src, dst_ref=dst, send_sem=send, recv_sem=recv, device_id=where, device_id_type=MESH
    )


def tile_loop(size, tile, step):
    while size % tile:
        tile //= 2

    def run(i, carry):
        step(pl.ds(pl.multiple_of(i * tile, tile), tile))
        return carry

    lax.fori_loop(0, size // tile, run, 0)


TUNED_ORDER = (
    "begin", "own_in", ("bo", 0, 0), ("bi", 1, 1), ("bi", 0, 1), "grads_out", ("bo", 0, 1), ("bo", 1, 0),
    ("grads", 3), ("grads", 2), ("bo", 0, 2), ("grads", 0), ("grads", 1), ("z", 0, 0, 0), ("bo", 2, 0),
    ("bi", 1, 4), ("bi", 0, 2), "q_in", ("bi", 0, 4), ("bi", 1, 5), ("bi", 0, 5), ("z", 0, 0, 2), ("bi", 1, 2),
    "grads_in", ("bo", 0, 3), ("rot", 0, 3), ("bo", 1, 1), ("core", 0, 3), ("add", 0, 1, 3), ("rot", 0, 1),
    ("bi", 1, 3), ("rot", 0, 2), ("add", 0, 0, 3), ("rot", 0, 0), ("bi", 0, 3), ("z", 0, 0, 1), ("bo", 1, 2),
    ("bo", 3, 0), ("bo", 2, 1), ("bi", 0, 6), ("bi", 1, 6), ("core", 0, 2), ("add", 0, 1, 2), ("core", 0, 1),
    ("add", 0, 1, 1), ("bi", 0, 7), ("bi", 1, 7), ("z", 0, 0, 3), ("add", 0, 0, 2), ("z", 0, 1, 0), ("z", 0, 1, 2),
    ("bo", 1, 3), ("add", 0, 0, 1), ("rot", 1, 3), ("core", 0, 0), ("core", 1, 3), ("add", 1, 0, 3), ("rot", 1, 0),
    ("add", 1, 1, 3), ("rot", 1, 2), ("add", 0, 1, 0), ("add", 0, 0, 0), ("z", 1, 0, 0), ("core", 1, 0),
    ("rot", 1, 1), ("core", 1, 1), ("add", 1, 0, 1), ("core", 1, 2), ("add", 1, 0, 2), ("z", 1, 0, 1),
    ("add", 1, 1, 1), ("keep", 0), ("add", 1, 1, 2), ("bo", 2, 2), ("bo", 3, 1), ("add", 1, 0, 0), ("z", 0, 1, 3),
    ("bo", 2, 3), ("rot", 2, 3), ("g", 0, 0), ("add", 1, 1, 0), ("keep", 1), ("g", 1, 0), ("core", 2, 3),
    ("z", 2, 0, 1), ("add", 2, 1, 3), ("add", 2, 0, 3), ("bo", 3, 2), ("z", 1, 1, 0), ("z", 2, 0, 0), ("rot", 2, 1),
    ("rot", 2, 2), ("core", 2, 2), ("core", 2, 1), ("add", 2, 1, 2), ("z", 0, 2, 0), ("add", 2, 1, 1),
    ("z", 0, 1, 1), ("rot", 2, 0), ("add", 2, 0, 1), ("add", 2, 0, 2), ("z", 2, 0, 2), ("bo", 3, 3), ("core", 2, 0),
    ("g", 0, 1), ("z", 0, 2, 2), ("rot", 3, 3), ("core", 3, 3), ("add", 3, 1, 3), ("rot", 3, 1), ("z", 1, 1, 1),
    ("add", 3, 0, 3), ("add", 2, 0, 0), ("add", 2, 1, 0), ("z", 3, 0, 0), ("core", 3, 1), ("add", 3, 0, 1),
    ("rot", 3, 2), ("z", 2, 1, 1), ("core", 3, 2), ("add", 3, 1, 2), ("z", 0, 2, 3), ("add", 3, 1, 1),
    ("rot", 3, 0), ("z", 1, 0, 2), ("g", 1, 1), ("z", 0, 2, 1), ("keep", 2), ("z", 1, 2, 0), ("add", 3, 0, 2),
    "acts", ("core", 3, 0), ("add", 3, 1, 0), ("g", 2, 0), ("g", 0, 2), ("add", 3, 0, 0), ("keep", 3), ("g", 3, 0),
    ("z", 4, 0, 0), ("z", 3, 1, 0), ("z", 3, 0, 1), ("a", 0, 2), ("a", 0, 3), ("z", 2, 1, 0), ("a", 1, 2),
    ("a", 1, 3), ("zown", 1), ("z", 4, 0, 1), ("g", 3, 1), ("z", 3, 2, 0), ("z", 3, 0, 2), ("a", 0, 4), ("a", 1, 4),
    ("a", 1, 5), ("g", 1, 2), ("z", 4, 1, 0), ("a", 0, 6), ("g", 1, 3), ("a", 1, 6), ("g", 3, 2), ("g", 3, 3),
    ("a", 0, 5), ("g", 2, 1), ("a", 0, 1), ("g", 0, 3), ("a", 1, 1), ("a", 1, 7), ("zsum", 1), ("a", 0, 7),
    ("score", 0), ("z", 2, 2, 0), ("zown", 2), ("zsum", 2), ("z", 4, 0, 2), ("z", 3, 1, 1), ("g", 2, 2),
    ("z", 4, 1, 1), ("z", 4, 2, 0), ("score", 1), ("zown", 3), ("zsum", 3), ("g", 2, 3), ("score", 2), ("zown", 4),
    ("zsum", 4), ("score", 3),
)


class Schedule:
    def __init__(self):
        self.actions = {}
        self.done = set()

    def at(self, when, name, action, *needs):
        self.actions[name] = (when, len(self.actions), action, needs)

    def do(self, name):
        if name in self.done:
            return
        self.done.add(name)
        for need in self.actions[name][3]:
            self.do(need)
        self.actions[name][2]()

    def run(self):
        for name in sorted(self.actions, key=lambda name: self.actions[name][:2]):
            self.do(name)


class Gather:
    def __init__(self, me, bits, view, own, send_sem, recv_sem, drains):
        self.me, self.bits, self.view, self.own = me, bits, view, own
        self.send_sem, self.recv_sem, self.drains = send_sem, recv_sem, drains
        upper = list(range(1, bits))
        self.orders = [upper + [0], upper[::-1] + [0]]

    def send(self, h, mask, bit):
        there = self.view(h, flip_mask(self.me, mask, self.bits))
        src = self.own(h) if mask == 0 else there
        slot = mask | (1 << bit)
        copy = remote(src, there, self.send_sem.at[h, slot], self.recv_sem.at[h, slot], example=flip(self.me, bit))
        copy.start()
        self.drains.append(copy.wait_send)

    def start(self):
        for place in range(self.bits - 1):
            for h in range(2):
                self.send(h, 0, self.orders[h][place])
            if place == 0:
                for h in range(2):
                    self.send(h, 0, 0)

    def before(self, h, mask):
        return mask & ~(1 << self.orders[h][last_level(mask, self.orders[h])])

    def receive(self, h, mask):
        here = self.view(h, flip_mask(self.me, mask, self.bits))
        remote(here, here, self.send_sem.at[h, mask], self.recv_sem.at[h, mask], example=flip(self.me, 0)).wait_recv()
        for bit in self.orders[h][last_level(mask, self.orders[h]) + 1 :]:
            self.send(h, mask, bit)

    def masks(self):
        pairs = [(h, mask) for mask in range(1, 1 << self.bits) for h in range(2)]
        return sorted(pairs, key=lambda p: (last_level(p[1], self.orders[p[0]]), bin(p[1]).count("1"), p[1], p[0]))


class Line:
    def __init__(self, t, n, piece, send_sem, recv_sem, drains):
        self.t, self.n, self.piece = t, n, piece
        self.send_sem, self.recv_sem, self.drains = send_sem, recv_sem, drains

    def send(self, cond, s, src, way):
        ref = self.piece(src, s)
        copy = remote(ref, ref, self.send_sem.at[way, s, src], self.recv_sem.at[s, src], tensor=self.t + 1 - 2 * way)

        @pl.when(cond)
        def _():
            copy.start()

        def drain():
            @pl.when(cond)
            def _():
                copy.wait_send()

        self.drains.append(drain)

    def own(self, s):
        self.send(self.t < self.n - 1, s, self.t, 0)
        self.send(self.t > 0, s, self.t, 1)

    def receive(self, s, d):
        for way in range(2):
            sign = 1 - 2 * way
            src = self.t - sign * d
            here = src >= 0 if way == 0 else src < self.n
            on = self.t < self.n - 1 if way == 0 else self.t > 0

            @pl.when(here)
            def _():
                ref = self.piece(src, s)
                remote(ref, ref, self.send_sem.at[way, s, src], self.recv_sem.at[s, src],
                       tensor=self.t - sign).wait_recv()

            if d < self.n - 1:
                self.send(here & on, s, src, way)


def plan_times(n, slices, chip_bits):
    hop, period, lag, step, rise = 5.5, 16.5, 21.0, 6.0, 6.0
    times = {"begin": -9.0, "own_in": 0.5, "grads_out": 0.1, "q_in": 1.5, "grads_in": 20.0}
    for k in range(n):
        times["grads", k] = 8.0 + k
    orders = [list(range(chip_bits)), list(range(chip_bits))[::-1]]
    full = [[bit + 1 for bit in order] + [0] for order in orders]
    count = 2 << chip_bits

    def gather(label, base, gap):
        for h in range(2):
            for mask in range(1, count):
                upper = last_level(mask & ~1, full[h]) + bin(mask >> 1).count("1") if mask & ~1 else 0
                times[label, h, mask] = base + gap * upper + (mask & 1)

    gather("bi", 3.0, 10.5)
    for cm in range(n):
        ready = 3.0 + 10.5 * (cm.bit_length() + (bin(cm).count("1") > 1)) + 2 if cm else 4.5
        for q in range(n - 1):
            times["z", 0, q, cm] = ready + step * q
    acts = 3.0 + 10.5 * (chip_bits + 1) + step * n
    times["acts"] = acts
    gather("a", acts + 3, 3.0)
    for s in range(slices):
        base = 4 + s * period
        times["bo", s, 0] = base - period - hop if s else 0.0
        for d in range(1, n):
            times["bo", s, d] = base + d * hop
        rot = base + lag
        for i, cm in enumerate(sorted(range(n), key=lambda m: -bin(m).count("1"))):
            times["rot", s, cm] = rot + 0.8 * i
            times["core", s, cm] = rot + 1.6 + 0.8 * i
            for h in range(2):
                times["add", s, h, cm] = rot + 1.7 + rise * level_of(cm, orders[h]) + 0.1 * i
        done = rot + 2.5 + rise * chip_bits
        times["keep", s] = done
        for d in range(n):
            times["g", s, d] = done + 4.0 * d
        a = s + 1
        for q in range(n - 1):
            for k in range(n - 1 - q):
                times["z", a, q, k] = done + 0.1 + step * (q + (k if q else 0)) + 0.5 * k
        own = done + step * n
        times["zown", a] = own - 1
        times["zsum", a] = own
        times["score", s] = own + 0.1
    if set(TUNED_ORDER) == set(times):
        times = {name: float(place) for place, name in enumerate(TUNED_ORDER)}
    return times


def whole_kernel(
    n, bits, tk,
    q_ref, bi_ref, bo_ref, grads_ref, acts_ref, eig_ref, out_ref,
    left, hop, bo_all, bi_all, prod, core_in, xy_in, fin, gall, zheld, zin, cacc, acts_t, aall, acc, red_t, red_e,
    own_sem, hop_send, hop_recv, grad_send, grad_recv, bo_send, bo_recv, g_send, g_recv, bi_send, bi_recv, a_send, a_recv,
    core_send, core_recv, xy_send, xy_recv, z_send, z_recv, rt_send, rt_recv, re_send, re_recv,
):
    me = lax.axis_index("example")
    t = lax.axis_index("tensor")
    count = 1 << bits
    pair = me // 2
    core = me % 2
    chip_bits = bits - 1
    width, wide = q_ref.shape
    share = tk // n
    slices = width // LANES
    total_rows = left.shape[0]
    half = total_rows // 2
    orders = [list(range(chip_bits)), list(range(chip_bits))[::-1]]
    drains = []
    plan = Schedule()

    tables = []
    for h in range(2):
        table = {}
        for place in range(chip_bits):
            for mask in range(1 << chip_bits):
                if level_of(mask, orders[h]) > place:
                    table[(place, mask)] = len(table)
        tables.append(table)

    bo_copies = []
    for s in range(slices):
        for h in range(2):
            copy = pltpu.make_async_copy(
                bo_ref.at[:, pl.ds(h * width + s * LANES, LANES)],
                bo_all.at[t, s, :, pl.ds(h * LANES, LANES)],
                own_sem.at[2 * s + h],
            )
            copy.start()
            bo_copies.append(copy)

    barrier = pltpu.get_barrier_semaphore()
    for k in range(1, n):
        pl.semaphore_signal(barrier, inc=1, device_id={"tensor": (t + k) % n}, device_id_type=MESH)
    for k in range(1, count):
        pl.semaphore_signal(barrier, inc=1, device_id={"example": (me + k) % count}, device_id_type=MESH)
    for i in range(width // LANES):
        rows = pl.ds(pl.multiple_of(core * width + i * LANES, LANES), LANES)
        bi_all[pair, rows, :] = bi_ref[:, i * LANES : (i + 1) * LANES].T
    pl.semaphore_wait(barrier, n + count - 2)

    def hop_copy(k):
        there = (t + k) % n
        rows = pl.ds(pl.multiple_of(there * share, share), share)
        return remote(grads_ref.at[rows], hop.at[t], hop_send.at[k], hop_recv.at[t], tensor=there)

    def grads_out():
        for k in range(1, n):
            copy = hop_copy(k)
            copy.start()
            drains.append(copy.wait_send)
        local = pltpu.make_async_copy(
            grads_ref.at[pl.ds(pl.multiple_of(t * share, share), share)], hop.at[t], hop_send.at[0]
        )
        local.start()
        local.wait()

    def grad_rows(e):
        return left.at[pl.ds(pl.multiple_of(wide + e * share, share), share)]

    def grads_on(k):
        src = (t + k) % n
        if k:
            remote(hop.at[src], hop.at[src], hop_send.at[k], hop_recv.at[src], tensor=src).wait_recv()
        for h in range(2):
            goal = 2 * src + h
            piece = hop.at[src, :, pl.ds(h * width, width)]
            copy = remote(piece, grad_rows(me), grad_send.at[k, h], grad_recv.at[me], example=goal)
            local = pltpu.make_async_copy(piece, grad_rows(me), grad_send.at[k, h])

            @pl.when(goal != me)
            def _():
                copy.start()

            @pl.when(goal == me)
            def _():
                local.start()

            def drain(copy=copy, goal=goal):
                @pl.when(goal != me)
                def _():
                    copy.wait_send()

            drains.append(drain)

    def grads_in():
        for k in range(1, count):
            src = (me + k) % count
            remote(grad_rows(src), grad_rows(src), grad_send.at[0, 0], grad_recv.at[src], example=src).wait_recv()
        for k in range(n):
            for h in range(2):
                piece = hop.at[(t + k) % n, :, pl.ds(h * width, width)]

                @pl.when(2 * ((t + k) % n) + h == me)
                def _():
                    pltpu.make_async_copy(piece, grad_rows(me), grad_send.at[k, h]).wait()

    bo_line = Line(t, n, lambda src, s: bo_all.at[src, s], bo_send, bo_recv, drains)
    g_line = Line(t, n, lambda src, s: gall.at[s, :, pl.ds(pl.multiple_of(src * share, share), share)], g_send, g_recv, drains)
    quarter = width // 2

    def bi_view(h, e):
        return bi_all.at[e // 2, pl.ds(pl.multiple_of((e % 2) * width + h * quarter, quarter), quarter)]

    bi_gather = Gather(me, bits, bi_view, lambda h: bi_view(h, me), bi_send, bi_recv, drains)

    def a_view(h, e):
        return aall.at[e, pl.ds(h * (wide // 2), wide // 2)]

    a_gather = Gather(me, bits, a_view, lambda h: a_view(h, me), a_send, a_recv, drains)

    def core_copy(s, cm):
        return remote(prod.at[s, cm, 1 - core], core_in.at[s, cm], core_send.at[s, cm], core_recv.at[s, cm],
                      example=flip(me, 0))

    def rotate(s, cm):
        owner = flip_mask(pair, cm, chip_bits)

        def step(rows):
            res = jnp.dot(left[rows, :], bo_all[owner, s], preferred_element_type=F32).astype(BF)
            prod[s, cm, 0, rows, :] = res[:, :LANES]
            prod[s, cm, 1, rows, :] = res[:, LANES:]

        tile_loop(total_rows, total_rows, step)
        copy = core_copy(s, cm)
        copy.start()
        drains.append(copy.wait_send)

    def xy_copy(s, h, mask, place):
        bit = orders[h][place]
        slot = tables[h][(place, mask & ~(1 << bit))]
        rows = pl.ds(h * half, half)
        return remote(prod.at[s, mask, core, rows], xy_in.at[s, slot, rows], xy_send.at[s, h, mask],
                      xy_recv.at[s, h, slot], example=flip(me, bit + 1))

    def add_up(s, h, mask):
        level = level_of(mask, orders[h])
        for place in range(level):
            xy_copy(s, h, mask | (1 << orders[h][place]), place).wait_recv()
        inboxes = [tables[h][(place, mask)] for place in range(level)]

        def step(rows):
            rows = pl.ds(pl.multiple_of(rows.start + h * half, rows.size), rows.size)
            total = prod[s, mask, core, rows, :].astype(F32) + core_in[s, mask, rows, :].astype(F32)
            for slot in inboxes:
                total += xy_in[s, slot, rows, :].astype(F32)
            if mask:
                prod[s, mask, core, rows, :] = total.astype(BF)
            else:
                fin[s, rows, :] = total.astype(BF)

        tile_loop(half, 128, step)
        if mask:
            copy = xy_copy(s, h, mask, level)
            copy.start()
            drains.append(copy.wait_send)

    def keep_grads(s):
        rows = pl.ds(pl.multiple_of(t * share, share), share)
        for e in range(count):
            gall[s, e, rows, :] = fin[s, wide + e * share : wide + (e + 1) * share, :]

    def z_product(a, block, rows):
        right = acts_t[...] if a == 0 else fin[a - 1, :wide, :]
        return jnp.dot(bi_all[block, rows, :], right, preferred_element_type=F32)

    def z_unit(a, q, block_up, block_down):
        up = (t == q) & (block_up > q)
        down = (t == n - 1 - q) & (block_down < n - 1 - q)
        block = jnp.where(up, block_up, block_down)
        toward = jnp.where(up, 1, -1)
        slot = block + jnp.where(up, 1, 0)
        copy = remote(zheld.at[a, block], zin.at[a, slot], z_send.at[a, block], z_recv.at[a, slot], tensor=t + toward)

        @pl.when(up | down)
        def _():
            def first(rows):
                zheld[a, block, rows, :] = z_product(a, block, rows).astype(BF)

            tile_loop(wide, 512, first)
            if q:
                remote(zin.at[a, slot], zin.at[a, slot], z_send.at[a, block], z_recv.at[a, slot],
                       tensor=t - toward).wait_recv()

                def second(rows):
                    total = zheld[a, block, rows, :].astype(F32) + zin[a, slot, rows, :].astype(F32)
                    zheld[a, block, rows, :] = total.astype(BF)

                tile_loop(wide, 256, second)
            copy.start()

        def drain():
            @pl.when(up | down)
            def _():
                copy.wait_send()

        drains.append(drain)

    def z_own_product(a):
        def first(rows):
            cacc[rows, :] = z_product(a, t, rows)

        tile_loop(wide, 512, first)

    def z_own_sum(a):
        for way in range(2):
            slot = t + 1 - way

            @pl.when(t > 0 if way == 0 else t < n - 1)
            def _():
                remote(zin.at[a, slot], zin.at[a, slot], z_send.at[a, t], z_recv.at[a, slot],
                       tensor=t - 1 + 2 * way).wait_recv()

                def second(rows):
                    cacc[rows, :] += zin[a, slot, rows, :].astype(F32)

                tile_loop(wide, 256, second)

    def keep_acts():
        def step(rows):
            aall[me, rows, :] = cacc[rows, :].astype(BF)

        tile_loop(wide, 256, step)

    def score(s):
        def step(rows):
            scaled = (cacc[rows, :] / eig_ref[rows, s * LANES : (s + 1) * LANES]).astype(BF)
            for group in range(n):
                tokens = gall[s, 2 * group : 2 * group + 2].reshape(2 * tk, LANES)
                weighted = lax.dot_general(
                    scaled, tokens, (((1,), (1,)), ((), ())), preferred_element_type=F32
                )
                for c in range(2):
                    e = 2 * group + c
                    part = weighted[:, c * tk : (c + 1) * tk] * aall[e, rows, :].astype(F32)
                    acc[e] += jnp.sum(part.reshape(-1, 8, tk), axis=0)

        tile_loop(wide, 256, step)

    def begin():
        bi_gather.start()
        for copy in bo_copies:
            copy.wait()

    def own_in():
        acc[...] = jnp.zeros_like(acc)
        acts_t[...] = acts_ref[...].T

    def q_in():
        for i in range(wide // LANES):
            left[i * LANES : (i + 1) * LANES, :] = q_ref[:, i * LANES : (i + 1) * LANES].T

    part = functools.partial
    times = plan_times(n, slices, chip_bits)
    plan.at(times["begin"], "begin", begin)
    plan.at(times["own_in"], "own_in", own_in, "begin")
    plan.at(times["grads_out"], "grads_out", grads_out, "begin")
    plan.at(times["q_in"], "q_in", q_in, "begin")
    for k in range(n):
        plan.at(times["grads", k], ("grads", k), part(grads_on, k), "grads_out")
    plan.at(times["grads_in"], "grads_in", grads_in, *[("grads", k) for k in range(n)])

    def plan_line(label, line, s, *needs):
        plan.at(times[label, s, 0], (label, s, 0), part(line.own, s), *needs)
        for d in range(1, n):
            plan.at(times[label, s, d], (label, s, d), part(line.receive, s, d), (label, s, d - 1))

    def plan_gather(label, gather, start):
        for h, mask in gather.masks():
            before = gather.before(h, mask)
            plan.at(times[label, h, mask], (label, h, mask), part(gather.receive, h, mask),
                    (label, h, before) if before else start)

    for s in range(slices):
        plan_line("bo", bo_line, s, "begin")
    plan_gather("bi", bi_gather, "begin")

    def bi_of(cm):
        return [("bi", h, 2 * cm + c) for h in range(2) for c in range(2) if cm or c]

    def plan_z(a, q, k, block_up, block_down, *needs):
        name = ("z", a, q, k)
        plan.at(times[name], name, part(z_unit, a, q, block_up, block_down), *needs)

    for cm in range(n):
        block = flip_mask(pair, cm, chip_bits)
        for q in range(n - 1):
            plan_z(0, q, cm, block, block, *(bi_of(cm) + ["own_in"] if q == 0 else [("z", 0, q - 1, cm)]))
    all_bi = [name for cm in range(n) for name in bi_of(cm)]

    def acts_in():
        z_own_product(0)
        z_own_sum(0)
        keep_acts()
        a_gather.start()

    plan.at(times["acts"], "acts", acts_in, *[("z", 0, n - 2, cm) for cm in range(n)])
    plan_gather("a", a_gather, "acts")
    all_acts = [("a", h, mask) for h, mask in a_gather.masks()]

    for s in range(slices):
        for cm in range(n):
            name = ("rot", s, cm)
            plan.at(times[name], name, part(rotate, s, cm), "q_in", "grads_in", *[("bo", s, d) for d in range(n)])
            plan.at(times["core", s, cm], ("core", s, cm), lambda s=s, cm=cm: core_copy(s, cm).wait_recv(), name)
            for h in range(2):
                level = level_of(cm, orders[h])
                sent = [("add", s, h, cm | (1 << orders[h][place])) for place in range(level)]
                plan.at(times["add", s, h, cm], ("add", s, h, cm), part(add_up, s, h, cm), ("core", s, cm), *sent)
        rotated = [("add", s, h, 0) for h in range(2)]
        plan_line("g", g_line, s, ("keep", s))
        plan.at(times["keep", s], ("keep", s), part(keep_grads, s), *rotated)
        a = s + 1
        for q in range(n - 1):
            for k in range(n - 1 - q):
                needs = rotated + all_bi if q == 0 else [("z", a, q - 1, k)]
                plan_z(a, q, k, n - 1 - k, k, *needs)
        free = ("score", s - 1) if s else "acts"
        plan.at(times["zown", a], ("zown", a), part(z_own_product, a), free, *(rotated + all_bi))
        sums = [("z", a, q, n - 2 - q) for q in range(n - 1)]
        plan.at(times["zsum", a], ("zsum", a), part(z_own_sum, a), ("zown", a), *sums)
        plan.at(times["score", s], ("score", s), part(score, s), ("zsum", a), *([("g", s, d) for d in range(n)] + all_acts))

    plan.run()

    red_t[t] = jnp.concatenate([jnp.sum(acc[e], axis=0, keepdims=True) for e in range(count)], axis=0)
    copies = []
    for k in range(1, n):
        copy = remote(red_t.at[t], red_t.at[t], rt_send.at[k - 1], rt_recv.at[t], tensor=(t + k) % n)
        copy.start()
        copies.append(copy)
    for drain in drains:
        drain()
    for k in range(1, n):
        src = (t + k) % n
        remote(red_t.at[src], red_t.at[src], rt_send.at[k - 1], rt_recv.at[src], tensor=src).wait_recv()
    total = red_t[0]
    for k in range(1, n):
        total += red_t[k]
    red_e[me] = total
    for k in range(1, count):
        copy = remote(red_e.at[me], red_e.at[me], re_send.at[k - 1], re_recv.at[me], example=(me + k) % count)
        copy.start()
        copies.append(copy)
    for k in range(1, count):
        src = (me + k) % count
        remote(red_e.at[src], red_e.at[src], re_send.at[k - 1], re_recv.at[src], example=src).wait_recv()
    total = red_e[0]
    for k in range(1, count):
        total += red_e[k]
    out_ref[...] = total
    for copy in copies:
        copy.wait_send()


def token_totals(q, bi, bo, grads, acts, eig, n, count):
    bits = count.bit_length() - 1
    width, wide = q.shape
    tk = grads.shape[0]
    slices = width // LANES
    rows = wide + 2 * tk
    chips = count // 2
    anywhere = pl.BlockSpec(memory_space=pl.ANY)
    vmem = pl.BlockSpec(memory_space=pltpu.VMEM)
    dma = pltpu.SemaphoreType.DMA
    return pl.pallas_call(
        functools.partial(whole_kernel, n, bits, tk),
        out_shape=jax.ShapeDtypeStruct((count, tk), F32),
        in_specs=[vmem, vmem, anywhere, anywhere, vmem, vmem],
        out_specs=vmem,
        scratch_shapes=[
            pltpu.VMEM((rows, width), BF),
            pltpu.VMEM((n, tk // n, wide), BF),
            pltpu.VMEM((n, slices, width, 2 * LANES), BF),
            pltpu.VMEM((n, wide, wide), BF),
            pltpu.VMEM((slices, chips, 2, rows, LANES), BF),
            pltpu.VMEM((slices, chips, rows, LANES), BF),
            pltpu.VMEM((slices, chips - 1, rows, LANES), BF),
            pltpu.VMEM((slices, rows, LANES), BF),
            pltpu.VMEM((slices, count, tk, LANES), BF),
            pltpu.VMEM((slices + 1, n, wide, LANES), BF),
            pltpu.VMEM((slices + 1, n + 1, wide, LANES), BF),
            pltpu.VMEM((wide, LANES), F32),
            pltpu.VMEM((wide, tk), BF),
            pltpu.VMEM((count, wide, tk), BF),
            pltpu.VMEM((count, 8, tk), F32),
            pltpu.VMEM((n, count, tk), F32),
            pltpu.VMEM((count, count, tk), F32),
            dma((2 * slices,)),
            dma((n,)),
            dma((n,)),
            dma((n, 2)),
            dma((count,)),
            dma((2, slices, n)),
            dma((slices, n)),
            dma((2, slices, n)),
            dma((slices, n)),
            dma((2, count)),
            dma((2, count)),
            dma((2, count)),
            dma((2, count)),
            dma((slices, chips)),
            dma((slices, chips)),
            dma((slices, 2, chips)),
            dma((slices, 2, chips)),
            dma((slices + 1, n)),
            dma((slices + 1, n + 1)),
            dma((n,)),
            dma((n,)),
            dma((count,)),
            dma((count,)),
        ],
        compiler_params=pltpu.CompilerParams(
            collective_id=0, has_side_effects=True, vmem_limit_bytes=VMEM_LIMIT
        ),
        name="token_totals",
    )(q, bi, bo, grads, acts, eig)


def body(
    queries, basis_out, basis_in, eigvals, input_fac, grad_fac, cand_slot, score_list, token_count
):
    count = lax.axis_size("example")
    n = lax.axis_size("tensor")
    my_index = lax.axis_index("example")
    cand_total = cand_slot.shape[0]
    token_len = input_fac.shape[1]
    wide = queries.shape[2]
    acts = input_fac.reshape(-1, wide)
    grads = grad_fac.reshape(-1, wide)

    by_slot = []
    for q in range(queries.shape[0]):
        totals = token_totals(queries[q], basis_in, basis_out, grads, acts, eigvals, n, count)
        by_slot.append(totals.reshape(cand_total, token_len))
    by_slot = jnp.stack(by_slot)

    my_list = lax.dynamic_index_in_dim(score_list, my_index, 0, keepdims=False)
    ids = jnp.arange(cand_total, dtype=jnp.int32)
    matches = my_list[:, None] == ids[None, :]
    my_slot = jnp.sum(jnp.where(matches, cand_slot[None, :], 0), axis=1)
    my_count = jnp.sum(jnp.where(matches, token_count[None, :], 0), axis=1)
    pick = my_slot[:, None] == ids[None, :]
    scores = jnp.sum(jnp.where(pick[None, :, :, None], by_slot[:, None], F32(0.0)), axis=2)
    live = jnp.arange(token_len, dtype=jnp.int32)[None, :] < my_count[:, None]
    return jnp.where(live[None], scores, F32(0.0))


def solution(mesh):
    in_specs = (
        P(None, "example", "tensor"),
        P("example", "tensor"),
        P("tensor", "example"),
        P("tensor", "example"),
        P("example", None, "tensor"),
        P("example", None, "tensor"),
        P(),
        P(),
        P(),
    )
    out_specs = P(None, "example", None)
    return jax.shard_map(body, mesh=mesh, in_specs=in_specs, out_specs=out_specs, check_vma=False)
```

```python
import functools

import jax
import jax.numpy as jnp
from jax import lax
from jax.experimental import pallas as pl
from jax.experimental.pallas import tpu as pltpu
from jax.sharding import PartitionSpec as P

BF = jnp.bfloat16
F32 = jnp.float32
MESH = pl.DeviceIdType.MESH
VMEM_LIMIT = 60 * 1024 * 1024
LANES = 128


def flip(index, bit):
    size = 1 << bit
    return index + size * (1 - 2 * ((index // size) % 2))


def flip_mask(index, mask, bits):
    for bit in range(bits):
        if (mask >> bit) & 1:
            index = flip(index, bit)
    return index


def level_of(mask, order):
    for place, bit in enumerate(order):
        if (mask >> bit) & 1:
            return place
    return len(order)


def last_level(mask, order):
    return max(place for place, bit in enumerate(order) if (mask >> bit) & 1)


def remote(src, dst, send, recv, **where):
    return pltpu.make_async_remote_copy(
        src_ref=src, dst_ref=dst, send_sem=send, recv_sem=recv, device_id=where, device_id_type=MESH
    )


def tile_loop(size, tile, step):
    while size % tile:
        tile //= 2

    def run(i, carry):
        step(pl.ds(pl.multiple_of(i * tile, tile), tile))
        return carry

    lax.fori_loop(0, size // tile, run, 0)


TUNED_ORDER = (
    "begin", ("bo", 0, 0), "grads_out", ("bo", 0, 1), ("grads", 0), ("grads", 1), ("bo", 1, 0), ("grads", 3),
    ("bi", 1, 1), ("bo", 0, 2), ("grads", 2), ("bo", 2, 0), "q_in", ("bo", 1, 1), "own_in", ("bi", 0, 1),
    ("z", 0, 0, 0), ("bi", 0, 4), ("bi", 1, 2), ("bo", 3, 0), "grads_in", ("bi", 1, 4), ("bi", 0, 2), ("bi", 0, 3),
    ("bi", 1, 3), ("bo", 0, 3), ("z", 0, 1, 0), ("rot", 0, 3), ("bi", 1, 5), ("core", 0, 3), ("z", 0, 0, 1),
    ("add", 0, 1, 3), ("rot", 0, 1), ("bi", 0, 5), ("rot", 0, 2), ("z", 0, 0, 2), ("add", 0, 0, 3), ("rot", 0, 0),
    ("bi", 1, 6), ("core", 0, 1), ("core", 0, 2), ("add", 0, 1, 2), ("add", 0, 0, 1), ("bi", 0, 6),
    ("add", 0, 1, 1), ("bo", 1, 2), ("bi", 1, 7), ("bo", 2, 1), ("add", 0, 0, 2), ("bi", 0, 7), ("z", 0, 1, 2),
    ("z", 0, 0, 3), ("core", 0, 0), ("bo", 1, 3), ("rot", 1, 3), ("add", 0, 1, 0), ("add", 0, 0, 0), ("keep", 0),
    ("g", 0, 0), ("z", 1, 0, 1), ("z", 1, 0, 2), ("z", 0, 1, 1), ("core", 1, 3), ("add", 1, 1, 3), ("add", 1, 0, 3),
    ("rot", 1, 0), ("bo", 2, 2), ("z", 1, 0, 0), ("bo", 3, 1), ("rot", 1, 2), ("rot", 1, 1), ("core", 1, 2),
    ("add", 1, 0, 2), ("core", 1, 1), ("add", 1, 1, 2), ("add", 1, 1, 1), ("bo", 2, 3), ("z", 0, 1, 3),
    ("rot", 2, 0), ("rot", 2, 1), ("add", 1, 0, 1), ("rot", 2, 3), ("rot", 2, 2), ("core", 2, 3), ("add", 2, 1, 3),
    ("core", 1, 0), ("add", 1, 1, 0), ("add", 1, 0, 0), ("keep", 1), ("g", 1, 0), ("add", 2, 0, 3), ("bo", 3, 2),
    ("z", 1, 1, 1), ("z", 2, 0, 0), ("core", 2, 2), ("z", 2, 0, 1), ("z", 2, 0, 2), ("core", 2, 1),
    ("add", 2, 0, 1), ("bo", 3, 3), ("z", 0, 2, 2), ("z", 0, 2, 3), ("add", 2, 1, 2), ("rot", 3, 2), ("z", 0, 2, 0),
    ("rot", 3, 3), ("rot", 3, 0), ("z", 0, 2, 1), ("z", 1, 1, 0), ("add", 2, 1, 1), ("rot", 3, 1), ("g", 1, 1),
    ("add", 2, 0, 2), ("core", 3, 3), ("add", 3, 0, 3), "acts", ("g", 0, 1), ("add", 3, 1, 3), ("core", 2, 0),
    ("add", 2, 0, 0), ("add", 2, 1, 0), ("keep", 2), ("g", 2, 0), ("z", 2, 1, 1), ("a", 0, 1), ("g", 1, 2),
    ("core", 3, 2), ("add", 3, 1, 2), ("add", 3, 0, 2), ("z", 3, 0, 0), ("core", 3, 1), ("add", 3, 0, 1),
    ("z", 2, 1, 0), ("z", 3, 0, 1), ("zown", 1), ("core", 3, 0), ("z", 1, 2, 0), ("a", 0, 2), ("g", 0, 2),
    ("g", 2, 1), ("add", 3, 1, 1), ("add", 3, 1, 0), ("add", 3, 0, 0), ("a", 1, 1), ("keep", 3), ("g", 3, 0),
    ("a", 1, 2), ("z", 3, 1, 0), ("g", 0, 3), ("z", 4, 0, 0), ("a", 1, 4), ("z", 4, 0, 1), ("z", 3, 0, 2),
    ("z", 2, 2, 0), ("a", 0, 4), ("a", 0, 5), ("g", 2, 2), ("g", 1, 3), ("a", 1, 6), ("a", 0, 6), ("g", 3, 1),
    ("z", 3, 1, 1), ("z", 3, 2, 0), ("g", 2, 3), ("a", 0, 7), ("a", 0, 3), ("a", 1, 7), ("z", 4, 0, 2), ("zsum", 1),
    ("a", 1, 5), ("a", 1, 3), ("score", 0), ("zown", 2), ("g", 3, 2), ("zsum", 2), ("z", 4, 1, 0), ("z", 4, 1, 1),
    ("z", 4, 2, 0), ("g", 3, 3), ("score", 1), ("zown", 3), ("zsum", 3), ("score", 2), ("zown", 4), ("zsum", 4),
    ("score", 3),
)


class Schedule:
    def __init__(self):
        self.actions = {}
        self.done = set()

    def at(self, when, name, action, *needs):
        self.actions[name] = (when, len(self.actions), action, needs)

    def do(self, name):
        if name in self.done:
            return
        self.done.add(name)
        for need in self.actions[name][3]:
            self.do(need)
        self.actions[name][2]()

    def run(self):
        for name in sorted(self.actions, key=lambda name: self.actions[name][:2]):
            self.do(name)


class Gather:
    def __init__(self, me, bits, view, own, send_sem, recv_sem, drains):
        self.me, self.bits, self.view, self.own = me, bits, view, own
        self.send_sem, self.recv_sem, self.drains = send_sem, recv_sem, drains
        upper = list(range(1, bits))
        self.orders = [upper + [0], upper[::-1] + [0]]

    def send(self, h, mask, bit):
        there = self.view(h, flip_mask(self.me, mask, self.bits))
        src = self.own(h) if mask == 0 else there
        slot = mask | (1 << bit)
        copy = remote(src, there, self.send_sem.at[h, slot], self.recv_sem.at[h, slot], example=flip(self.me, bit))
        copy.start()
        self.drains.append(copy.wait_send)

    def start(self):
        for place in range(self.bits - 1):
            for h in range(2):
                self.send(h, 0, self.orders[h][place])
            if place == 0:
                for h in range(2):
                    self.send(h, 0, 0)

    def before(self, h, mask):
        return mask & ~(1 << self.orders[h][last_level(mask, self.orders[h])])

    def receive(self, h, mask):
        here = self.view(h, flip_mask(self.me, mask, self.bits))
        remote(here, here, self.send_sem.at[h, mask], self.recv_sem.at[h, mask], example=flip(self.me, 0)).wait_recv()
        for bit in self.orders[h][last_level(mask, self.orders[h]) + 1 :]:
            self.send(h, mask, bit)

    def masks(self):
        pairs = [(h, mask) for mask in range(1, 1 << self.bits) for h in range(2)]
        return sorted(pairs, key=lambda p: (last_level(p[1], self.orders[p[0]]), bin(p[1]).count("1"), p[1], p[0]))


class Line:
    def __init__(self, t, n, piece, send_sem, recv_sem, drains):
        self.t, self.n, self.piece = t, n, piece
        self.send_sem, self.recv_sem, self.drains = send_sem, recv_sem, drains

    def send(self, cond, s, src, way):
        ref = self.piece(src, s)
        copy = remote(ref, ref, self.send_sem.at[way, s, src], self.recv_sem.at[s, src], tensor=self.t + 1 - 2 * way)

        @pl.when(cond)
        def _():
            copy.start()

        def drain():
            @pl.when(cond)
            def _():
                copy.wait_send()

        self.drains.append(drain)

    def own(self, s):
        self.send(self.t < self.n - 1, s, self.t, 0)
        self.send(self.t > 0, s, self.t, 1)

    def receive(self, s, d):
        for way in range(2):
            sign = 1 - 2 * way
            src = self.t - sign * d
            here = src >= 0 if way == 0 else src < self.n
            on = self.t < self.n - 1 if way == 0 else self.t > 0

            @pl.when(here)
            def _():
                ref = self.piece(src, s)
                remote(ref, ref, self.send_sem.at[way, s, src], self.recv_sem.at[s, src],
                       tensor=self.t - sign).wait_recv()

            if d < self.n - 1:
                self.send(here & on, s, src, way)


def plan_times(n, slices, chip_bits):
    hop, period, lag, step, rise = 5.5, 16.5, 21.0, 6.0, 6.0
    times = {"begin": -9.0, "own_in": 0.5, "grads_out": 0.1, "q_in": 1.5, "grads_in": 20.0}
    for k in range(n):
        times["grads", k] = 8.0 + k
    orders = [list(range(chip_bits)), list(range(chip_bits))[::-1]]
    full = [[bit + 1 for bit in order] + [0] for order in orders]
    count = 2 << chip_bits

    def gather(label, base, gap):
        for h in range(2):
            for mask in range(1, count):
                upper = last_level(mask & ~1, full[h]) + bin(mask >> 1).count("1") if mask & ~1 else 0
                times[label, h, mask] = base + gap * upper + (mask & 1)

    gather("bi", 3.0, 10.5)
    for cm in range(n):
        ready = 3.0 + 10.5 * (cm.bit_length() + (bin(cm).count("1") > 1)) + 2 if cm else 4.5
        for q in range(n - 1):
            times["z", 0, q, cm] = ready + step * q
    acts = 3.0 + 10.5 * (chip_bits + 1) + step * n
    times["acts"] = acts
    gather("a", acts + 3, 3.0)
    for s in range(slices):
        base = 4 + s * period
        times["bo", s, 0] = base - period - hop if s else 0.0
        for d in range(1, n):
            times["bo", s, d] = base + d * hop
        rot = base + lag
        for i, cm in enumerate(sorted(range(n), key=lambda m: -bin(m).count("1"))):
            times["rot", s, cm] = rot + 0.8 * i
            times["core", s, cm] = rot + 1.6 + 0.8 * i
            for h in range(2):
                times["add", s, h, cm] = rot + 1.7 + rise * level_of(cm, orders[h]) + 0.1 * i
        done = rot + 2.5 + rise * chip_bits
        times["keep", s] = done
        for d in range(n):
            times["g", s, d] = done + 4.0 * d
        a = s + 1
        for q in range(n - 1):
            for k in range(n - 1 - q):
                times["z", a, q, k] = done + 0.1 + step * (q + (k if q else 0)) + 0.5 * k
        own = done + step * n
        times["zown", a] = own - 1
        times["zsum", a] = own
        times["score", s] = own + 0.1
    if set(TUNED_ORDER) == set(times):
        times = {name: float(place) for place, name in enumerate(TUNED_ORDER)}
    return times


def choose(slot_ref, list_ref, count_ref, found, alive, fold, me):
    count, length, tk = found.shape
    token_len = fold.shape[1]
    mine = jnp.broadcast_to(list_ref[pl.ds(me, 1), :], (length, length))
    diagonal = lax.broadcasted_iota(jnp.int32, (length, length), 0) == lax.broadcasted_iota(
        jnp.int32, (length, length), 1
    )
    mine = jnp.sum(jnp.where(diagonal, mine, 0), axis=1, keepdims=True)
    total = slot_ref.shape[1]
    matches = mine == lax.broadcasted_iota(jnp.int32, (length, total), 1)
    slots = jnp.sum(jnp.where(matches, slot_ref[...], 0), axis=1, keepdims=True)
    live = jnp.sum(jnp.where(matches, count_ref[...], 0), axis=1, keepdims=True)
    place = lax.broadcasted_iota(jnp.int32, (length, tk), 1) // token_len
    for e in range(count):
        found[e] = (slots == place + e * length).astype(F32)
    alive[...] = (lax.broadcasted_iota(jnp.int32, (length, token_len), 1) < live).astype(F32)
    same = lax.broadcasted_iota(jnp.int32, (tk, token_len), 0) % token_len == lax.broadcasted_iota(
        jnp.int32, (tk, token_len), 1
    )
    fold[...] = same.astype(F32)


def listed(total, found, alive, fold):
    spread = jnp.zeros(found.shape[1:], F32)
    for e in range(found.shape[0]):
        spread += jnp.where(found[e] > 0.5, total[e : e + 1, :], F32(0.0))
    scores = jnp.dot(spread, fold[...], precision=lax.Precision.HIGHEST, preferred_element_type=F32)
    return jnp.where(alive[...] > 0.5, scores, F32(0.0))


def whole_kernel(
    n, bits, tk,
    q_hbm, bi_hbm, bo_ref, grads_ref, acts_hbm, eig_hbm,
    slot_hbm, list_hbm, count_hbm, out_ref,
    slot_ref, list_ref, count_ref, found, alive, fold, q_ref, bi_ref, acts_ref, eig_ref,
    left, hop, bo_all, bi_all, prod, core_in, xy_in, fin, gall, zheld, zin, cacc, acts_t, aall, acc, red_t, red_e,
    own_sem, hop_send, hop_recv, grad_send, grad_recv, bo_send, bo_recv, g_send, g_recv, bi_send, bi_recv, a_send, a_recv,
    core_send, core_recv, xy_send, xy_recv, z_send, z_recv, rt_send, rt_recv, re_send, re_recv,
):
    me = lax.axis_index("example")
    t = lax.axis_index("tensor")
    count = 1 << bits
    pair = me // 2
    core = me % 2
    chip_bits = bits - 1
    width, wide = q_hbm.shape
    tk = grads_ref.shape[0]
    share = tk // n
    slices = width // LANES
    total_rows = left.shape[0]
    half = total_rows // 2
    orders = [list(range(chip_bits)), list(range(chip_bits))[::-1]]
    drains, early = [], []
    plan = Schedule()

    tables = []
    for h in range(2):
        table = {}
        for place in range(chip_bits):
            for mask in range(1 << chip_bits):
                if level_of(mask, orders[h]) > place:
                    table[(place, mask)] = len(table)
        tables.append(table)

    bi_copy = pltpu.make_async_copy(bi_hbm, bi_ref, own_sem.at[2 * slices])
    bi_copy.start()
    acts_copy = pltpu.make_async_copy(acts_hbm, acts_ref, own_sem.at[2 * slices + 1])
    q_copy = pltpu.make_async_copy(q_hbm, q_ref, own_sem.at[2 * slices + 2])
    eig_copy = pltpu.make_async_copy(eig_hbm, eig_ref, own_sem.at[2 * slices + 3])
    bo_copies = []
    for s in range(slices):
        for h in range(2):
            copy = pltpu.make_async_copy(
                bo_ref.at[:, pl.ds(h * width + s * LANES, LANES)],
                bo_all.at[t, s, :, pl.ds(h * LANES, LANES)],
                own_sem.at[2 * s + h],
            )
            copy.start()
            bo_copies.append(copy)
    table_copies = [
        pltpu.make_async_copy(src, dst, own_sem.at[2 * slices + 4 + i])
        for i, (src, dst) in enumerate(((slot_hbm, slot_ref), (list_hbm, list_ref), (count_hbm, count_ref)))
    ]
    for copy in (acts_copy, q_copy, eig_copy, *table_copies):
        copy.start()

    barrier = pltpu.get_barrier_semaphore()
    for k in range(1, n):
        pl.semaphore_signal(barrier, inc=1, device_id={"tensor": (t + k) % n}, device_id_type=MESH)
    for k in range(1, count):
        pl.semaphore_signal(barrier, inc=1, device_id={"example": (me + k) % count}, device_id_type=MESH)
    bi_copy.wait()
    for i in range(width // LANES):
        rows = pl.ds(pl.multiple_of(core * width + i * LANES, LANES), LANES)
        bi_all[pair, rows, :] = bi_ref[:, i * LANES : (i + 1) * LANES].T
    pl.semaphore_wait(barrier, n + count - 2)

    def hop_copy(k):
        there = (t + k) % n
        rows = pl.ds(pl.multiple_of(there * share, share), share)
        return remote(grads_ref.at[rows], hop.at[t], hop_send.at[k], hop_recv.at[t], tensor=there)

    def grads_out():
        for k in range(1, n):
            copy = hop_copy(k)
            copy.start()
            drains.append(copy.wait_send)
        local = pltpu.make_async_copy(
            grads_ref.at[pl.ds(pl.multiple_of(t * share, share), share)], hop.at[t], hop_send.at[0]
        )
        local.start()
        local.wait()

    def grad_rows(e):
        return left.at[pl.ds(pl.multiple_of(wide + e * share, share), share)]

    def grads_on(k):
        src = (t + k) % n
        if k:
            remote(hop.at[src], hop.at[src], hop_send.at[k], hop_recv.at[src], tensor=src).wait_recv()
        for h in range(2):
            goal = 2 * src + h
            piece = hop.at[src, :, pl.ds(h * width, width)]
            copy = remote(piece, grad_rows(me), grad_send.at[k, h], grad_recv.at[me], example=goal)
            local = pltpu.make_async_copy(piece, grad_rows(me), grad_send.at[k, h])

            @pl.when(goal != me)
            def _():
                copy.start()

            @pl.when(goal == me)
            def _():
                local.start()

            def drain(copy=copy, goal=goal):
                @pl.when(goal != me)
                def _():
                    copy.wait_send()

            drains.append(drain)

    def grads_in():
        for k in range(1, count):
            src = (me + k) % count
            remote(grad_rows(src), grad_rows(src), grad_send.at[0, 0], grad_recv.at[src], example=src).wait_recv()
        for k in range(n):
            for h in range(2):
                piece = hop.at[(t + k) % n, :, pl.ds(h * width, width)]

                @pl.when(2 * ((t + k) % n) + h == me)
                def _():
                    pltpu.make_async_copy(piece, grad_rows(me), grad_send.at[k, h]).wait()

    bo_line = Line(t, n, lambda src, s: bo_all.at[src, s], bo_send, bo_recv, drains)
    g_line = Line(t, n, lambda src, s: gall.at[s, :, pl.ds(pl.multiple_of(src * share, share), share)], g_send, g_recv, drains)
    quarter = width // 2

    def bi_view(h, e):
        return bi_all.at[e // 2, pl.ds(pl.multiple_of((e % 2) * width + h * quarter, quarter), quarter)]

    bi_gather = Gather(me, bits, bi_view, lambda h: bi_view(h, me), bi_send, bi_recv, drains)

    def a_view(h, e):
        return aall.at[e, pl.ds(h * (wide // 2), wide // 2)]

    a_gather = Gather(me, bits, a_view, lambda h: a_view(h, me), a_send, a_recv, drains)

    def core_copy(s, cm):
        return remote(prod.at[s, cm, 1 - core], core_in.at[s, cm], core_send.at[s, cm], core_recv.at[s, cm],
                      example=flip(me, 0))

    def rotate(s, cm):
        owner = flip_mask(pair, cm, chip_bits)

        def step(rows):
            res = jnp.dot(left[rows, :], bo_all[owner, s], preferred_element_type=F32).astype(BF)
            prod[s, cm, 0, rows, :] = res[:, :LANES]
            prod[s, cm, 1, rows, :] = res[:, LANES:]

        tile_loop(total_rows, total_rows, step)
        copy = core_copy(s, cm)
        copy.start()
        drains.append(copy.wait_send)

    def xy_copy(s, h, mask, place):
        bit = orders[h][place]
        slot = tables[h][(place, mask & ~(1 << bit))]
        rows = pl.ds(h * half, half)
        return remote(prod.at[s, mask, core, rows], xy_in.at[s, slot, rows], xy_send.at[s, h, mask],
                      xy_recv.at[s, h, slot], example=flip(me, bit + 1))

    def add_up(s, h, mask):
        level = level_of(mask, orders[h])
        for place in range(level):
            xy_copy(s, h, mask | (1 << orders[h][place]), place).wait_recv()
        inboxes = [tables[h][(place, mask)] for place in range(level)]

        def step(rows):
            rows = pl.ds(pl.multiple_of(rows.start + h * half, rows.size), rows.size)
            total = prod[s, mask, core, rows, :].astype(F32) + core_in[s, mask, rows, :].astype(F32)
            for slot in inboxes:
                total += xy_in[s, slot, rows, :].astype(F32)
            if mask:
                prod[s, mask, core, rows, :] = total.astype(BF)
            else:
                fin[s, rows, :] = total.astype(BF)

        tile_loop(half, 128, step)
        if mask:
            copy = xy_copy(s, h, mask, level)
            copy.start()
            drains.append(copy.wait_send)

    def keep_grads(s):
        rows = pl.ds(pl.multiple_of(t * share, share), share)
        for e in range(count):
            gall[s, e, rows, :] = fin[s, wide + e * share : wide + (e + 1) * share, :]

    def z_product(a, block, rows):
        right = acts_t[...] if a == 0 else fin[a - 1, :wide, :]
        return jnp.dot(bi_all[block, rows, :], right, preferred_element_type=F32)

    def z_unit(a, q, block_up, block_down):
        up = (t == q) & (block_up > q)
        down = (t == n - 1 - q) & (block_down < n - 1 - q)
        block = jnp.where(up, block_up, block_down)
        toward = jnp.where(up, 1, -1)
        slot = block + jnp.where(up, 1, 0)
        copy = remote(zheld.at[a, block], zin.at[a, slot], z_send.at[a, block], z_recv.at[a, slot], tensor=t + toward)

        @pl.when(up | down)
        def _():
            def first(rows):
                zheld[a, block, rows, :] = z_product(a, block, rows).astype(BF)

            tile_loop(wide, 512, first)
            if q:
                remote(zin.at[a, slot], zin.at[a, slot], z_send.at[a, block], z_recv.at[a, slot],
                       tensor=t - toward).wait_recv()

                def second(rows):
                    total = zheld[a, block, rows, :].astype(F32) + zin[a, slot, rows, :].astype(F32)
                    zheld[a, block, rows, :] = total.astype(BF)

                tile_loop(wide, 256, second)
            copy.start()

        def drain():
            @pl.when(up | down)
            def _():
                copy.wait_send()

        drains.append(drain)

    def z_own_product(a):
        def first(rows):
            cacc[rows, :] = z_product(a, t, rows)

        tile_loop(wide, 512, first)

    def z_own_sum(a):
        for way in range(2):
            slot = t + 1 - way

            @pl.when(t > 0 if way == 0 else t < n - 1)
            def _():
                remote(zin.at[a, slot], zin.at[a, slot], z_send.at[a, t], z_recv.at[a, slot],
                       tensor=t - 1 + 2 * way).wait_recv()

                def second(rows):
                    cacc[rows, :] += zin[a, slot, rows, :].astype(F32)

                tile_loop(wide, 256, second)

    def keep_acts():
        def step(rows):
            aall[me, rows, :] = cacc[rows, :].astype(BF)

        tile_loop(wide, 256, step)

    def score(s):
        def step(rows):
            scaled = (cacc[rows, :] / eig_ref[rows, s * LANES : (s + 1) * LANES]).astype(BF)
            for group in range(n):
                tokens = gall[s, 2 * group : 2 * group + 2].reshape(2 * tk, LANES)
                weighted = lax.dot_general(
                    scaled, tokens, (((1,), (1,)), ((), ())), preferred_element_type=F32
                )
                for c in range(2):
                    e = 2 * group + c
                    part = weighted[:, c * tk : (c + 1) * tk] * aall[e, rows, :].astype(F32)
                    acc[e] += jnp.sum(part.reshape(-1, 8, tk), axis=0)

        tile_loop(wide, 256, step)

    def set_aside(s):
        early.extend(drains)
        drains.clear()
        score(s)

    def last_product(a):
        for drain in early:
            drain()
        z_own_product(a)

    def begin():
        bi_gather.start()
        for copy in bo_copies:
            copy.wait()

    def own_in():
        acc[...] = jnp.zeros_like(acc)
        acts_copy.wait()
        acts_t[...] = acts_ref[...].T
        eig_copy.wait()
        for copy in table_copies:
            copy.wait()
        choose(slot_ref, list_ref, count_ref, found, alive, fold, me)

    def q_in():
        q_copy.wait()
        for i in range(wide // LANES):
            left[i * LANES : (i + 1) * LANES, :] = q_ref[:, i * LANES : (i + 1) * LANES].T

    part = functools.partial
    times = plan_times(n, slices, chip_bits)
    plan.at(times["begin"], "begin", begin)
    plan.at(times["own_in"], "own_in", own_in, "begin")
    plan.at(times["grads_out"], "grads_out", grads_out, "begin")
    plan.at(times["q_in"], "q_in", q_in, "begin")
    for k in range(n):
        plan.at(times["grads", k], ("grads", k), part(grads_on, k), "grads_out")
    plan.at(times["grads_in"], "grads_in", grads_in, *[("grads", k) for k in range(n)])

    def plan_line(label, line, s, *needs):
        plan.at(times[label, s, 0], (label, s, 0), part(line.own, s), *needs)
        for d in range(1, n):
            plan.at(times[label, s, d], (label, s, d), part(line.receive, s, d), (label, s, d - 1))

    def plan_gather(label, gather, start):
        for h, mask in gather.masks():
            before = gather.before(h, mask)
            plan.at(times[label, h, mask], (label, h, mask), part(gather.receive, h, mask),
                    (label, h, before) if before else start)

    for s in range(slices):
        plan_line("bo", bo_line, s, "begin")
    plan_gather("bi", bi_gather, "begin")

    def bi_of(cm):
        return [("bi", h, 2 * cm + c) for h in range(2) for c in range(2) if cm or c]

    def plan_z(a, q, k, block_up, block_down, *needs):
        name = ("z", a, q, k)
        plan.at(times[name], name, part(z_unit, a, q, block_up, block_down), *needs)

    for cm in range(n):
        block = flip_mask(pair, cm, chip_bits)
        for q in range(n - 1):
            plan_z(0, q, cm, block, block, *(bi_of(cm) + ["own_in"] if q == 0 else [("z", 0, q - 1, cm)]))
    all_bi = [name for cm in range(n) for name in bi_of(cm)]

    def acts_in():
        z_own_product(0)
        z_own_sum(0)
        keep_acts()
        a_gather.start()

    plan.at(times["acts"], "acts", acts_in, *[("z", 0, n - 2, cm) for cm in range(n)])
    plan_gather("a", a_gather, "acts")
    all_acts = [("a", h, mask) for h, mask in a_gather.masks()]

    for s in range(slices):
        for cm in range(n):
            name = ("rot", s, cm)
            plan.at(times[name], name, part(rotate, s, cm), "q_in", "grads_in", *[("bo", s, d) for d in range(n)])
            plan.at(times["core", s, cm], ("core", s, cm), lambda s=s, cm=cm: core_copy(s, cm).wait_recv(), name)
            for h in range(2):
                level = level_of(cm, orders[h])
                sent = [("add", s, h, cm | (1 << orders[h][place])) for place in range(level)]
                plan.at(times["add", s, h, cm], ("add", s, h, cm), part(add_up, s, h, cm), ("core", s, cm), *sent)
        rotated = [("add", s, h, 0) for h in range(2)]
        plan_line("g", g_line, s, ("keep", s))
        plan.at(times["keep", s], ("keep", s), part(keep_grads, s), *rotated)
        a = s + 1
        for q in range(n - 1):
            for k in range(n - 1 - q):
                needs = rotated + all_bi if q == 0 else [("z", a, q - 1, k)]
                plan_z(a, q, k, n - 1 - k, k, *needs)
        free = ("score", s - 1) if s else "acts"
        plan.at(times["zown", a], ("zown", a), part(last_product if a == slices else z_own_product, a), free, *(rotated + all_bi))
        sums = [("z", a, q, n - 2 - q) for q in range(n - 1)]
        plan.at(times["zsum", a], ("zsum", a), part(z_own_sum, a), ("zown", a), *sums)
        plan.at(times["score", s], ("score", s), part(set_aside if s == max(slices - 3, 0) else score, s), ("zsum", a), *([("g", s, d) for d in range(n)] + all_acts))

    plan.run()

    red_t[t] = jnp.concatenate([jnp.sum(acc[e], axis=0, keepdims=True) for e in range(count)], axis=0)
    copies = []
    for k in range(1, n):
        copy = remote(red_t.at[t], red_t.at[t], rt_send.at[k - 1], rt_recv.at[t], tensor=(t + k) % n)
        copy.start()
        copies.append(copy)
    for drain in drains:
        drain()
    for k in range(1, n):
        src = (t + k) % n
        remote(red_t.at[src], red_t.at[src], rt_send.at[k - 1], rt_recv.at[src], tensor=src).wait_recv()
    total = red_t[0]
    for k in range(1, n):
        total += red_t[k]
    red_e[me] = total
    for k in range(1, count):
        copy = remote(red_e.at[me], red_e.at[me], re_send.at[k - 1], re_recv.at[me], example=(me + k) % count)
        copy.start()
        copies.append(copy)
    for k in range(1, count):
        src = (me + k) % count
        remote(red_e.at[src], red_e.at[src], re_send.at[k - 1], re_recv.at[src], example=src).wait_recv()
    total = red_e[0]
    for k in range(1, count):
        total += red_e[k]
    out_ref[...] = listed(total, found, alive, fold)
    for copy in copies:
        copy.wait_send()


def list_scores(q, bi, bo, grads, acts, eig, slot, lists, live, token_len, n, count):
    bits = count.bit_length() - 1
    width, wide = q.shape
    tk = grads.shape[0]
    slices = width // LANES
    rows = wide + 2 * tk
    chips = count // 2
    anywhere = pl.BlockSpec(memory_space=pl.ANY)
    vmem = pl.BlockSpec(memory_space=pltpu.VMEM)
    dma = pltpu.SemaphoreType.DMA
    return pl.pallas_call(
        functools.partial(whole_kernel, n, bits, tk),
        out_shape=jax.ShapeDtypeStruct((tk // token_len, token_len), F32),
        in_specs=[anywhere] * 9,
        out_specs=vmem,
        scratch_shapes=[
            pltpu.VMEM((1, slot.shape[0]), jnp.int32),
            pltpu.VMEM(lists.shape, jnp.int32),
            pltpu.VMEM((1, live.shape[0]), jnp.int32),
            pltpu.VMEM((count, tk // token_len, tk), F32),
            pltpu.VMEM((tk // token_len, token_len), F32),
            pltpu.VMEM((tk, token_len), F32),
            pltpu.VMEM((width, wide), BF),
            pltpu.VMEM((wide, width), BF),
            pltpu.VMEM((tk, wide), BF),
            pltpu.VMEM((wide, width), F32),
            pltpu.VMEM((rows, width), BF),
            pltpu.VMEM((n, tk // n, wide), BF),
            pltpu.VMEM((n, slices, width, 2 * LANES), BF),
            pltpu.VMEM((n, wide, wide), BF),
            pltpu.VMEM((slices, chips, 2, rows, LANES), BF),
            pltpu.VMEM((slices, chips, rows, LANES), BF),
            pltpu.VMEM((slices, chips - 1, rows, LANES), BF),
            pltpu.VMEM((slices, rows, LANES), BF),
            pltpu.VMEM((slices, count, tk, LANES), BF),
            pltpu.VMEM((slices + 1, n, wide, LANES), BF),
            pltpu.VMEM((slices + 1, n + 1, wide, LANES), BF),
            pltpu.VMEM((wide, LANES), F32),
            pltpu.VMEM((wide, tk), BF),
            pltpu.VMEM((count, wide, tk), BF),
            pltpu.VMEM((count, 8, tk), F32),
            pltpu.VMEM((n, count, tk), F32),
            pltpu.VMEM((count, count, tk), F32),
            dma((2 * slices + 7,)),
            dma((n,)),
            dma((n,)),
            dma((n, 2)),
            dma((count,)),
            dma((2, slices, n)),
            dma((slices, n)),
            dma((2, slices, n)),
            dma((slices, n)),
            dma((2, count)),
            dma((2, count)),
            dma((2, count)),
            dma((2, count)),
            dma((slices, chips)),
            dma((slices, chips)),
            dma((slices, 2, chips)),
            dma((slices, 2, chips)),
            dma((slices + 1, n)),
            dma((slices + 1, n + 1)),
            dma((n,)),
            dma((n,)),
            dma((count,)),
            dma((count,)),
        ],
        compiler_params=pltpu.CompilerParams(
            collective_id=0, has_side_effects=True, vmem_limit_bytes=VMEM_LIMIT
        ),
        name="list_scores",
    )(q, bi, bo, grads, acts, eig, slot.reshape(1, -1), lists, live.reshape(1, -1))


def body(
    queries, basis_out, basis_in, eigvals, input_fac, grad_fac, cand_slot, score_list, token_count
):
    count = lax.axis_size("example")
    n = lax.axis_size("tensor")
    token_len = input_fac.shape[1]
    wide = queries.shape[2]
    acts = input_fac.reshape(-1, wide)
    grads = grad_fac.reshape(-1, wide)
    scores = [
        list_scores(queries[q], basis_in, basis_out, grads, acts, eigvals, cand_slot, score_list, token_count,
                    token_len, n, count)
        for q in range(queries.shape[0])
    ]
    return jnp.stack(scores)


def solution(mesh):
    in_specs = (
        P(None, "example", "tensor"),
        P("example", "tensor"),
        P("tensor", "example"),
        P("tensor", "example"),
        P("example", None, "tensor"),
        P("example", None, "tensor"),
        P(),
        P(),
        P(),
    )
    out_specs = P(None, "example", None)
    return jax.shard_map(body, mesh=mesh, in_specs=in_specs, out_specs=out_specs, check_vma=False)
```

```python
import functools

import jax
import jax.numpy as jnp
from jax import lax
from jax.experimental import pallas as pl
from jax.experimental.pallas import tpu as pltpu
from jax.sharding import PartitionSpec as P

BF = jnp.bfloat16
F32 = jnp.float32
MESH = pl.DeviceIdType.MESH
VMEM_LIMIT = 60 * 1024 * 1024
LANES = 128


def flip(index, bit):
    size = 1 << bit
    return index + size * (1 - 2 * ((index // size) % 2))


def flip_mask(index, mask, bits):
    for bit in range(bits):
        if (mask >> bit) & 1:
            index = flip(index, bit)
    return index


def level_of(mask, order):
    for place, bit in enumerate(order):
        if (mask >> bit) & 1:
            return place
    return len(order)


def last_level(mask, order):
    return max(place for place, bit in enumerate(order) if (mask >> bit) & 1)


def remote(src, dst, send, recv, **where):
    return pltpu.make_async_remote_copy(
        src_ref=src, dst_ref=dst, send_sem=send, recv_sem=recv, device_id=where, device_id_type=MESH
    )


def tile_loop(size, tile, step):
    while size % tile:
        tile //= 2

    def run(i, carry):
        step(pl.ds(pl.multiple_of(i * tile, tile), tile))
        return carry

    lax.fori_loop(0, size // tile, run, 0)


TUNED_ORDER = (
    "begin", ("bo", 0, 0), "grads_out", "q_in", ("bo", 0, 1), ("grads", 1), ("bo", 1, 0), ("grads", 2),
    ("bo", 0, 2), ("grads", 3), ("bo", 2, 0), ("bi", 1, 1), ("grads", 0), ("bo", 1, 1), ("bi", 1, 4), ("bi", 0, 2),
    "own_in", ("bi", 0, 1), ("z", 0, 0, 0), ("bo", 3, 0), "grads_in", ("bo", 0, 3), ("rot", 0, 2), ("bi", 1, 2),
    ("rot", 0, 0), ("rot", 0, 1), ("bi", 0, 4), ("bi", 1, 3), ("bi", 1, 5), ("rot", 0, 3), ("bi", 0, 3),
    ("z", 0, 0, 1), ("core", 0, 3), ("add", 0, 1, 3), ("bi", 0, 5), ("z", 0, 0, 2), ("core", 0, 2),
    ("add", 0, 1, 2), ("z", 0, 1, 0), ("add", 0, 0, 3), ("bi", 1, 6), ("bo", 1, 2), ("core", 0, 1),
    ("add", 0, 0, 1), ("bo", 2, 1), ("bi", 0, 6), ("bi", 1, 7), ("z", 0, 1, 2), ("add", 0, 0, 2), ("add", 0, 1, 1),
    ("z", 0, 1, 1), ("bi", 0, 7), ("z", 0, 0, 3), ("core", 0, 0), ("add", 0, 0, 0), ("add", 0, 1, 0), ("keep", 0),
    ("g", 0, 0), ("z", 1, 0, 0), ("bo", 1, 3), ("rot", 1, 1), ("z", 1, 0, 2), ("rot", 1, 3), ("rot", 1, 2),
    ("core", 1, 3), ("add", 1, 0, 3), ("add", 1, 1, 3), ("bo", 2, 2), ("bo", 3, 1), ("core", 1, 2), ("core", 1, 1),
    ("add", 1, 0, 1), ("add", 1, 1, 2), ("z", 0, 1, 3), ("z", 1, 0, 1), ("z", 1, 1, 0), ("add", 1, 0, 2),
    ("add", 1, 1, 1), ("rot", 1, 0), ("core", 1, 0), ("bo", 2, 3), ("rot", 2, 2), ("rot", 2, 3), ("add", 1, 1, 0),
    ("add", 1, 0, 0), ("keep", 1), ("g", 1, 0), ("z", 2, 0, 0), ("g", 0, 1), ("z", 2, 0, 1), ("core", 2, 3),
    ("add", 2, 1, 3), ("add", 2, 0, 3), ("core", 2, 2), ("add", 2, 1, 2), ("z", 2, 0, 2), ("bo", 3, 2),
    ("rot", 2, 0), ("core", 2, 0), ("rot", 2, 1), ("z", 0, 2, 3), ("core", 2, 1), ("add", 2, 0, 1), ("bo", 3, 3),
    ("rot", 3, 2), ("z", 1, 1, 1), ("g", 1, 1), ("rot", 3, 1), ("add", 2, 0, 2), ("add", 2, 1, 1), ("z", 2, 1, 0),
    ("z", 0, 2, 2), ("core", 3, 2), ("add", 3, 1, 2), ("rot", 3, 3), ("core", 3, 1), ("add", 3, 0, 1),
    ("z", 0, 2, 0), ("z", 0, 2, 1), ("core", 3, 3), ("add", 2, 0, 0), ("add", 2, 1, 0), ("add", 3, 1, 3),
    ("keep", 2), ("g", 2, 0), ("z", 2, 1, 1), ("z", 1, 2, 0), ("add", 3, 0, 3), ("z", 3, 0, 0), ("rot", 3, 0),
    ("z", 2, 2, 0), ("g", 1, 2), ("add", 3, 1, 1), ("z", 3, 0, 1), ("g", 2, 1), ("add", 3, 0, 2), "acts",
    ("core", 3, 0), ("add", 3, 0, 0), ("add", 3, 1, 0), ("keep", 3), ("g", 3, 0), ("z", 3, 1, 0), ("a", 1, 1),
    ("z", 4, 0, 0), ("zown", 1), ("z", 4, 0, 1), ("z", 3, 1, 1), ("a", 1, 4), ("g", 2, 2), ("g", 0, 2), ("a", 0, 2),
    ("a", 1, 2), ("g", 3, 1), ("g", 1, 3), ("z", 3, 2, 0), ("z", 3, 0, 2), ("a", 1, 3), ("a", 0, 6), ("z", 4, 1, 0),
    ("g", 0, 3), ("a", 0, 4), ("a", 1, 6), ("a", 0, 5), ("a", 1, 7), ("g", 3, 2), ("a", 0, 7), ("g", 3, 3),
    ("z", 4, 0, 2), ("a", 0, 1), ("zsum", 1), ("a", 0, 3), ("a", 1, 5), ("score", 0), ("zown", 2), ("z", 4, 1, 1),
    ("z", 4, 2, 0), ("zsum", 2), ("g", 2, 3), ("score", 1), ("zown", 3), ("zsum", 3), ("score", 2), ("zown", 4),
    ("zsum", 4), ("score", 3),
)


class Schedule:
    def __init__(self):
        self.actions = {}
        self.done = set()

    def at(self, when, name, action, *needs):
        self.actions[name] = (when, len(self.actions), action, needs)

    def do(self, name):
        if name in self.done:
            return
        self.done.add(name)
        for need in self.actions[name][3]:
            self.do(need)
        self.actions[name][2]()

    def run(self):
        for name in sorted(self.actions, key=lambda name: self.actions[name][:2]):
            self.do(name)


class Gather:
    def __init__(self, me, bits, view, own, send_sem, recv_sem, drains):
        self.me, self.bits, self.view, self.own = me, bits, view, own
        self.send_sem, self.recv_sem, self.drains = send_sem, recv_sem, drains
        upper = list(range(1, bits))
        self.orders = [upper + [0], upper[::-1] + [0]]

    def send(self, h, mask, bit):
        there = self.view(h, flip_mask(self.me, mask, self.bits))
        src = self.own(h) if mask == 0 else there
        slot = mask | (1 << bit)
        copy = remote(src, there, self.send_sem.at[h, slot], self.recv_sem.at[h, slot], example=flip(self.me, bit))
        copy.start()
        self.drains.append(copy.wait_send)

    def start(self):
        for place in range(self.bits - 1):
            for h in range(2):
                self.send(h, 0, self.orders[h][place])
            if place == 0:
                for h in range(2):
                    self.send(h, 0, 0)

    def before(self, h, mask):
        return mask & ~(1 << self.orders[h][last_level(mask, self.orders[h])])

    def receive(self, h, mask):
        here = self.view(h, flip_mask(self.me, mask, self.bits))
        remote(here, here, self.send_sem.at[h, mask], self.recv_sem.at[h, mask], example=flip(self.me, 0)).wait_recv()
        for bit in self.orders[h][last_level(mask, self.orders[h]) + 1 :]:
            self.send(h, mask, bit)

    def masks(self):
        pairs = [(h, mask) for mask in range(1, 1 << self.bits) for h in range(2)]
        return sorted(pairs, key=lambda p: (last_level(p[1], self.orders[p[0]]), bin(p[1]).count("1"), p[1], p[0]))


class Line:
    def __init__(self, t, n, piece, send_sem, recv_sem, drains):
        self.t, self.n, self.piece = t, n, piece
        self.send_sem, self.recv_sem, self.drains = send_sem, recv_sem, drains

    def send(self, cond, s, src, way):
        ref = self.piece(src, s)
        copy = remote(ref, ref, self.send_sem.at[way, s, src], self.recv_sem.at[s, src], tensor=self.t + 1 - 2 * way)

        @pl.when(cond)
        def _():
            copy.start()

        def drain():
            @pl.when(cond)
            def _():
                copy.wait_send()

        self.drains.append(drain)

    def own(self, s):
        self.send(self.t < self.n - 1, s, self.t, 0)
        self.send(self.t > 0, s, self.t, 1)

    def receive(self, s, d):
        for way in range(2):
            sign = 1 - 2 * way
            src = self.t - sign * d
            here = src >= 0 if way == 0 else src < self.n
            on = self.t < self.n - 1 if way == 0 else self.t > 0

            @pl.when(here)
            def _():
                ref = self.piece(src, s)
                remote(ref, ref, self.send_sem.at[way, s, src], self.recv_sem.at[s, src],
                       tensor=self.t - sign).wait_recv()

            if d < self.n - 1:
                self.send(here & on, s, src, way)


def plan_times(n, slices, chip_bits):
    hop, period, lag, step, rise = 5.5, 16.5, 21.0, 6.0, 6.0
    times = {"begin": -9.0, "own_in": 0.5, "grads_out": 0.1, "q_in": 1.5, "grads_in": 20.0}
    for k in range(n):
        times["grads", k] = 8.0 + k
    orders = [list(range(chip_bits)), list(range(chip_bits))[::-1]]
    full = [[bit + 1 for bit in order] + [0] for order in orders]
    count = 2 << chip_bits

    def gather(label, base, gap):
        for h in range(2):
            for mask in range(1, count):
                upper = last_level(mask & ~1, full[h]) + bin(mask >> 1).count("1") if mask & ~1 else 0
                times[label, h, mask] = base + gap * upper + (mask & 1)

    gather("bi", 3.0, 10.5)
    for cm in range(n):
        ready = 3.0 + 10.5 * (cm.bit_length() + (bin(cm).count("1") > 1)) + 2 if cm else 4.5
        for q in range(n - 1):
            times["z", 0, q, cm] = ready + step * q
    acts = 3.0 + 10.5 * (chip_bits + 1) + step * n
    times["acts"] = acts
    gather("a", acts + 3, 3.0)
    for s in range(slices):
        base = 4 + s * period
        times["bo", s, 0] = base - period - hop if s else 0.0
        for d in range(1, n):
            times["bo", s, d] = base + d * hop
        rot = base + lag
        for i, cm in enumerate(sorted(range(n), key=lambda m: -bin(m).count("1"))):
            times["rot", s, cm] = rot + 0.8 * i
            times["core", s, cm] = rot + 1.6 + 0.8 * i
            for h in range(2):
                times["add", s, h, cm] = rot + 1.7 + rise * level_of(cm, orders[h]) + 0.1 * i
        done = rot + 2.5 + rise * chip_bits
        times["keep", s] = done
        for d in range(n):
            times["g", s, d] = done + 4.0 * d
        a = s + 1
        for q in range(n - 1):
            for k in range(n - 1 - q):
                times["z", a, q, k] = done + 0.1 + step * (q + (k if q else 0)) + 0.5 * k
        own = done + step * n
        times["zown", a] = own - 1
        times["zsum", a] = own
        times["score", s] = own + 0.1
    if set(TUNED_ORDER) == set(times):
        times = {name: float(place) for place, name in enumerate(TUNED_ORDER)}
    return times


def choose(slot_ref, list_ref, count_ref, found, alive, fold, me):
    count, length, tk = found.shape
    token_len = fold.shape[1]
    mine = jnp.broadcast_to(list_ref[pl.ds(me, 1), :], (length, length))
    diagonal = lax.broadcasted_iota(jnp.int32, (length, length), 0) == lax.broadcasted_iota(
        jnp.int32, (length, length), 1
    )
    mine = jnp.sum(jnp.where(diagonal, mine, 0), axis=1, keepdims=True)
    total = slot_ref.shape[1]
    matches = mine == lax.broadcasted_iota(jnp.int32, (length, total), 1)
    slots = jnp.sum(jnp.where(matches, slot_ref[...], 0), axis=1, keepdims=True)
    live = jnp.sum(jnp.where(matches, count_ref[...], 0), axis=1, keepdims=True)
    place = lax.broadcasted_iota(jnp.int32, (length, tk), 1) // token_len
    for e in range(count):
        found[e] = (slots == place + e * length).astype(F32)
    alive[...] = (lax.broadcasted_iota(jnp.int32, (length, token_len), 1) < live).astype(F32)
    same = lax.broadcasted_iota(jnp.int32, (tk, token_len), 0) % token_len == lax.broadcasted_iota(
        jnp.int32, (tk, token_len), 1
    )
    fold[...] = same.astype(F32)


def listed(total, found, alive, fold):
    spread = jnp.zeros(found.shape[1:], F32)
    for e in range(found.shape[0]):
        spread += jnp.where(found[e] > 0.5, total[e : e + 1, :], F32(0.0))
    scores = jnp.dot(spread, fold[...], precision=lax.Precision.HIGHEST, preferred_element_type=F32)
    return jnp.where(alive[...] > 0.5, scores, F32(0.0))


def whole_kernel(
    n, bits, tk,
    q_hbm, bi_hbm, bo_ref, grads_ref, acts_hbm, eig_hbm,
    slot_hbm, list_hbm, count_hbm, out_ref,
    slot_ref, list_ref, count_ref, found, alive, fold, q_ref, bi_ref, acts_ref, eig_ref,
    left, hop, bo_all, bi_all, prod, core_in, xy_in, fin, gall, zheld, zin, cacc, acts_t, aall, acc, red_t, red_e,
    own_sem, hop_send, hop_recv, grad_send, grad_recv, bo_send, bo_recv, g_send, g_recv, bi_send, bi_recv, a_send, a_recv,
    core_send, core_recv, xy_send, xy_recv, z_send, z_recv, rt_send, rt_recv, re_send, re_recv,
):
    me = lax.axis_index("example")
    t = lax.axis_index("tensor")
    count = 1 << bits
    pair = me // 2
    core = me % 2
    chip_bits = bits - 1
    width, wide = q_hbm.shape
    tk = grads_ref.shape[0]
    share = tk // n
    slices = width // LANES
    total_rows = left.shape[0]
    half = total_rows // 2
    orders = [list(range(chip_bits)), list(range(chip_bits))[::-1]]
    drains, early = [], []
    plan = Schedule()

    tables = []
    for h in range(2):
        table = {}
        for place in range(chip_bits):
            for mask in range(1 << chip_bits):
                if level_of(mask, orders[h]) > place:
                    table[(place, mask)] = len(table)
        tables.append(table)

    bi_copy = pltpu.make_async_copy(bi_hbm, bi_ref, own_sem.at[2 * slices])
    bi_copy.start()
    acts_copy = pltpu.make_async_copy(acts_hbm, acts_ref, own_sem.at[2 * slices + 1])
    q_copy = pltpu.make_async_copy(q_hbm, q_ref, own_sem.at[2 * slices + 2])
    eig_copy = pltpu.make_async_copy(eig_hbm, eig_ref, own_sem.at[2 * slices + 3])
    bo_copies = []
    for s in range(slices):
        for h in range(2):
            copy = pltpu.make_async_copy(
                bo_ref.at[:, pl.ds(h * width + s * LANES, LANES)],
                bo_all.at[t, s, :, pl.ds(h * LANES, LANES)],
                own_sem.at[2 * s + h],
            )
            copy.start()
            bo_copies.append(copy)
    table_copies = [
        pltpu.make_async_copy(src, dst, own_sem.at[2 * slices + 4 + i])
        for i, (src, dst) in enumerate(((slot_hbm, slot_ref), (list_hbm, list_ref), (count_hbm, count_ref)))
    ]
    for copy in (acts_copy, q_copy, eig_copy, *table_copies):
        copy.start()

    barrier = pltpu.get_barrier_semaphore()
    for k in range(1, n):
        pl.semaphore_signal(barrier, inc=1, device_id={"tensor": (t + k) % n}, device_id_type=MESH)
    for k in range(1, count):
        pl.semaphore_signal(barrier, inc=1, device_id={"example": (me + k) % count}, device_id_type=MESH)
    bi_copy.wait()
    for i in range(width // LANES):
        rows = pl.ds(pl.multiple_of(core * width + i * LANES, LANES), LANES)
        bi_all[pair, rows, :] = bi_ref[:, i * LANES : (i + 1) * LANES].T
    pl.semaphore_wait(barrier, n + count - 2)

    def hop_copy(k):
        there = (t + k) % n
        rows = pl.ds(pl.multiple_of(there * share, share), share)
        return remote(grads_ref.at[rows], hop.at[t], hop_send.at[k], hop_recv.at[t], tensor=there)

    def grads_out():
        for k in range(1, n):
            copy = hop_copy(k)
            copy.start()
            drains.append(copy.wait_send)
        local = pltpu.make_async_copy(
            grads_ref.at[pl.ds(pl.multiple_of(t * share, share), share)], hop.at[t], hop_send.at[0]
        )
        local.start()
        local.wait()

    def grad_rows(e):
        return left.at[pl.ds(pl.multiple_of(wide + e * share, share), share)]

    def grads_on(k):
        src = (t + k) % n
        if k:
            remote(hop.at[src], hop.at[src], hop_send.at[k], hop_recv.at[src], tensor=src).wait_recv()
        for h in range(2):
            goal = 2 * src + h
            piece = hop.at[src, :, pl.ds(h * width, width)]
            copy = remote(piece, grad_rows(me), grad_send.at[k, h], grad_recv.at[me], example=goal)
            local = pltpu.make_async_copy(piece, grad_rows(me), grad_send.at[k, h])

            @pl.when(goal != me)
            def _():
                copy.start()

            @pl.when(goal == me)
            def _():
                local.start()

            def drain(copy=copy, goal=goal):
                @pl.when(goal != me)
                def _():
                    copy.wait_send()

            drains.append(drain)

    def grads_in():
        for k in range(1, count):
            src = (me + k) % count
            remote(grad_rows(src), grad_rows(src), grad_send.at[0, 0], grad_recv.at[src], example=src).wait_recv()
        for k in range(n):
            for h in range(2):
                piece = hop.at[(t + k) % n, :, pl.ds(h * width, width)]

                @pl.when(2 * ((t + k) % n) + h == me)
                def _():
                    pltpu.make_async_copy(piece, grad_rows(me), grad_send.at[k, h]).wait()

    bo_line = Line(t, n, lambda src, s: bo_all.at[src, s], bo_send, bo_recv, drains)
    g_line = Line(t, n, lambda src, s: gall.at[s, :, pl.ds(pl.multiple_of(src * share, share), share)], g_send, g_recv, drains)
    quarter = width // 2

    def bi_view(h, e):
        return bi_all.at[e // 2, pl.ds(pl.multiple_of((e % 2) * width + h * quarter, quarter), quarter)]

    bi_gather = Gather(me, bits, bi_view, lambda h: bi_view(h, me), bi_send, bi_recv, drains)

    def a_view(h, e):
        return aall.at[e, pl.ds(h * (wide // 2), wide // 2)]

    a_gather = Gather(me, bits, a_view, lambda h: a_view(h, me), a_send, a_recv, drains)

    def core_copy(s, cm):
        return remote(prod.at[s, cm, 1 - core], core_in.at[s, cm], core_send.at[s, cm], core_recv.at[s, cm],
                      example=flip(me, 0))

    def rotate(s, cm):
        owner = flip_mask(pair, cm, chip_bits)

        def step(rows):
            res = jnp.dot(left[rows, :], bo_all[owner, s], preferred_element_type=F32).astype(BF)
            prod[s, cm, 0, rows, :] = res[:, :LANES]
            prod[s, cm, 1, rows, :] = res[:, LANES:]

        tile_loop(total_rows, total_rows, step)
        copy = core_copy(s, cm)
        copy.start()
        drains.append(copy.wait_send)

    def xy_copy(s, h, mask, place):
        bit = orders[h][place]
        slot = tables[h][(place, mask & ~(1 << bit))]
        rows = pl.ds(h * half, half)
        return remote(prod.at[s, mask, core, rows], xy_in.at[s, slot, rows], xy_send.at[s, h, mask],
                      xy_recv.at[s, h, slot], example=flip(me, bit + 1))

    def add_up(s, h, mask):
        level = level_of(mask, orders[h])
        for place in range(level):
            xy_copy(s, h, mask | (1 << orders[h][place]), place).wait_recv()
        inboxes = [tables[h][(place, mask)] for place in range(level)]

        def step(rows):
            rows = pl.ds(pl.multiple_of(rows.start + h * half, rows.size), rows.size)
            total = prod[s, mask, core, rows, :].astype(F32) + core_in[s, mask, rows, :].astype(F32)
            for slot in inboxes:
                total += xy_in[s, slot, rows, :].astype(F32)
            if mask:
                prod[s, mask, core, rows, :] = total.astype(BF)
            else:
                fin[s, rows, :] = total.astype(BF)

        tile_loop(half, 128, step)
        if mask:
            copy = xy_copy(s, h, mask, level)
            copy.start()
            drains.append(copy.wait_send)

    def keep_grads(s):
        rows = pl.ds(pl.multiple_of(t * share, share), share)
        for e in range(count):
            gall[s, e, rows, :] = fin[s, wide + e * share : wide + (e + 1) * share, :]

    def z_product(a, block, rows):
        right = acts_t[...] if a == 0 else fin[a - 1, :wide, :]
        return jnp.dot(bi_all[block, rows, :], right, preferred_element_type=F32)

    def z_unit(a, q, block_up, block_down):
        up = (t == q) & (block_up > q)
        down = (t == n - 1 - q) & (block_down < n - 1 - q)
        block = jnp.where(up, block_up, block_down)
        toward = jnp.where(up, 1, -1)
        slot = block + jnp.where(up, 1, 0)
        copy = remote(zheld.at[a, block], zin.at[a, slot], z_send.at[a, block], z_recv.at[a, slot], tensor=t + toward)

        @pl.when(up | down)
        def _():
            def first(rows):
                zheld[a, block, rows, :] = z_product(a, block, rows).astype(BF)

            tile_loop(wide, 512, first)
            if q:
                remote(zin.at[a, slot], zin.at[a, slot], z_send.at[a, block], z_recv.at[a, slot],
                       tensor=t - toward).wait_recv()

                def second(rows):
                    total = zheld[a, block, rows, :].astype(F32) + zin[a, slot, rows, :].astype(F32)
                    zheld[a, block, rows, :] = total.astype(BF)

                tile_loop(wide, 256, second)
            copy.start()

        def drain():
            @pl.when(up | down)
            def _():
                copy.wait_send()

        drains.append(drain)

    def z_own_product(a):
        def first(rows):
            cacc[rows, :] = z_product(a, t, rows)

        tile_loop(wide, 512, first)

    def z_own_sum(a):
        for way in range(2):
            slot = t + 1 - way

            @pl.when(t > 0 if way == 0 else t < n - 1)
            def _():
                remote(zin.at[a, slot], zin.at[a, slot], z_send.at[a, t], z_recv.at[a, slot],
                       tensor=t - 1 + 2 * way).wait_recv()

                def second(rows):
                    cacc[rows, :] += zin[a, slot, rows, :].astype(F32)

                tile_loop(wide, 256, second)

    def keep_acts():
        def step(rows):
            aall[me, rows, :] = cacc[rows, :].astype(BF)

        tile_loop(wide, 256, step)

    def score(s):
        def step(rows):
            scaled = (cacc[rows, :] / eig_ref[rows, s * LANES : (s + 1) * LANES]).astype(BF)
            for group in range(n):
                tokens = gall[s, 2 * group : 2 * group + 2].reshape(2 * tk, LANES)
                weighted = lax.dot_general(
                    scaled, tokens, (((1,), (1,)), ((), ())), preferred_element_type=F32
                )
                for c in range(2):
                    e = 2 * group + c
                    part = weighted[:, c * tk : (c + 1) * tk] * aall[e, rows, :].astype(F32)
                    acc[e] += jnp.sum(part.reshape(-1, 8, tk), axis=0)

        tile_loop(wide, 1024, step)

    def set_aside(s):
        early.extend(drains)
        drains.clear()
        score(s)

    def last_product(a):
        for drain in early:
            drain()
        z_own_product(a)

    def begin():
        bi_gather.start()
        for copy in bo_copies:
            copy.wait()

    def own_in():
        acc[...] = jnp.zeros_like(acc)
        acts_copy.wait()
        acts_t[...] = acts_ref[...].T
        eig_copy.wait()
        for copy in table_copies:
            copy.wait()
        choose(slot_ref, list_ref, count_ref, found, alive, fold, me)

    def q_in():
        q_copy.wait()
        for i in range(wide // LANES):
            left[i * LANES : (i + 1) * LANES, :] = q_ref[:, i * LANES : (i + 1) * LANES].T

    part = functools.partial
    times = plan_times(n, slices, chip_bits)
    plan.at(times["begin"], "begin", begin)
    plan.at(times["own_in"], "own_in", own_in, "begin")
    plan.at(times["grads_out"], "grads_out", grads_out, "begin")
    plan.at(times["q_in"], "q_in", q_in, "begin")
    for k in range(n):
        plan.at(times["grads", k], ("grads", k), part(grads_on, k), "grads_out")
    plan.at(times["grads_in"], "grads_in", grads_in, *[("grads", k) for k in range(n)])

    def plan_line(label, line, s, *needs):
        plan.at(times[label, s, 0], (label, s, 0), part(line.own, s), *needs)
        for d in range(1, n):
            plan.at(times[label, s, d], (label, s, d), part(line.receive, s, d), (label, s, d - 1))

    def plan_gather(label, gather, start):
        for h, mask in gather.masks():
            before = gather.before(h, mask)
            plan.at(times[label, h, mask], (label, h, mask), part(gather.receive, h, mask),
                    (label, h, before) if before else start)

    for s in range(slices):
        plan_line("bo", bo_line, s, "begin")
    plan_gather("bi", bi_gather, "begin")

    def bi_of(cm):
        return [("bi", h, 2 * cm + c) for h in range(2) for c in range(2) if cm or c]

    def plan_z(a, q, k, block_up, block_down, *needs):
        name = ("z", a, q, k)
        plan.at(times[name], name, part(z_unit, a, q, block_up, block_down), *needs)

    for cm in range(n):
        block = flip_mask(pair, cm, chip_bits)
        for q in range(n - 1):
            plan_z(0, q, cm, block, block, *(bi_of(cm) + ["own_in"] if q == 0 else [("z", 0, q - 1, cm)]))
    all_bi = [name for cm in range(n) for name in bi_of(cm)]

    def acts_in():
        z_own_product(0)
        z_own_sum(0)
        keep_acts()
        a_gather.start()

    plan.at(times["acts"], "acts", acts_in, *[("z", 0, n - 2, cm) for cm in range(n)])
    plan_gather("a", a_gather, "acts")
    all_acts = [("a", h, mask) for h, mask in a_gather.masks()]

    for s in range(slices):
        for cm in range(n):
            name = ("rot", s, cm)
            plan.at(times[name], name, part(rotate, s, cm), "q_in", "grads_in", *[("bo", s, d) for d in range(n)])
            plan.at(times["core", s, cm], ("core", s, cm), lambda s=s, cm=cm: core_copy(s, cm).wait_recv(), name)
            for h in range(2):
                level = level_of(cm, orders[h])
                sent = [("add", s, h, cm | (1 << orders[h][place])) for place in range(level)]
                plan.at(times["add", s, h, cm], ("add", s, h, cm), part(add_up, s, h, cm), ("core", s, cm), *sent)
        rotated = [("add", s, h, 0) for h in range(2)]
        plan_line("g", g_line, s, ("keep", s))
        plan.at(times["keep", s], ("keep", s), part(keep_grads, s), *rotated)
        a = s + 1
        for q in range(n - 1):
            for k in range(n - 1 - q):
                needs = rotated + all_bi if q == 0 else [("z", a, q - 1, k)]
                plan_z(a, q, k, n - 1 - k, k, *needs)
        free = ("score", s - 1) if s else "acts"
        plan.at(times["zown", a], ("zown", a), part(last_product if a == slices else z_own_product, a), free, *(rotated + all_bi))
        sums = [("z", a, q, n - 2 - q) for q in range(n - 1)]
        plan.at(times["zsum", a], ("zsum", a), part(z_own_sum, a), ("zown", a), *sums)
        plan.at(times["score", s], ("score", s), part(set_aside if s == max(slices - 3, 0) else score, s), ("zsum", a), *([("g", s, d) for d in range(n)] + all_acts))

    plan.run()

    red_t[t] = jnp.concatenate([jnp.sum(acc[e], axis=0, keepdims=True) for e in range(count)], axis=0)
    copies = []
    for k in range(1, n):
        copy = remote(red_t.at[t], red_t.at[t], rt_send.at[k - 1], rt_recv.at[t], tensor=(t + k) % n)
        copy.start()
        copies.append(copy)
    for drain in drains:
        drain()
    for k in range(1, n):
        src = (t + k) % n
        remote(red_t.at[src], red_t.at[src], rt_send.at[k - 1], rt_recv.at[src], tensor=src).wait_recv()
    total = red_t[0]
    for k in range(1, n):
        total += red_t[k]
    red_e[me] = total
    for k in range(1, count):
        copy = remote(red_e.at[me], red_e.at[me], re_send.at[k - 1], re_recv.at[me], example=(me + k) % count)
        copy.start()
        copies.append(copy)
    for k in range(1, count):
        src = (me + k) % count
        remote(red_e.at[src], red_e.at[src], re_send.at[k - 1], re_recv.at[src], example=src).wait_recv()
    total = red_e[0]
    for k in range(1, count):
        total += red_e[k]
    out_ref[...] = listed(total, found, alive, fold)
    for copy in copies:
        copy.wait_send()


def list_scores(q, bi, bo, grads, acts, eig, slot, lists, live, token_len, n, count):
    bits = count.bit_length() - 1
    width, wide = q.shape
    tk = grads.shape[0]
    slices = width // LANES
    rows = wide + 2 * tk
    chips = count // 2
    anywhere = pl.BlockSpec(memory_space=pl.ANY)
    vmem = pl.BlockSpec(memory_space=pltpu.VMEM)
    dma = pltpu.SemaphoreType.DMA
    return pl.pallas_call(
        functools.partial(whole_kernel, n, bits, tk),
        out_shape=jax.ShapeDtypeStruct((tk // token_len, token_len), F32),
        in_specs=[anywhere] * 9,
        out_specs=vmem,
        scratch_shapes=[
            pltpu.VMEM((1, slot.shape[0]), jnp.int32),
            pltpu.VMEM(lists.shape, jnp.int32),
            pltpu.VMEM((1, live.shape[0]), jnp.int32),
            pltpu.VMEM((count, tk // token_len, tk), F32),
            pltpu.VMEM((tk // token_len, token_len), F32),
            pltpu.VMEM((tk, token_len), F32),
            pltpu.VMEM((width, wide), BF),
            pltpu.VMEM((wide, width), BF),
            pltpu.VMEM((tk, wide), BF),
            pltpu.VMEM((wide, width), F32),
            pltpu.VMEM((rows, width), BF),
            pltpu.VMEM((n, tk // n, wide), BF),
            pltpu.VMEM((n, slices, width, 2 * LANES), BF),
            pltpu.VMEM((n, wide, wide), BF),
            pltpu.VMEM((slices, chips, 2, rows, LANES), BF),
            pltpu.VMEM((slices, chips, rows, LANES), BF),
            pltpu.VMEM((slices, chips - 1, rows, LANES), BF),
            pltpu.VMEM((slices, rows, LANES), BF),
            pltpu.VMEM((slices, count, tk, LANES), BF),
            pltpu.VMEM((slices + 1, n, wide, LANES), BF),
            pltpu.VMEM((slices + 1, n + 1, wide, LANES), BF),
            pltpu.VMEM((wide, LANES), F32),
            pltpu.VMEM((wide, tk), BF),
            pltpu.VMEM((count, wide, tk), BF),
            pltpu.VMEM((count, 8, tk), F32),
            pltpu.VMEM((n, count, tk), F32),
            pltpu.VMEM((count, count, tk), F32),
            dma((2 * slices + 7,)),
            dma((n,)),
            dma((n,)),
            dma((n, 2)),
            dma((count,)),
            dma((2, slices, n)),
            dma((slices, n)),
            dma((2, slices, n)),
            dma((slices, n)),
            dma((2, count)),
            dma((2, count)),
            dma((2, count)),
            dma((2, count)),
            dma((slices, chips)),
            dma((slices, chips)),
            dma((slices, 2, chips)),
            dma((slices, 2, chips)),
            dma((slices + 1, n)),
            dma((slices + 1, n + 1)),
            dma((n,)),
            dma((n,)),
            dma((count,)),
            dma((count,)),
        ],
        compiler_params=pltpu.CompilerParams(
            collective_id=0, has_side_effects=True, vmem_limit_bytes=VMEM_LIMIT
        ),
        name="list_scores",
    )(q, bi, bo, grads, acts, eig, slot.reshape(1, -1), lists, live.reshape(1, -1))


def body(
    queries, basis_out, basis_in, eigvals, input_fac, grad_fac, cand_slot, score_list, token_count
):
    count = lax.axis_size("example")
    n = lax.axis_size("tensor")
    token_len = input_fac.shape[1]
    wide = queries.shape[2]
    acts = input_fac.reshape(-1, wide)
    grads = grad_fac.reshape(-1, wide)
    scores = [
        list_scores(queries[q], basis_in, basis_out, grads, acts, eigvals, cand_slot, score_list, token_count,
                    token_len, n, count)
        for q in range(queries.shape[0])
    ]
    return jnp.stack(scores)


def solution(mesh):
    in_specs = (
        P(None, "example", "tensor"),
        P("example", "tensor"),
        P("tensor", "example"),
        P("tensor", "example"),
        P("example", None, "tensor"),
        P("example", None, "tensor"),
        P(),
        P(),
        P(),
    )
    out_specs = P(None, "example", None)
    return jax.shard_map(body, mesh=mesh, in_specs=in_specs, out_specs=out_specs, check_vma=False)
```

```python
import functools

import jax
import jax.numpy as jnp
from jax import lax
from jax.experimental import pallas as pl
from jax.experimental.pallas import tpu as pltpu
from jax.sharding import PartitionSpec as P

BF = jnp.bfloat16
F32 = jnp.float32
MESH = pl.DeviceIdType.MESH
VMEM_LIMIT = 60 * 1024 * 1024
LANES = 128


def flip(index, bit):
    size = 1 << bit
    return index + size * (1 - 2 * ((index // size) % 2))


def flip_mask(index, mask, bits):
    for bit in range(bits):
        if (mask >> bit) & 1:
            index = flip(index, bit)
    return index


def level_of(mask, order):
    for place, bit in enumerate(order):
        if (mask >> bit) & 1:
            return place
    return len(order)


def last_level(mask, order):
    return max(place for place, bit in enumerate(order) if (mask >> bit) & 1)


def remote(src, dst, send, recv, **where):
    return pltpu.make_async_remote_copy(
        src_ref=src, dst_ref=dst, send_sem=send, recv_sem=recv, device_id=where, device_id_type=MESH
    )


def tile_loop(size, tile, step):
    while size % tile:
        tile //= 2

    def run(i, carry):
        step(pl.ds(pl.multiple_of(i * tile, tile), tile))
        return carry

    lax.fori_loop(0, size // tile, run, 0)


TUNED_ORDER = (
    "begin", ("bo", 0, 0), "grads_out", "q_in", ("bo", 0, 1), ("grads", 1), ("bo", 1, 0), ("grads", 2),
    ("bo", 0, 2), ("grads", 3), ("bo", 2, 0), ("bi", 1, 1), ("grads", 0), ("bo", 1, 1), ("bi", 1, 4), ("bi", 0, 2),
    "own_in", ("bi", 0, 1), ("z", 0, 0, 0), ("bo", 3, 0), "grads_in", ("bo", 0, 3), ("rot", 0, 2), ("bi", 1, 2),
    ("rot", 0, 0), ("rot", 0, 1), ("bi", 0, 4), ("bi", 1, 3), ("bi", 1, 5), ("rot", 0, 3), ("bi", 0, 3),
    ("z", 0, 0, 1), ("core", 0, 3), ("add", 0, 1, 3), ("bi", 0, 5), ("z", 0, 0, 2), ("core", 0, 2),
    ("add", 0, 1, 2), ("z", 0, 1, 0), ("add", 0, 0, 3), ("bi", 1, 6), ("bo", 1, 2), ("core", 0, 1),
    ("add", 0, 0, 1), ("bo", 2, 1), ("bi", 0, 6), ("bi", 1, 7), ("z", 0, 1, 2), ("add", 0, 0, 2), ("add", 0, 1, 1),
    ("z", 0, 1, 1), ("bi", 0, 7), ("z", 0, 0, 3), ("core", 0, 0), ("add", 0, 0, 0), ("add", 0, 1, 0), ("keep", 0),
    ("g", 0, 0), ("z", 1, 0, 0), ("bo", 1, 3), ("rot", 1, 1), ("z", 1, 0, 2), ("rot", 1, 3), ("rot", 1, 2),
    ("core", 1, 3), ("add", 1, 0, 3), ("add", 1, 1, 3), ("bo", 2, 2), ("bo", 3, 1), ("core", 1, 2), ("core", 1, 1),
    ("add", 1, 0, 1), ("add", 1, 1, 2), ("z", 0, 1, 3), ("z", 1, 0, 1), ("z", 1, 1, 0), ("add", 1, 0, 2),
    ("add", 1, 1, 1), ("rot", 1, 0), ("core", 1, 0), ("bo", 2, 3), ("rot", 2, 2), ("rot", 2, 3), ("add", 1, 1, 0),
    ("add", 1, 0, 0), ("keep", 1), ("g", 1, 0), ("z", 2, 0, 0), ("g", 0, 1), ("z", 2, 0, 1), ("core", 2, 3),
    ("add", 2, 1, 3), ("add", 2, 0, 3), ("core", 2, 2), ("add", 2, 1, 2), ("z", 2, 0, 2), ("bo", 3, 2),
    ("rot", 2, 0), ("core", 2, 0), ("rot", 2, 1), ("z", 0, 2, 3), ("core", 2, 1), ("add", 2, 0, 1), ("bo", 3, 3),
    ("rot", 3, 2), ("z", 1, 1, 1), ("g", 1, 1), ("rot", 3, 1), ("add", 2, 0, 2), ("add", 2, 1, 1), ("z", 2, 1, 0),
    ("z", 0, 2, 2), ("core", 3, 2), ("add", 3, 1, 2), ("rot", 3, 3), ("core", 3, 1), ("add", 3, 0, 1),
    ("z", 0, 2, 0), ("z", 0, 2, 1), ("core", 3, 3), ("add", 2, 0, 0), ("add", 2, 1, 0), ("add", 3, 1, 3),
    ("keep", 2), ("g", 2, 0), ("z", 2, 1, 1), ("z", 1, 2, 0), ("add", 3, 0, 3), ("z", 3, 0, 0), ("rot", 3, 0),
    ("z", 2, 2, 0), ("g", 1, 2), ("add", 3, 1, 1), ("z", 3, 0, 1), ("g", 2, 1), ("add", 3, 0, 2), "acts",
    ("core", 3, 0), ("add", 3, 0, 0), ("add", 3, 1, 0), ("keep", 3), ("g", 3, 0), ("z", 3, 1, 0), ("a", 1, 1),
    ("z", 4, 0, 0), ("zown", 1), ("z", 4, 0, 1), ("z", 3, 1, 1), ("a", 1, 4), ("g", 2, 2), ("g", 0, 2), ("a", 0, 2),
    ("a", 1, 2), ("g", 3, 1), ("g", 1, 3), ("z", 3, 2, 0), ("z", 3, 0, 2), ("a", 1, 3), ("a", 0, 6), ("z", 4, 1, 0),
    ("g", 0, 3), ("a", 0, 4), ("a", 1, 6), ("a", 0, 5), ("a", 1, 7), ("g", 3, 2), ("a", 0, 7), ("g", 3, 3),
    ("z", 4, 0, 2), ("a", 0, 1), ("zsum", 1), ("a", 0, 3), ("a", 1, 5), ("score", 0), ("zown", 2), ("z", 4, 1, 1),
    ("z", 4, 2, 0), ("zsum", 2), ("g", 2, 3), ("score", 1), ("zown", 3), ("zsum", 3), ("score", 2), ("zown", 4),
    ("zsum", 4), ("score", 3),
)


class Schedule:
    def __init__(self):
        self.actions = {}
        self.done = set()

    def at(self, when, name, action, *needs):
        self.actions[name] = (when, len(self.actions), action, needs)

    def do(self, name):
        if name in self.done:
            return
        self.done.add(name)
        for need in self.actions[name][3]:
            self.do(need)
        self.actions[name][2]()

    def run(self):
        for name in sorted(self.actions, key=lambda name: self.actions[name][:2]):
            self.do(name)


class Gather:
    def __init__(self, me, bits, view, own, send_sem, recv_sem, drains):
        self.me, self.bits, self.view, self.own = me, bits, view, own
        self.send_sem, self.recv_sem, self.drains = send_sem, recv_sem, drains
        upper = list(range(1, bits))
        self.orders = [upper + [0], upper[::-1] + [0]]

    def send(self, h, mask, bit):
        there = self.view(h, flip_mask(self.me, mask, self.bits))
        src = self.own(h) if mask == 0 else there
        slot = mask | (1 << bit)
        copy = remote(src, there, self.send_sem.at[h, slot], self.recv_sem.at[h, slot], example=flip(self.me, bit))
        copy.start()
        self.drains.append(copy.wait_send)

    def start(self):
        for place in range(self.bits - 1):
            for h in range(2):
                self.send(h, 0, self.orders[h][place])
            if place == 0:
                for h in range(2):
                    self.send(h, 0, 0)

    def before(self, h, mask):
        return mask & ~(1 << self.orders[h][last_level(mask, self.orders[h])])

    def receive(self, h, mask):
        here = self.view(h, flip_mask(self.me, mask, self.bits))
        remote(here, here, self.send_sem.at[h, mask], self.recv_sem.at[h, mask], example=flip(self.me, 0)).wait_recv()
        for bit in self.orders[h][last_level(mask, self.orders[h]) + 1 :]:
            self.send(h, mask, bit)

    def masks(self):
        pairs = [(h, mask) for mask in range(1, 1 << self.bits) for h in range(2)]
        return sorted(pairs, key=lambda p: (last_level(p[1], self.orders[p[0]]), bin(p[1]).count("1"), p[1], p[0]))


class Line:
    def __init__(self, t, n, piece, send_sem, recv_sem, drains):
        self.t, self.n, self.piece = t, n, piece
        self.send_sem, self.recv_sem, self.drains = send_sem, recv_sem, drains

    def send(self, cond, s, src, way):
        ref = self.piece(src, s)
        copy = remote(ref, ref, self.send_sem.at[way, s, src], self.recv_sem.at[s, src], tensor=self.t + 1 - 2 * way)

        @pl.when(cond)
        def _():
            copy.start()

        def drain():
            @pl.when(cond)
            def _():
                copy.wait_send()

        self.drains.append(drain)

    def own(self, s):
        self.send(self.t < self.n - 1, s, self.t, 0)
        self.send(self.t > 0, s, self.t, 1)

    def receive(self, s, d):
        for way in range(2):
            sign = 1 - 2 * way
            src = self.t - sign * d
            here = src >= 0 if way == 0 else src < self.n
            on = self.t < self.n - 1 if way == 0 else self.t > 0

            @pl.when(here)
            def _():
                ref = self.piece(src, s)
                remote(ref, ref, self.send_sem.at[way, s, src], self.recv_sem.at[s, src],
                       tensor=self.t - sign).wait_recv()

            if d < self.n - 1:
                self.send(here & on, s, src, way)


def plan_times(n, slices, chip_bits):
    hop, period, lag, step, rise = 5.5, 16.5, 21.0, 6.0, 6.0
    times = {"begin": -9.0, "own_in": 0.5, "grads_out": 0.1, "q_in": 1.5, "grads_in": 20.0}
    for k in range(n):
        times["grads", k] = 8.0 + k
    orders = [list(range(chip_bits)), list(range(chip_bits))[::-1]]
    full = [[bit + 1 for bit in order] + [0] for order in orders]
    count = 2 << chip_bits

    def gather(label, base, gap):
        for h in range(2):
            for mask in range(1, count):
                upper = last_level(mask & ~1, full[h]) + bin(mask >> 1).count("1") if mask & ~1 else 0
                times[label, h, mask] = base + gap * upper + (mask & 1)

    gather("bi", 3.0, 10.5)
    for cm in range(n):
        ready = 3.0 + 10.5 * (cm.bit_length() + (bin(cm).count("1") > 1)) + 2 if cm else 4.5
        for q in range(n - 1):
            times["z", 0, q, cm] = ready + step * q
    acts = 3.0 + 10.5 * (chip_bits + 1) + step * n
    times["acts"] = acts
    gather("a", acts + 3, 3.0)
    for s in range(slices):
        base = 4 + s * period
        times["bo", s, 0] = base - period - hop if s else 0.0
        for d in range(1, n):
            times["bo", s, d] = base + d * hop
        rot = base + lag
        for i, cm in enumerate(sorted(range(n), key=lambda m: -bin(m).count("1"))):
            times["rot", s, cm] = rot + 0.8 * i
            times["core", s, cm] = rot + 1.6 + 0.8 * i
            for h in range(2):
                times["add", s, h, cm] = rot + 1.7 + rise * level_of(cm, orders[h]) + 0.1 * i
        done = rot + 2.5 + rise * chip_bits
        times["keep", s] = done
        for d in range(n):
            times["g", s, d] = done + 4.0 * d
        a = s + 1
        for q in range(n - 1):
            for k in range(n - 1 - q):
                times["z", a, q, k] = done + 0.1 + step * (q + (k if q else 0)) + 0.5 * k
        own = done + step * n
        times["zown", a] = own - 1
        times["zsum", a] = own
        times["score", s] = own + 0.1
    if set(TUNED_ORDER) == set(times):
        times = {name: float(place) for place, name in enumerate(TUNED_ORDER)}
    return times


def choose(slot_ref, list_ref, count_ref, found, alive, fold, me):
    count, length, tk = found.shape
    token_len = fold.shape[1]
    mine = jnp.broadcast_to(list_ref[pl.ds(me, 1), :], (length, length))
    diagonal = lax.broadcasted_iota(jnp.int32, (length, length), 0) == lax.broadcasted_iota(
        jnp.int32, (length, length), 1
    )
    mine = jnp.sum(jnp.where(diagonal, mine, 0), axis=1, keepdims=True)
    total = slot_ref.shape[1]
    matches = mine == lax.broadcasted_iota(jnp.int32, (length, total), 1)
    slots = jnp.sum(jnp.where(matches, slot_ref[...], 0), axis=1, keepdims=True)
    live = jnp.sum(jnp.where(matches, count_ref[...], 0), axis=1, keepdims=True)
    place = lax.broadcasted_iota(jnp.int32, (length, tk), 1) // token_len
    for e in range(count):
        found[e] = (slots == place + e * length).astype(F32)
    alive[...] = (lax.broadcasted_iota(jnp.int32, (length, token_len), 1) < live).astype(F32)
    same = lax.broadcasted_iota(jnp.int32, (tk, token_len), 0) % token_len == lax.broadcasted_iota(
        jnp.int32, (tk, token_len), 1
    )
    fold[...] = same.astype(F32)


def listed(total, found, alive, fold):
    spread = jnp.zeros(found.shape[1:], F32)
    for e in range(found.shape[0]):
        spread += jnp.where(found[e] > 0.5, total[e : e + 1, :], F32(0.0))
    scores = jnp.dot(spread, fold[...], precision=lax.Precision.HIGHEST, preferred_element_type=F32)
    return jnp.where(alive[...] > 0.5, scores, F32(0.0))


def whole_kernel(
    n, bits, tk,
    q_hbm, bi_hbm, bo_ref, grads_ref, acts_hbm, eig_hbm,
    slot_hbm, list_hbm, count_hbm, out_ref,
    slot_ref, list_ref, count_ref, found, alive, fold, q_ref, bi_ref, acts_ref, eig_ref,
    left, hop, bo_all, bi_all, prod, core_in, xy_in, fin, gall, zheld, zin, cacc, acts_t, aall, acc, red_t, red_e,
    own_sem, hop_send, hop_recv, grad_send, grad_recv, bo_send, bo_recv, g_send, g_recv, bi_send, bi_recv, a_send, a_recv,
    core_send, core_recv, xy_send, xy_recv, z_send, z_recv, rt_send, rt_recv, re_send, re_recv,
):
    me = lax.axis_index("example")
    t = lax.axis_index("tensor")
    count = 1 << bits
    pair = me // 2
    core = me % 2
    chip_bits = bits - 1
    width, wide = q_hbm.shape
    tk = grads_ref.shape[0]
    share = tk // n
    slices = width // LANES
    total_rows = left.shape[0]
    half = total_rows // 2
    orders = [list(range(chip_bits)), list(range(chip_bits))[::-1]]
    drains, early = [], []
    plan = Schedule()

    tables = []
    for h in range(2):
        table = {}
        for place in range(chip_bits):
            for mask in range(1 << chip_bits):
                if level_of(mask, orders[h]) > place:
                    table[(place, mask)] = len(table)
        tables.append(table)

    bi_copy = pltpu.make_async_copy(bi_hbm, bi_ref, own_sem.at[2 * slices])
    bi_copy.start()
    acts_copy = pltpu.make_async_copy(acts_hbm, acts_ref, own_sem.at[2 * slices + 1])
    q_copy = pltpu.make_async_copy(q_hbm, q_ref, own_sem.at[2 * slices + 2])
    eig_copy = pltpu.make_async_copy(eig_hbm, eig_ref, own_sem.at[2 * slices + 3])
    bo_copies = []
    for s in range(slices):
        for h in range(2):
            copy = pltpu.make_async_copy(
                bo_ref.at[:, pl.ds(h * width + s * LANES, LANES)],
                bo_all.at[t, s, :, pl.ds(h * LANES, LANES)],
                own_sem.at[2 * s + h],
            )
            copy.start()
            bo_copies.append(copy)
    table_copies = [
        pltpu.make_async_copy(src, dst, own_sem.at[2 * slices + 4 + i])
        for i, (src, dst) in enumerate(((slot_hbm, slot_ref), (list_hbm, list_ref), (count_hbm, count_ref)))
    ]
    for copy in (acts_copy, q_copy, eig_copy, *table_copies):
        copy.start()

    barrier = pltpu.get_barrier_semaphore()
    for k in range(1, n):
        pl.semaphore_signal(barrier, inc=1, device_id={"tensor": (t + k) % n}, device_id_type=MESH)
    for k in range(1, count):
        pl.semaphore_signal(barrier, inc=1, device_id={"example": (me + k) % count}, device_id_type=MESH)
    bi_copy.wait()
    for i in range(width // LANES):
        rows = pl.ds(pl.multiple_of(core * width + i * LANES, LANES), LANES)
        bi_all[pair, rows, :] = bi_ref[:, i * LANES : (i + 1) * LANES].T
    pl.semaphore_wait(barrier, n + count - 2)

    def hop_copy(k):
        there = (t + k) % n
        rows = pl.ds(pl.multiple_of(there * share, share), share)
        return remote(grads_ref.at[rows], hop.at[t], hop_send.at[k], hop_recv.at[t], tensor=there)

    def grads_out():
        for k in range(1, n):
            copy = hop_copy(k)
            copy.start()
            drains.append(copy.wait_send)
        local = pltpu.make_async_copy(
            grads_ref.at[pl.ds(pl.multiple_of(t * share, share), share)], hop.at[t], hop_send.at[0]
        )
        local.start()
        local.wait()

    def grad_rows(e):
        return left.at[pl.ds(pl.multiple_of(wide + e * share, share), share)]

    def grads_on(k):
        src = (t + k) % n
        if k:
            remote(hop.at[src], hop.at[src], hop_send.at[k], hop_recv.at[src], tensor=src).wait_recv()
        for h in range(2):
            goal = 2 * src + h
            piece = hop.at[src, :, pl.ds(h * width, width)]
            copy = remote(piece, grad_rows(me), grad_send.at[k, h], grad_recv.at[me], example=goal)
            local = pltpu.make_async_copy(piece, grad_rows(me), grad_send.at[k, h])

            @pl.when(goal != me)
            def _():
                copy.start()

            @pl.when(goal == me)
            def _():
                local.start()

            def drain(copy=copy, goal=goal):
                @pl.when(goal != me)
                def _():
                    copy.wait_send()

            drains.append(drain)

    def grads_in():
        for k in range(1, count):
            src = (me + k) % count
            remote(grad_rows(src), grad_rows(src), grad_send.at[0, 0], grad_recv.at[src], example=src).wait_recv()
        for k in range(n):
            for h in range(2):
                piece = hop.at[(t + k) % n, :, pl.ds(h * width, width)]

                @pl.when(2 * ((t + k) % n) + h == me)
                def _():
                    pltpu.make_async_copy(piece, grad_rows(me), grad_send.at[k, h]).wait()

    bo_line = Line(t, n, lambda src, s: bo_all.at[src, s], bo_send, bo_recv, drains)
    g_line = Line(t, n, lambda src, s: gall.at[s, :, pl.ds(pl.multiple_of(src * share, share), share)], g_send, g_recv, drains)
    quarter = width // 2

    def bi_view(h, e):
        return bi_all.at[e // 2, pl.ds(pl.multiple_of((e % 2) * width + h * quarter, quarter), quarter)]

    bi_gather = Gather(me, bits, bi_view, lambda h: bi_view(h, me), bi_send, bi_recv, drains)

    def a_view(h, e):
        return aall.at[e, pl.ds(h * (wide // 2), wide // 2)]

    a_gather = Gather(me, bits, a_view, lambda h: a_view(h, me), a_send, a_recv, drains)

    def core_copy(s, cm):
        return remote(prod.at[s, cm, 1 - core], core_in.at[s, cm], core_send.at[s, cm], core_recv.at[s, cm],
                      example=flip(me, 0))

    def rotate(s, cm):
        owner = flip_mask(pair, cm, chip_bits)

        def step(rows):
            res = jnp.dot(left[rows, :], bo_all[owner, s], preferred_element_type=F32).astype(BF)
            prod[s, cm, 0, rows, :] = res[:, :LANES]
            prod[s, cm, 1, rows, :] = res[:, LANES:]

        tile_loop(total_rows, total_rows, step)
        copy = core_copy(s, cm)
        copy.start()
        drains.append(copy.wait_send)

    def xy_copy(s, h, mask, place):
        bit = orders[h][place]
        slot = tables[h][(place, mask & ~(1 << bit))]
        rows = pl.ds(h * half, half)
        return remote(prod.at[s, mask, core, rows], xy_in.at[s, slot, rows], xy_send.at[s, h, mask],
                      xy_recv.at[s, h, slot], example=flip(me, bit + 1))

    def add_up(s, h, mask):
        level = level_of(mask, orders[h])
        for place in range(level):
            xy_copy(s, h, mask | (1 << orders[h][place]), place).wait_recv()
        inboxes = [tables[h][(place, mask)] for place in range(level)]

        def step(rows):
            rows = pl.ds(pl.multiple_of(rows.start + h * half, rows.size), rows.size)
            total = prod[s, mask, core, rows, :].astype(F32) + core_in[s, mask, rows, :].astype(F32)
            for slot in inboxes:
                total += xy_in[s, slot, rows, :].astype(F32)
            if mask:
                prod[s, mask, core, rows, :] = total.astype(BF)
            else:
                fin[s, rows, :] = total.astype(BF)

        tile_loop(half, half, step)
        if mask:
            copy = xy_copy(s, h, mask, level)
            copy.start()
            drains.append(copy.wait_send)

    def keep_grads(s):
        rows = pl.ds(pl.multiple_of(t * share, share), share)
        for e in range(count):
            gall[s, e, rows, :] = fin[s, wide + e * share : wide + (e + 1) * share, :]

    def z_product(a, block, rows):
        right = acts_t[...] if a == 0 else fin[a - 1, :wide, :]
        return jnp.dot(bi_all[block, rows, :], right, preferred_element_type=F32)

    def z_unit(a, q, block_up, block_down):
        up = (t == q) & (block_up > q)
        down = (t == n - 1 - q) & (block_down < n - 1 - q)
        block = jnp.where(up, block_up, block_down)
        toward = jnp.where(up, 1, -1)
        slot = block + jnp.where(up, 1, 0)
        copy = remote(zheld.at[a, block], zin.at[a, slot], z_send.at[a, block], z_recv.at[a, slot], tensor=t + toward)

        @pl.when(up | down)
        def _():
            def first(rows):
                zheld[a, block, rows, :] = z_product(a, block, rows).astype(BF)

            tile_loop(wide, 512, first)
            if q:
                remote(zin.at[a, slot], zin.at[a, slot], z_send.at[a, block], z_recv.at[a, slot],
                       tensor=t - toward).wait_recv()

                def second(rows):
                    total = zheld[a, block, rows, :].astype(F32) + zin[a, slot, rows, :].astype(F32)
                    zheld[a, block, rows, :] = total.astype(BF)

                tile_loop(wide, 512, second)
            copy.start()

        def drain():
            @pl.when(up | down)
            def _():
                copy.wait_send()

        drains.append(drain)

    def z_own_product(a):
        def first(rows):
            cacc[rows, :] = z_product(a, t, rows)

        tile_loop(wide, 512, first)

    def z_own_sum(a):
        for way in range(2):
            slot = t + 1 - way

            @pl.when(t > 0 if way == 0 else t < n - 1)
            def _():
                remote(zin.at[a, slot], zin.at[a, slot], z_send.at[a, t], z_recv.at[a, slot],
                       tensor=t - 1 + 2 * way).wait_recv()

                def second(rows):
                    cacc[rows, :] += zin[a, slot, rows, :].astype(F32)

                tile_loop(wide, 512, second)

    def keep_acts():
        def step(rows):
            aall[me, rows, :] = cacc[rows, :].astype(BF)

        tile_loop(wide, 256, step)

    def score(s):
        def step(rows):
            scaled = (cacc[rows, :] / eig_ref[rows, s * LANES : (s + 1) * LANES]).astype(BF)
            for group in range(n):
                tokens = gall[s, 2 * group : 2 * group + 2].reshape(2 * tk, LANES)
                weighted = lax.dot_general(
                    scaled, tokens, (((1,), (1,)), ((), ())), preferred_element_type=F32
                )
                for c in range(2):
                    e = 2 * group + c
                    part = weighted[:, c * tk : (c + 1) * tk] * aall[e, rows, :].astype(F32)
                    acc[e] += jnp.sum(part.reshape(-1, 8, tk), axis=0)

        tile_loop(wide, 1024, step)

    def set_aside(s):
        early.extend(drains)
        drains.clear()
        score(s)

    def last_product(a):
        for drain in early:
            drain()
        z_own_product(a)

    def begin():
        bi_gather.start()
        for copy in bo_copies:
            copy.wait()

    def own_in():
        acc[...] = jnp.zeros_like(acc)
        acts_copy.wait()
        acts_t[...] = acts_ref[...].T
        eig_copy.wait()
        for copy in table_copies:
            copy.wait()
        choose(slot_ref, list_ref, count_ref, found, alive, fold, me)

    def q_in():
        q_copy.wait()
        for i in range(wide // LANES):
            left[i * LANES : (i + 1) * LANES, :] = q_ref[:, i * LANES : (i + 1) * LANES].T

    part = functools.partial
    times = plan_times(n, slices, chip_bits)
    plan.at(times["begin"], "begin", begin)
    plan.at(times["own_in"], "own_in", own_in, "begin")
    plan.at(times["grads_out"], "grads_out", grads_out, "begin")
    plan.at(times["q_in"], "q_in", q_in, "begin")
    for k in range(n):
        plan.at(times["grads", k], ("grads", k), part(grads_on, k), "grads_out")
    plan.at(times["grads_in"], "grads_in", grads_in, *[("grads", k) for k in range(n)])

    def plan_line(label, line, s, *needs):
        plan.at(times[label, s, 0], (label, s, 0), part(line.own, s), *needs)
        for d in range(1, n):
            plan.at(times[label, s, d], (label, s, d), part(line.receive, s, d), (label, s, d - 1))

    def plan_gather(label, gather, start):
        for h, mask in gather.masks():
            before = gather.before(h, mask)
            plan.at(times[label, h, mask], (label, h, mask), part(gather.receive, h, mask),
                    (label, h, before) if before else start)

    for s in range(slices):
        plan_line("bo", bo_line, s, "begin")
    plan_gather("bi", bi_gather, "begin")

    def bi_of(cm):
        return [("bi", h, 2 * cm + c) for h in range(2) for c in range(2) if cm or c]

    def plan_z(a, q, k, block_up, block_down, *needs):
        name = ("z", a, q, k)
        plan.at(times[name], name, part(z_unit, a, q, block_up, block_down), *needs)

    for cm in range(n):
        block = flip_mask(pair, cm, chip_bits)
        for q in range(n - 1):
            plan_z(0, q, cm, block, block, *(bi_of(cm) + ["own_in"] if q == 0 else [("z", 0, q - 1, cm)]))
    all_bi = [name for cm in range(n) for name in bi_of(cm)]

    def acts_in():
        z_own_product(0)
        z_own_sum(0)
        keep_acts()
        a_gather.start()

    plan.at(times["acts"], "acts", acts_in, *[("z", 0, n - 2, cm) for cm in range(n)])
    plan_gather("a", a_gather, "acts")
    all_acts = [("a", h, mask) for h, mask in a_gather.masks()]

    for s in range(slices):
        for cm in range(n):
            name = ("rot", s, cm)
            plan.at(times[name], name, part(rotate, s, cm), "q_in", "grads_in", *[("bo", s, d) for d in range(n)])
            plan.at(times["core", s, cm], ("core", s, cm), lambda s=s, cm=cm: core_copy(s, cm).wait_recv(), name)
            for h in range(2):
                level = level_of(cm, orders[h])
                sent = [("add", s, h, cm | (1 << orders[h][place])) for place in range(level)]
                plan.at(times["add", s, h, cm], ("add", s, h, cm), part(add_up, s, h, cm), ("core", s, cm), *sent)
        rotated = [("add", s, h, 0) for h in range(2)]
        plan_line("g", g_line, s, ("keep", s))
        plan.at(times["keep", s], ("keep", s), part(keep_grads, s), *rotated)
        a = s + 1
        for q in range(n - 1):
            for k in range(n - 1 - q):
                needs = rotated + all_bi if q == 0 else [("z", a, q - 1, k)]
                plan_z(a, q, k, n - 1 - k, k, *needs)
        free = ("score", s - 1) if s else "acts"
        plan.at(times["zown", a], ("zown", a), part(last_product if a == slices else z_own_product, a), free, *(rotated + all_bi))
        sums = [("z", a, q, n - 2 - q) for q in range(n - 1)]
        plan.at(times["zsum", a], ("zsum", a), part(z_own_sum, a), ("zown", a), *sums)
        plan.at(times["score", s], ("score", s), part(set_aside if s == max(slices - 3, 0) else score, s), ("zsum", a), *([("g", s, d) for d in range(n)] + all_acts))

    plan.run()

    red_t[t] = jnp.concatenate([jnp.sum(acc[e], axis=0, keepdims=True) for e in range(count)], axis=0)
    copies = []
    for k in range(1, n):
        copy = remote(red_t.at[t], red_t.at[t], rt_send.at[k - 1], rt_recv.at[t], tensor=(t + k) % n)
        copy.start()
        copies.append(copy)
    for drain in drains:
        drain()
    for k in range(1, n):
        src = (t + k) % n
        remote(red_t.at[src], red_t.at[src], rt_send.at[k - 1], rt_recv.at[src], tensor=src).wait_recv()
    total = red_t[0]
    for k in range(1, n):
        total += red_t[k]
    red_e[me] = total
    for k in range(1, count):
        copy = remote(red_e.at[me], red_e.at[me], re_send.at[k - 1], re_recv.at[me], example=(me + k) % count)
        copy.start()
        copies.append(copy)
    for k in range(1, count):
        src = (me + k) % count
        remote(red_e.at[src], red_e.at[src], re_send.at[k - 1], re_recv.at[src], example=src).wait_recv()
    total = red_e[0]
    for k in range(1, count):
        total += red_e[k]
    out_ref[...] = listed(total, found, alive, fold)
    for copy in copies:
        copy.wait_send()


def list_scores(q, bi, bo, grads, acts, eig, slot, lists, live, token_len, n, count):
    bits = count.bit_length() - 1
    width, wide = q.shape
    tk = grads.shape[0]
    slices = width // LANES
    rows = wide + 2 * tk
    chips = count // 2
    anywhere = pl.BlockSpec(memory_space=pl.ANY)
    vmem = pl.BlockSpec(memory_space=pltpu.VMEM)
    dma = pltpu.SemaphoreType.DMA
    return pl.pallas_call(
        functools.partial(whole_kernel, n, bits, tk),
        out_shape=jax.ShapeDtypeStruct((tk // token_len, token_len), F32),
        in_specs=[anywhere] * 9,
        out_specs=vmem,
        scratch_shapes=[
            pltpu.VMEM((1, slot.shape[0]), jnp.int32),
            pltpu.VMEM(lists.shape, jnp.int32),
            pltpu.VMEM((1, live.shape[0]), jnp.int32),
            pltpu.VMEM((count, tk // token_len, tk), F32),
            pltpu.VMEM((tk // token_len, token_len), F32),
            pltpu.VMEM((tk, token_len), F32),
            pltpu.VMEM((width, wide), BF),
            pltpu.VMEM((wide, width), BF),
            pltpu.VMEM((tk, wide), BF),
            pltpu.VMEM((wide, width), F32),
            pltpu.VMEM((rows, width), BF),
            pltpu.VMEM((n, tk // n, wide), BF),
            pltpu.VMEM((n, slices, width, 2 * LANES), BF),
            pltpu.VMEM((n, wide, wide), BF),
            pltpu.VMEM((slices, chips, 2, rows, LANES), BF),
            pltpu.VMEM((slices, chips, rows, LANES), BF),
            pltpu.VMEM((slices, chips - 1, rows, LANES), BF),
            pltpu.VMEM((slices, rows, LANES), BF),
            pltpu.VMEM((slices, count, tk, LANES), BF),
            pltpu.VMEM((slices + 1, n, wide, LANES), BF),
            pltpu.VMEM((slices + 1, n + 1, wide, LANES), BF),
            pltpu.VMEM((wide, LANES), F32),
            pltpu.VMEM((wide, tk), BF),
            pltpu.VMEM((count, wide, tk), BF),
            pltpu.VMEM((count, 8, tk), F32),
            pltpu.VMEM((n, count, tk), F32),
            pltpu.VMEM((count, count, tk), F32),
            dma((2 * slices + 7,)),
            dma((n,)),
            dma((n,)),
            dma((n, 2)),
            dma((count,)),
            dma((2, slices, n)),
            dma((slices, n)),
            dma((2, slices, n)),
            dma((slices, n)),
            dma((2, count)),
            dma((2, count)),
            dma((2, count)),
            dma((2, count)),
            dma((slices, chips)),
            dma((slices, chips)),
            dma((slices, 2, chips)),
            dma((slices, 2, chips)),
            dma((slices + 1, n)),
            dma((slices + 1, n + 1)),
            dma((n,)),
            dma((n,)),
            dma((count,)),
            dma((count,)),
        ],
        compiler_params=pltpu.CompilerParams(
            collective_id=0, has_side_effects=True, vmem_limit_bytes=VMEM_LIMIT
        ),
        name="list_scores",
    )(q, bi, bo, grads, acts, eig, slot.reshape(1, -1), lists, live.reshape(1, -1))


def body(
    queries, basis_out, basis_in, eigvals, input_fac, grad_fac, cand_slot, score_list, token_count
):
    count = lax.axis_size("example")
    n = lax.axis_size("tensor")
    token_len = input_fac.shape[1]
    wide = queries.shape[2]
    acts = input_fac.reshape(-1, wide)
    grads = grad_fac.reshape(-1, wide)
    scores = [
        list_scores(queries[q], basis_in, basis_out, grads, acts, eigvals, cand_slot, score_list, token_count,
                    token_len, n, count)
        for q in range(queries.shape[0])
    ]
    return jnp.stack(scores)


def solution(mesh):
    in_specs = (
        P(None, "example", "tensor"),
        P("example", "tensor"),
        P("tensor", "example"),
        P("tensor", "example"),
        P("example", None, "tensor"),
        P("example", None, "tensor"),
        P(),
        P(),
        P(),
    )
    out_specs = P(None, "example", None)
    return jax.shard_map(body, mesh=mesh, in_specs=in_specs, out_specs=out_specs, check_vma=False)
```

```python
import functools

import jax
import jax.numpy as jnp
from jax import lax
from jax.experimental import pallas as pl
from jax.experimental.pallas import tpu as pltpu
from jax.sharding import PartitionSpec as P

BF = jnp.bfloat16
F32 = jnp.float32
MESH = pl.DeviceIdType.MESH
VMEM_LIMIT = 60 * 1024 * 1024
LANES = 128


def flip(index, bit):
    size = 1 << bit
    return index + size * (1 - 2 * ((index // size) % 2))


def flip_mask(index, mask, bits):
    for bit in range(bits):
        if (mask >> bit) & 1:
            index = flip(index, bit)
    return index


def level_of(mask, order):
    for place, bit in enumerate(order):
        if (mask >> bit) & 1:
            return place
    return len(order)


def last_level(mask, order):
    return max(place for place, bit in enumerate(order) if (mask >> bit) & 1)


def remote(src, dst, send, recv, **where):
    return pltpu.make_async_remote_copy(
        src_ref=src, dst_ref=dst, send_sem=send, recv_sem=recv, device_id=where, device_id_type=MESH
    )


def tile_loop(size, tile, step):
    while size % tile:
        tile //= 2

    def run(i, carry):
        step(pl.ds(pl.multiple_of(i * tile, tile), tile))
        return carry

    lax.fori_loop(0, size // tile, run, 0)


TUNED_ORDER = (
    "begin", ("bo", 0, 0), "grads_out", "q_in", ("bo", 0, 1), ("grads", 1), ("bo", 1, 0), ("grads", 2),
    ("bo", 0, 2), ("grads", 3), ("bo", 2, 0), ("bi", 1, 1), ("grads", 0), ("bo", 1, 1), ("bi", 1, 4), ("bi", 0, 2),
    "own_in", ("bi", 0, 1), ("z", 0, 0, 0), ("bo", 3, 0), "grads_in", ("bo", 0, 3), ("rot", 0, 2), ("bi", 1, 2),
    ("rot", 0, 0), ("rot", 0, 1), ("bi", 0, 4), ("bi", 1, 3), ("bi", 1, 5), ("rot", 0, 3), ("bi", 0, 3),
    ("z", 0, 0, 1), ("core", 0, 3), ("add", 0, 1, 3), ("bi", 0, 5), ("z", 0, 0, 2), ("core", 0, 2),
    ("add", 0, 1, 2), ("z", 0, 1, 0), ("add", 0, 0, 3), ("bi", 1, 6), ("bo", 1, 2), ("core", 0, 1),
    ("add", 0, 0, 1), ("bo", 2, 1), ("bi", 0, 6), ("bi", 1, 7), ("z", 0, 1, 2), ("add", 0, 0, 2), ("add", 0, 1, 1),
    ("z", 0, 1, 1), ("bi", 0, 7), ("z", 0, 0, 3), ("core", 0, 0), ("add", 0, 0, 0), ("add", 0, 1, 0), ("keep", 0),
    ("g", 0, 0), ("z", 1, 0, 0), ("bo", 1, 3), ("rot", 1, 1), ("z", 1, 0, 2), ("rot", 1, 3), ("rot", 1, 2),
    ("core", 1, 3), ("add", 1, 0, 3), ("add", 1, 1, 3), ("bo", 2, 2), ("bo", 3, 1), ("core", 1, 2), ("core", 1, 1),
    ("add", 1, 0, 1), ("add", 1, 1, 2), ("z", 0, 1, 3), ("z", 1, 0, 1), ("z", 1, 1, 0), ("add", 1, 0, 2),
    ("add", 1, 1, 1), ("rot", 1, 0), ("core", 1, 0), ("bo", 2, 3), ("rot", 2, 2), ("rot", 2, 3), ("add", 1, 1, 0),
    ("add", 1, 0, 0), ("keep", 1), ("g", 1, 0), ("z", 2, 0, 0), ("g", 0, 1), ("z", 2, 0, 1), ("core", 2, 3),
    ("add", 2, 1, 3), ("add", 2, 0, 3), ("core", 2, 2), ("add", 2, 1, 2), ("z", 2, 0, 2), ("bo", 3, 2),
    ("rot", 2, 0), ("core", 2, 0), ("rot", 2, 1), ("z", 0, 2, 3), ("core", 2, 1), ("add", 2, 0, 1), ("bo", 3, 3),
    ("rot", 3, 2), ("z", 1, 1, 1), ("g", 1, 1), ("rot", 3, 1), ("add", 2, 0, 2), ("add", 2, 1, 1), ("z", 2, 1, 0),
    ("z", 0, 2, 2), ("core", 3, 2), ("add", 3, 1, 2), ("rot", 3, 3), ("core", 3, 1), ("add", 3, 0, 1),
    ("z", 0, 2, 0), ("z", 0, 2, 1), ("core", 3, 3), ("add", 2, 0, 0), ("add", 2, 1, 0), ("add", 3, 1, 3),
    ("keep", 2), ("g", 2, 0), ("z", 2, 1, 1), ("z", 1, 2, 0), ("add", 3, 0, 3), ("z", 3, 0, 0), ("rot", 3, 0),
    ("z", 2, 2, 0), ("g", 1, 2), ("add", 3, 1, 1), ("z", 3, 0, 1), ("g", 2, 1), ("add", 3, 0, 2), "acts",
    ("core", 3, 0), ("add", 3, 0, 0), ("add", 3, 1, 0), ("keep", 3), ("g", 3, 0), ("z", 3, 1, 0), ("a", 1, 1),
    ("z", 4, 0, 0), ("zown", 1), ("z", 4, 0, 1), ("z", 3, 1, 1), ("a", 1, 4), ("g", 2, 2), ("g", 0, 2), ("a", 0, 2),
    ("a", 1, 2), ("g", 3, 1), ("g", 1, 3), ("z", 3, 2, 0), ("z", 3, 0, 2), ("a", 1, 3), ("a", 0, 6), ("z", 4, 1, 0),
    ("g", 0, 3), ("a", 0, 4), ("a", 1, 6), ("a", 0, 5), ("a", 1, 7), ("g", 3, 2), ("a", 0, 7), ("g", 3, 3),
    ("z", 4, 0, 2), ("a", 0, 1), ("zsum", 1), ("a", 0, 3), ("a", 1, 5), ("score", 0), ("zown", 2), ("z", 4, 1, 1),
    ("z", 4, 2, 0), ("zsum", 2), ("g", 2, 3), ("score", 1), ("zown", 3), ("zsum", 3), ("score", 2), ("zown", 4),
    ("zsum", 4), ("score", 3),
)


class Schedule:
    def __init__(self):
        self.actions = {}
        self.done = set()

    def at(self, when, name, action, *needs):
        self.actions[name] = (when, len(self.actions), action, needs)

    def do(self, name):
        if name in self.done:
            return
        self.done.add(name)
        for need in self.actions[name][3]:
            self.do(need)
        self.actions[name][2]()

    def run(self):
        for name in sorted(self.actions, key=lambda name: self.actions[name][:2]):
            self.do(name)


class Gather:
    def __init__(self, me, bits, view, own, send_sem, recv_sem, drains):
        self.me, self.bits, self.view, self.own = me, bits, view, own
        self.send_sem, self.recv_sem, self.drains = send_sem, recv_sem, drains
        upper = list(range(1, bits))
        self.orders = [upper + [0], upper[::-1] + [0]]

    def send(self, h, mask, bit):
        there = self.view(h, flip_mask(self.me, mask, self.bits))
        src = self.own(h) if mask == 0 else there
        slot = mask | (1 << bit)
        copy = remote(src, there, self.send_sem.at[h, slot], self.recv_sem.at[h, slot], example=flip(self.me, bit))
        copy.start()
        self.drains.append(copy.wait_send)

    def start(self):
        for place in range(self.bits - 1):
            for h in range(2):
                self.send(h, 0, self.orders[h][place])
            if place == 0:
                for h in range(2):
                    self.send(h, 0, 0)

    def before(self, h, mask):
        return mask & ~(1 << self.orders[h][last_level(mask, self.orders[h])])

    def receive(self, h, mask):
        here = self.view(h, flip_mask(self.me, mask, self.bits))
        remote(here, here, self.send_sem.at[h, mask], self.recv_sem.at[h, mask], example=flip(self.me, 0)).wait_recv()
        for bit in self.orders[h][last_level(mask, self.orders[h]) + 1 :]:
            self.send(h, mask, bit)

    def masks(self):
        pairs = [(h, mask) for mask in range(1, 1 << self.bits) for h in range(2)]
        return sorted(pairs, key=lambda p: (last_level(p[1], self.orders[p[0]]), bin(p[1]).count("1"), p[1], p[0]))


class Line:
    def __init__(self, t, n, piece, send_sem, recv_sem, drains):
        self.t, self.n, self.piece = t, n, piece
        self.send_sem, self.recv_sem, self.drains = send_sem, recv_sem, drains

    def send(self, cond, s, src, way):
        ref = self.piece(src, s)
        copy = remote(ref, ref, self.send_sem.at[way, s, src], self.recv_sem.at[s, src], tensor=self.t + 1 - 2 * way)

        @pl.when(cond)
        def _():
            copy.start()

        def drain():
            @pl.when(cond)
            def _():
                copy.wait_send()

        self.drains.append(drain)

    def own(self, s):
        self.send(self.t < self.n - 1, s, self.t, 0)
        self.send(self.t > 0, s, self.t, 1)

    def receive(self, s, d):
        for way in range(2):
            sign = 1 - 2 * way
            src = self.t - sign * d
            here = src >= 0 if way == 0 else src < self.n
            on = self.t < self.n - 1 if way == 0 else self.t > 0

            @pl.when(here)
            def _():
                ref = self.piece(src, s)
                remote(ref, ref, self.send_sem.at[way, s, src], self.recv_sem.at[s, src],
                       tensor=self.t - sign).wait_recv()

            if d < self.n - 1:
                self.send(here & on, s, src, way)


def plan_times(n, slices, chip_bits):
    hop, period, lag, step, rise = 5.5, 16.5, 21.0, 6.0, 6.0
    times = {"begin": -9.0, "own_in": 0.5, "grads_out": 0.1, "q_in": 1.5, "grads_in": 20.0}
    for k in range(n):
        times["grads", k] = 8.0 + k
    orders = [list(range(chip_bits)), list(range(chip_bits))[::-1]]
    full = [[bit + 1 for bit in order] + [0] for order in orders]
    count = 2 << chip_bits

    def gather(label, base, gap):
        for h in range(2):
            for mask in range(1, count):
                upper = last_level(mask & ~1, full[h]) + bin(mask >> 1).count("1") if mask & ~1 else 0
                times[label, h, mask] = base + gap * upper + (mask & 1)

    gather("bi", 3.0, 10.5)
    for cm in range(n):
        ready = 3.0 + 10.5 * (cm.bit_length() + (bin(cm).count("1") > 1)) + 2 if cm else 4.5
        for q in range(n - 1):
            times["z", 0, q, cm] = ready + step * q
    acts = 3.0 + 10.5 * (chip_bits + 1) + step * n
    times["acts"] = acts
    gather("a", acts + 3, 3.0)
    for s in range(slices):
        base = 4 + s * period
        times["bo", s, 0] = base - period - hop if s else 0.0
        for d in range(1, n):
            times["bo", s, d] = base + d * hop
        rot = base + lag
        for i, cm in enumerate(sorted(range(n), key=lambda m: -bin(m).count("1"))):
            times["rot", s, cm] = rot + 0.8 * i
            times["core", s, cm] = rot + 1.6 + 0.8 * i
            for h in range(2):
                times["add", s, h, cm] = rot + 1.7 + rise * level_of(cm, orders[h]) + 0.1 * i
        done = rot + 2.5 + rise * chip_bits
        times["keep", s] = done
        for d in range(n):
            times["g", s, d] = done + 4.0 * d
        a = s + 1
        for q in range(n - 1):
            for k in range(n - 1 - q):
                times["z", a, q, k] = done + 0.1 + step * (q + (k if q else 0)) + 0.5 * k
        own = done + step * n
        times["zown", a] = own - 1
        times["zsum", a] = own
        times["score", s] = own + 0.1
    if set(TUNED_ORDER) == set(times):
        times = {name: float(place) for place, name in enumerate(TUNED_ORDER)}
    return times


def choose(slot_ref, list_ref, count_ref, found, alive, fold, me):
    count, length, tk = found.shape
    token_len = fold.shape[1]
    mine = jnp.broadcast_to(list_ref[pl.ds(me, 1), :], (length, length))
    diagonal = lax.broadcasted_iota(jnp.int32, (length, length), 0) == lax.broadcasted_iota(
        jnp.int32, (length, length), 1
    )
    mine = jnp.sum(jnp.where(diagonal, mine, 0), axis=1, keepdims=True)
    total = slot_ref.shape[1]
    matches = mine == lax.broadcasted_iota(jnp.int32, (length, total), 1)
    slots = jnp.sum(jnp.where(matches, slot_ref[...], 0), axis=1, keepdims=True)
    live = jnp.sum(jnp.where(matches, count_ref[...], 0), axis=1, keepdims=True)
    place = lax.broadcasted_iota(jnp.int32, (length, tk), 1) // token_len
    for e in range(count):
        found[e] = (slots == place + e * length).astype(F32)
    alive[...] = (lax.broadcasted_iota(jnp.int32, (length, token_len), 1) < live).astype(F32)
    same = lax.broadcasted_iota(jnp.int32, (tk, token_len), 0) % token_len == lax.broadcasted_iota(
        jnp.int32, (tk, token_len), 1
    )
    fold[...] = same.astype(F32)


def listed(total, found, alive, fold):
    spread = jnp.zeros(found.shape[1:], F32)
    for e in range(found.shape[0]):
        spread += jnp.where(found[e] > 0.5, total[e : e + 1, :], F32(0.0))
    scores = jnp.dot(spread, fold[...], precision=lax.Precision.HIGHEST, preferred_element_type=F32)
    return jnp.where(alive[...] > 0.5, scores, F32(0.0))


def whole_kernel(
    n, bits, tk,
    q_hbm, bi_hbm, bo_ref, grads_ref, acts_hbm, eig_hbm,
    slot_hbm, list_hbm, count_hbm, out_ref,
    slot_ref, list_ref, count_ref, found, alive, fold, q_ref, bi_ref, acts_ref, eig_ref,
    left, hop, bo_all, bi_all, prod, core_in, xy_in, fin, gall, zheld, zin, cacc, acts_t, aall, acc, red_t, red_e,
    own_sem, hop_send, hop_recv, grad_send, grad_recv, bo_send, bo_recv, g_send, g_recv, bi_send, bi_recv, a_send, a_recv,
    core_send, core_recv, xy_send, xy_recv, z_send, z_recv, rt_send, rt_recv, re_send, re_recv,
):
    me = lax.axis_index("example")
    t = lax.axis_index("tensor")
    count = 1 << bits
    pair = me // 2
    core = me % 2
    chip_bits = bits - 1
    width, wide = q_hbm.shape
    tk = grads_ref.shape[0]
    share = tk // n
    slices = width // LANES
    total_rows = left.shape[0]
    half = total_rows // 2
    orders = [list(range(chip_bits)), list(range(chip_bits))[::-1]]
    drains, early = [], []
    plan = Schedule()

    tables = []
    for h in range(2):
        table = {}
        for place in range(chip_bits):
            for mask in range(1 << chip_bits):
                if level_of(mask, orders[h]) > place:
                    table[(place, mask)] = len(table)
        tables.append(table)

    bi_copy = pltpu.make_async_copy(bi_hbm, bi_ref, own_sem.at[2 * slices])
    bi_copy.start()
    acts_copy = pltpu.make_async_copy(acts_hbm, acts_ref, own_sem.at[2 * slices + 1])
    q_copy = pltpu.make_async_copy(q_hbm, q_ref, own_sem.at[2 * slices + 2])
    eig_copy = pltpu.make_async_copy(eig_hbm, eig_ref, own_sem.at[2 * slices + 3])
    bo_copies = []
    for s in range(slices):
        for h in range(2):
            copy = pltpu.make_async_copy(
                bo_ref.at[:, pl.ds(h * width + s * LANES, LANES)],
                bo_all.at[t, s, :, pl.ds(h * LANES, LANES)],
                own_sem.at[2 * s + h],
            )
            copy.start()
            bo_copies.append(copy)
    table_copies = [
        pltpu.make_async_copy(src, dst, own_sem.at[2 * slices + 4 + i])
        for i, (src, dst) in enumerate(((slot_hbm, slot_ref), (list_hbm, list_ref), (count_hbm, count_ref)))
    ]
    for copy in (acts_copy, q_copy, eig_copy, *table_copies):
        copy.start()

    barrier = pltpu.get_barrier_semaphore()
    for k in range(1, n):
        pl.semaphore_signal(barrier, inc=1, device_id={"tensor": (t + k) % n}, device_id_type=MESH)
    for k in range(1, count):
        pl.semaphore_signal(barrier, inc=1, device_id={"example": (me + k) % count}, device_id_type=MESH)
    bi_copy.wait()
    for i in range(width // LANES):
        rows = pl.ds(pl.multiple_of(core * width + i * LANES, LANES), LANES)
        bi_all[pair, rows, :] = bi_ref[:, i * LANES : (i + 1) * LANES].T
    pl.semaphore_wait(barrier, n + count - 2)

    def hop_copy(k):
        there = (t + k) % n
        rows = pl.ds(pl.multiple_of(there * share, share), share)
        return remote(grads_ref.at[rows], hop.at[t], hop_send.at[k], hop_recv.at[t], tensor=there)

    def grads_out():
        for k in range(1, n):
            copy = hop_copy(k)
            copy.start()
            drains.append(copy.wait_send)
        local = pltpu.make_async_copy(
            grads_ref.at[pl.ds(pl.multiple_of(t * share, share), share)], hop.at[t], hop_send.at[0]
        )
        local.start()
        local.wait()

    def grad_rows(e):
        return left.at[pl.ds(pl.multiple_of(wide + e * share, share), share)]

    def grads_on(k):
        src = (t + k) % n
        if k:
            remote(hop.at[src], hop.at[src], hop_send.at[k], hop_recv.at[src], tensor=src).wait_recv()
        for h in range(2):
            goal = 2 * src + h
            piece = hop.at[src, :, pl.ds(h * width, width)]
            copy = remote(piece, grad_rows(me), grad_send.at[k, h], grad_recv.at[me], example=goal)
            local = pltpu.make_async_copy(piece, grad_rows(me), grad_send.at[k, h])

            @pl.when(goal != me)
            def _():
                copy.start()

            @pl.when(goal == me)
            def _():
                local.start()

            def drain(copy=copy, goal=goal):
                @pl.when(goal != me)
                def _():
                    copy.wait_send()

            drains.append(drain)

    def grads_in():
        for k in range(1, count):
            src = (me + k) % count
            remote(grad_rows(src), grad_rows(src), grad_send.at[0, 0], grad_recv.at[src], example=src).wait_recv()
        for k in range(n):
            for h in range(2):
                piece = hop.at[(t + k) % n, :, pl.ds(h * width, width)]

                @pl.when(2 * ((t + k) % n) + h == me)
                def _():
                    pltpu.make_async_copy(piece, grad_rows(me), grad_send.at[k, h]).wait()

    bo_line = Line(t, n, lambda src, s: bo_all.at[src, s], bo_send, bo_recv, drains)
    g_line = Line(t, n, lambda src, s: gall.at[s, :, pl.ds(pl.multiple_of(src * share, share), share)], g_send, g_recv, drains)
    quarter = width // 2

    def bi_view(h, e):
        return bi_all.at[e // 2, pl.ds(pl.multiple_of((e % 2) * width + h * quarter, quarter), quarter)]

    bi_gather = Gather(me, bits, bi_view, lambda h: bi_view(h, me), bi_send, bi_recv, drains)

    def a_view(h, e):
        return aall.at[e, pl.ds(h * (wide // 2), wide // 2)]

    a_gather = Gather(me, bits, a_view, lambda h: a_view(h, me), a_send, a_recv, drains)

    def core_copy(s, cm):
        return remote(prod.at[s, cm, 1 - core], core_in.at[s, cm], core_send.at[s, cm], core_recv.at[s, cm],
                      example=flip(me, 0))

    def rotate(s, cm):
        owner = flip_mask(pair, cm, chip_bits)

        def step(rows):
            res = jnp.dot(left[rows, :], bo_all[owner, s], preferred_element_type=F32).astype(BF)
            prod[s, cm, 0, rows, :] = res[:, :LANES]
            prod[s, cm, 1, rows, :] = res[:, LANES:]

        tile_loop(total_rows, total_rows, step)
        copy = core_copy(s, cm)
        copy.start()
        drains.append(copy.wait_send)

    def xy_copy(s, h, mask, place):
        bit = orders[h][place]
        slot = tables[h][(place, mask & ~(1 << bit))]
        rows = pl.ds(h * half, half)
        return remote(prod.at[s, mask, core, rows], xy_in.at[s, slot, rows], xy_send.at[s, h, mask],
                      xy_recv.at[s, h, slot], example=flip(me, bit + 1))

    def add_up(s, h, mask):
        level = level_of(mask, orders[h])
        for place in range(level):
            xy_copy(s, h, mask | (1 << orders[h][place]), place).wait_recv()
        inboxes = [tables[h][(place, mask)] for place in range(level)]

        def step(rows):
            rows = pl.ds(pl.multiple_of(rows.start + h * half, rows.size), rows.size)
            total = prod[s, mask, core, rows, :].astype(F32) + core_in[s, mask, rows, :].astype(F32)
            for slot in inboxes:
                total += xy_in[s, slot, rows, :].astype(F32)
            if mask:
                prod[s, mask, core, rows, :] = total.astype(BF)
            else:
                fin[s, rows, :] = total.astype(BF)

        tile_loop(half, half, step)
        if mask:
            copy = xy_copy(s, h, mask, level)
            copy.start()
            drains.append(copy.wait_send)

    def keep_grads(s):
        rows = pl.ds(pl.multiple_of(t * share, share), share)
        for e in range(count):
            gall[s, e, rows, :] = fin[s, wide + e * share : wide + (e + 1) * share, :]

    def z_product(a, block, rows):
        right = acts_t[...] if a == 0 else fin[a - 1, :wide, :]
        return jnp.dot(bi_all[block, rows, :], right, preferred_element_type=F32)

    def z_unit(a, q, block_up, block_down):
        up = (t == q) & (block_up > q)
        down = (t == n - 1 - q) & (block_down < n - 1 - q)
        block = jnp.where(up, block_up, block_down)
        toward = jnp.where(up, 1, -1)
        slot = block + jnp.where(up, 1, 0)
        copy = remote(zheld.at[a, block], zin.at[a, slot], z_send.at[a, block], z_recv.at[a, slot], tensor=t + toward)

        @pl.when(up | down)
        def _():
            def first(rows):
                zheld[a, block, rows, :] = z_product(a, block, rows).astype(BF)

            tile_loop(wide, wide, first)
            if q:
                remote(zin.at[a, slot], zin.at[a, slot], z_send.at[a, block], z_recv.at[a, slot],
                       tensor=t - toward).wait_recv()

                def second(rows):
                    total = zheld[a, block, rows, :].astype(F32) + zin[a, slot, rows, :].astype(F32)
                    zheld[a, block, rows, :] = total.astype(BF)

                tile_loop(wide, wide, second)
            copy.start()

        def drain():
            @pl.when(up | down)
            def _():
                copy.wait_send()

        drains.append(drain)

    def z_own_product(a):
        def first(rows):
            cacc[rows, :] = z_product(a, t, rows)

        tile_loop(wide, 512, first)

    def z_own_sum(a):
        for way in range(2):
            slot = t + 1 - way

            @pl.when(t > 0 if way == 0 else t < n - 1)
            def _():
                remote(zin.at[a, slot], zin.at[a, slot], z_send.at[a, t], z_recv.at[a, slot],
                       tensor=t - 1 + 2 * way).wait_recv()

                def second(rows):
                    cacc[rows, :] += zin[a, slot, rows, :].astype(F32)

                tile_loop(wide, 512, second)

    def keep_acts():
        def step(rows):
            aall[me, rows, :] = cacc[rows, :].astype(BF)

        tile_loop(wide, 256, step)

    def score(s):
        def step(rows):
            scaled = (cacc[rows, :] / eig_ref[rows, s * LANES : (s + 1) * LANES]).astype(BF)
            for group in range(n):
                tokens = gall[s, 2 * group : 2 * group + 2].reshape(2 * tk, LANES)
                weighted = lax.dot_general(
                    scaled, tokens, (((1,), (1,)), ((), ())), preferred_element_type=F32
                )
                for c in range(2):
                    e = 2 * group + c
                    part = weighted[:, c * tk : (c + 1) * tk] * aall[e, rows, :].astype(F32)
                    acc[e] += jnp.sum(part.reshape(-1, 8, tk), axis=0)

        tile_loop(wide, 1024, step)

    def set_aside(s):
        early.extend(drains)
        drains.clear()
        score(s)

    def last_product(a):
        for drain in early:
            drain()
        z_own_product(a)

    def begin():
        bi_gather.start()
        for copy in bo_copies:
            copy.wait()

    def own_in():
        acc[...] = jnp.zeros_like(acc)
        acts_copy.wait()
        acts_t[...] = acts_ref[...].T
        eig_copy.wait()
        for copy in table_copies:
            copy.wait()
        choose(slot_ref, list_ref, count_ref, found, alive, fold, me)

    def q_in():
        q_copy.wait()
        for i in range(wide // LANES):
            left[i * LANES : (i + 1) * LANES, :] = q_ref[:, i * LANES : (i + 1) * LANES].T

    part = functools.partial
    times = plan_times(n, slices, chip_bits)
    plan.at(times["begin"], "begin", begin)
    plan.at(times["own_in"], "own_in", own_in, "begin")
    plan.at(times["grads_out"], "grads_out", grads_out, "begin")
    plan.at(times["q_in"], "q_in", q_in, "begin")
    for k in range(n):
        plan.at(times["grads", k], ("grads", k), part(grads_on, k), "grads_out")
    plan.at(times["grads_in"], "grads_in", grads_in, *[("grads", k) for k in range(n)])

    def plan_line(label, line, s, *needs):
        plan.at(times[label, s, 0], (label, s, 0), part(line.own, s), *needs)
        for d in range(1, n):
            plan.at(times[label, s, d], (label, s, d), part(line.receive, s, d), (label, s, d - 1))

    def plan_gather(label, gather, start):
        for h, mask in gather.masks():
            before = gather.before(h, mask)
            plan.at(times[label, h, mask], (label, h, mask), part(gather.receive, h, mask),
                    (label, h, before) if before else start)

    for s in range(slices):
        plan_line("bo", bo_line, s, "begin")
    plan_gather("bi", bi_gather, "begin")

    def bi_of(cm):
        return [("bi", h, 2 * cm + c) for h in range(2) for c in range(2) if cm or c]

    def plan_z(a, q, k, block_up, block_down, *needs):
        name = ("z", a, q, k)
        plan.at(times[name], name, part(z_unit, a, q, block_up, block_down), *needs)

    for cm in range(n):
        block = flip_mask(pair, cm, chip_bits)
        for q in range(n - 1):
            plan_z(0, q, cm, block, block, *(bi_of(cm) + ["own_in"] if q == 0 else [("z", 0, q - 1, cm)]))
    all_bi = [name for cm in range(n) for name in bi_of(cm)]

    def acts_in():
        z_own_product(0)
        z_own_sum(0)
        keep_acts()
        a_gather.start()

    plan.at(times["acts"], "acts", acts_in, *[("z", 0, n - 2, cm) for cm in range(n)])
    plan_gather("a", a_gather, "acts")
    all_acts = [("a", h, mask) for h, mask in a_gather.masks()]

    for s in range(slices):
        for cm in range(n):
            name = ("rot", s, cm)
            plan.at(times[name], name, part(rotate, s, cm), "q_in", "grads_in", *[("bo", s, d) for d in range(n)])
            plan.at(times["core", s, cm], ("core", s, cm), lambda s=s, cm=cm: core_copy(s, cm).wait_recv(), name)
            for h in range(2):
                level = level_of(cm, orders[h])
                sent = [("add", s, h, cm | (1 << orders[h][place])) for place in range(level)]
                plan.at(times["add", s, h, cm], ("add", s, h, cm), part(add_up, s, h, cm), ("core", s, cm), *sent)
        rotated = [("add", s, h, 0) for h in range(2)]
        plan_line("g", g_line, s, ("keep", s))
        plan.at(times["keep", s], ("keep", s), part(keep_grads, s), *rotated)
        a = s + 1
        for q in range(n - 1):
            for k in range(n - 1 - q):
                needs = rotated + all_bi if q == 0 else [("z", a, q - 1, k)]
                plan_z(a, q, k, n - 1 - k, k, *needs)
        free = ("score", s - 1) if s else "acts"
        plan.at(times["zown", a], ("zown", a), part(last_product if a == slices else z_own_product, a), free, *(rotated + all_bi))
        sums = [("z", a, q, n - 2 - q) for q in range(n - 1)]
        plan.at(times["zsum", a], ("zsum", a), part(z_own_sum, a), ("zown", a), *sums)
        plan.at(times["score", s], ("score", s), part(set_aside if s == max(slices - 3, 0) else score, s), ("zsum", a), *([("g", s, d) for d in range(n)] + all_acts))

    plan.run()

    red_t[t] = jnp.concatenate([jnp.sum(acc[e], axis=0, keepdims=True) for e in range(count)], axis=0)
    copies = []
    for k in range(1, n):
        copy = remote(red_t.at[t], red_t.at[t], rt_send.at[k - 1], rt_recv.at[t], tensor=(t + k) % n)
        copy.start()
        copies.append(copy)
    for drain in drains:
        drain()
    for k in range(1, n):
        src = (t + k) % n
        remote(red_t.at[src], red_t.at[src], rt_send.at[k - 1], rt_recv.at[src], tensor=src).wait_recv()
    total = red_t[0]
    for k in range(1, n):
        total += red_t[k]
    red_e[me] = total
    for k in range(1, count):
        copy = remote(red_e.at[me], red_e.at[me], re_send.at[k - 1], re_recv.at[me], example=(me + k) % count)
        copy.start()
        copies.append(copy)
    for k in range(1, count):
        src = (me + k) % count
        remote(red_e.at[src], red_e.at[src], re_send.at[k - 1], re_recv.at[src], example=src).wait_recv()
    total = red_e[0]
    for k in range(1, count):
        total += red_e[k]
    out_ref[...] = listed(total, found, alive, fold)
    for copy in copies:
        copy.wait_send()


def list_scores(q, bi, bo, grads, acts, eig, slot, lists, live, token_len, n, count):
    bits = count.bit_length() - 1
    width, wide = q.shape
    tk = grads.shape[0]
    slices = width // LANES
    rows = wide + 2 * tk
    chips = count // 2
    anywhere = pl.BlockSpec(memory_space=pl.ANY)
    vmem = pl.BlockSpec(memory_space=pltpu.VMEM)
    dma = pltpu.SemaphoreType.DMA
    return pl.pallas_call(
        functools.partial(whole_kernel, n, bits, tk),
        out_shape=jax.ShapeDtypeStruct((tk // token_len, token_len), F32),
        in_specs=[anywhere] * 9,
        out_specs=vmem,
        scratch_shapes=[
            pltpu.VMEM((1, slot.shape[0]), jnp.int32),
            pltpu.VMEM(lists.shape, jnp.int32),
            pltpu.VMEM((1, live.shape[0]), jnp.int32),
            pltpu.VMEM((count, tk // token_len, tk), F32),
            pltpu.VMEM((tk // token_len, token_len), F32),
            pltpu.VMEM((tk, token_len), F32),
            pltpu.VMEM((width, wide), BF),
            pltpu.VMEM((wide, width), BF),
            pltpu.VMEM((tk, wide), BF),
            pltpu.VMEM((wide, width), F32),
            pltpu.VMEM((rows, width), BF),
            pltpu.VMEM((n, tk // n, wide), BF),
            pltpu.VMEM((n, slices, width, 2 * LANES), BF),
            pltpu.VMEM((n, wide, wide), BF),
            pltpu.VMEM((slices, chips, 2, rows, LANES), BF),
            pltpu.VMEM((slices, chips, rows, LANES), BF),
            pltpu.VMEM((slices, chips - 1, rows, LANES), BF),
            pltpu.VMEM((slices, rows, LANES), BF),
            pltpu.VMEM((slices, count, tk, LANES), BF),
            pltpu.VMEM((slices + 1, n, wide, LANES), BF),
            pltpu.VMEM((slices + 1, n + 1, wide, LANES), BF),
            pltpu.VMEM((wide, LANES), F32),
            pltpu.VMEM((wide, tk), BF),
            pltpu.VMEM((count, wide, tk), BF),
            pltpu.VMEM((count, 8, tk), F32),
            pltpu.VMEM((n, count, tk), F32),
            pltpu.VMEM((count, count, tk), F32),
            dma((2 * slices + 7,)),
            dma((n,)),
            dma((n,)),
            dma((n, 2)),
            dma((count,)),
            dma((2, slices, n)),
            dma((slices, n)),
            dma((2, slices, n)),
            dma((slices, n)),
            dma((2, count)),
            dma((2, count)),
            dma((2, count)),
            dma((2, count)),
            dma((slices, chips)),
            dma((slices, chips)),
            dma((slices, 2, chips)),
            dma((slices, 2, chips)),
            dma((slices + 1, n)),
            dma((slices + 1, n + 1)),
            dma((n,)),
            dma((n,)),
            dma((count,)),
            dma((count,)),
        ],
        compiler_params=pltpu.CompilerParams(
            collective_id=0, has_side_effects=True, vmem_limit_bytes=VMEM_LIMIT
        ),
        name="list_scores",
    )(q, bi, bo, grads, acts, eig, slot.reshape(1, -1), lists, live.reshape(1, -1))


def body(
    queries, basis_out, basis_in, eigvals, input_fac, grad_fac, cand_slot, score_list, token_count
):
    count = lax.axis_size("example")
    n = lax.axis_size("tensor")
    token_len = input_fac.shape[1]
    wide = queries.shape[2]
    acts = input_fac.reshape(-1, wide)
    grads = grad_fac.reshape(-1, wide)
    scores = [
        list_scores(queries[q], basis_in, basis_out, grads, acts, eigvals, cand_slot, score_list, token_count,
                    token_len, n, count)
        for q in range(queries.shape[0])
    ]
    return jnp.stack(scores)


def solution(mesh):
    in_specs = (
        P(None, "example", "tensor"),
        P("example", "tensor"),
        P("tensor", "example"),
        P("tensor", "example"),
        P("example", None, "tensor"),
        P("example", None, "tensor"),
        P(),
        P(),
        P(),
    )
    out_specs = P(None, "example", None)
    return jax.shard_map(body, mesh=mesh, in_specs=in_specs, out_specs=out_specs, check_vma=False)
```
